32 devices in a mesh: node: 16 (over z, y, x), rep: 2 (over core).
Axes of the slice: x: 2, y: 2, z: 4, core: 2. Of those that a mesh axis runs over, the one named last changes fastest.
Arguments:
- features: bfloat16 [4096, 512], P(('rep', 'node')), parts along dimension 0, may hold values from -24 to 24
- upstream: bfloat16 [4096, 512], P(('rep', 'node')), parts along dimension 0, may hold values from -36 to 36
- weight_one: bfloat16 [512, 512], replicated, may hold values from -0.25 to 0.25
- weight_two: bfloat16 [512, 512], replicated, may hold values from -0.25 to 0.25
- neighbours: int32 [4096, 32], P(('rep', 'node')), parts along dimension 0, may hold values from 0 to 2047, as said below
- edge_weight: int32 [4096, 32], P(('rep', 'node')), parts along dimension 0, may hold values from 1 to 8
- fetch_block: int32 [512, 2], P('rep'), parts along dimension 0, may hold values from 0 to 15, as said below
- fetch_count: int32 [512], P('rep'), parts along dimension 0, may hold values from 0 to 2, as said below
Outputs:
- d_features: bfloat16 [4096, 512], P(('rep', 'node')), parts along dimension 0
- grad_one: bfloat16 [1024, 512], P('rep'), parts along dimension 0
- grad_two: bfloat16 [1024, 512], P('rep'), parts along dimension 0
The draws below stay inside these ranges and needn't reach their ends.
There are 2 independent parts, one for each index of `rep`. The reference program is written for one: setup_inputs(seed, part) draws one part's arguments, and reference() takes and returns one part's arrays. A program takes and returns all parts, laid end to end along the dimension named above; an argument that names none is the same for every part. Nothing has to cross between parts.
Inputs may be any that keep to these rules, and one draw needn't show every extreme that they name: `neighbours`: no node names itself. `fetch_block`: the 2 blocks listed for one pair of devices are distinct. `fetch_count`: zero where p = d; every device has 2 live blocks from some other device.
All inputs are finite; a program needn't handle non-finite values.
Results may differ from the reference program's by a relative error of at most 0.013.
Values may be sent and summed in bfloat16 or wider, within the bound.
No kernel may reach another device: no remote copies, remote signals or barrier semaphores. Data moves between devices by JAX's collectives and lax.ppermute only.
A program may use at most 64 MiB of HBM per device.

```python
import jax
import jax.numpy as jnp
from jax import lax

D = 512
K = 32
ROWS = 128
HALO = 32
BLK = 8
CAP = 2
K_OFF = 12
NODES = 2048
N_NODE = 16


def plan_tables(key):
    blocks_dev = ROWS // BLK
    scores = jax.random.randint(jax.random.fold_in(key, 11), (N_NODE * N_NODE, blocks_dev), 0, 1 << 20)
    scores = scores * blocks_dev + jnp.arange(blocks_dev, dtype=jnp.int32)[None, :]
    order = jnp.argsort(scores, axis=1)
    table = order[:, :CAP].astype(jnp.int32)
    spare = order[:, CAP].astype(jnp.int32)
    counts = jax.random.randint(jax.random.fold_in(key, 12), (N_NODE, N_NODE), 0, CAP + 1)
    devices = jnp.arange(N_NODE, dtype=jnp.int32)
    counts = jnp.where(devices[:, None] == devices[None, :], 0, counts)
    full_peer = (devices + N_NODE // 2) % N_NODE
    counts = jnp.where(full_peer[:, None] == devices[None, :], CAP, counts)
    return (table, counts.reshape(-1).astype(jnp.int32), spare)


def draw_fetch_block(key, part):
    table, counts, spare = plan_tables(key)
    return table


def draw_fetch_count(key, part):
    table, counts, spare = plan_tables(key)
    return counts


def draw_neighbours(key, part):
    table, counts, spare = plan_tables(key)
    nodes = ROWS * N_NODE
    node_ids = jnp.arange(nodes, dtype=jnp.int32)
    home_dev = node_ids // ROWS
    live_slot = (jnp.arange(CAP, dtype=jnp.int32)[None, None, :] < counts.reshape(N_NODE, N_NODE, 1)).astype(jnp.int32)
    cumul = jnp.cumsum(live_slot.reshape(N_NODE, N_NODE * CAP), axis=1).astype(jnp.int32)
    live_total = cumul[:, -1]
    raw_pick = jax.random.randint(jax.random.fold_in(key, 13), (nodes, K), 0, 1 << 20)
    picked = raw_pick % live_total[home_dev][:, None]
    flat_slot = jax.vmap(lambda row_cum, row_pick: jnp.searchsorted(row_cum, row_pick, side='right'))(cumul[home_dev], picked).astype(jnp.int32)
    peer_dev = flat_slot // CAP
    slot_index = flat_slot % CAP
    pair_row = home_dev[:, None] * N_NODE + peer_dev
    block_id = table[pair_row, slot_index]
    stray = jax.random.randint(jax.random.fold_in(key, 18), (nodes, K), 0, 16) == 0
    block_id = jnp.where(stray, spare[pair_row], block_id)
    inner_row = jax.random.randint(jax.random.fold_in(key, 14), (nodes, K), 0, BLK)
    far_node = peer_dev * ROWS + block_id * BLK + inner_row
    magnitude = jax.random.randint(jax.random.fold_in(key, 15), (nodes, K), 1, HALO + 1)
    signs = jax.random.randint(jax.random.fold_in(key, 16), (nodes, K), 0, 2) * 2 - 1
    offset = magnitude * signs
    near_node = node_ids[:, None] + offset
    near_node = jnp.where((near_node < 0) | (near_node >= nodes), node_ids[:, None] - offset, near_node)
    which = jax.random.randint(jax.random.fold_in(key, 17), (nodes, K), 0, K) < K_OFF
    return jnp.where(which, far_node, near_node).astype(jnp.int32)


def place_ends(values, rng, low, high):
    longest = values.shape.index(max(values.shape))
    spots = []
    for shift in (0, 1):
        where = [jax.random.randint(jax.random.fold_in(rng, axis), (), 0, length) for axis, length in enumerate(values.shape)]
        where[longest] = (where[longest] + shift) % values.shape[longest]
        spots.append(tuple(where))
    return values.at[spots[0]].set(low).at[spots[1]].set(high)


def block_levels(stream_key, shape, cuts, least, high):
    def one(axis_at, parts):
        draws = jax.random.uniform(jax.random.fold_in(jax.random.fold_in(stream_key, 6), axis_at), (parts,), jnp.float32, least / len(cuts), high / len(cuts))
        return jnp.repeat(jnp.exp(draws), shape[axis_at] // parts).reshape((-1,) + (1,) * (len(shape) - axis_at - 1))

    gain = one(*cuts[0])
    for cut in cuts[1:]:
        gain = gain * one(*cut)
    return gain


def noise(rng, extent, spread, reach, split=(), kind=jnp.bfloat16):
    entries = jax.random.normal(rng, extent, jnp.float32) * spread
    if len(split) > 0:
        entries = block_levels(rng, extent, split, -0.22, 0.18) * entries
    return jnp.clip(entries, min=-reach, max=reach).astype(kind)


def setup_inputs(seed: int = 0, part: int = 0) -> dict:
    arg_keys = jax.random.split(jax.random.key(seed), 9)
    part_keys = jax.random.split(jax.random.fold_in(arg_keys[8], part), 9)
    features = noise(part_keys[0], (NODES, D), 4.0, 24.0, ((0, 16),))
    upstream = noise(part_keys[1], (NODES, D), 6.0, 36.0, ((0, 16),))
    weight_one = noise(arg_keys[2], (D, D), D ** -0.5, 0.25)
    weight_two = noise(arg_keys[3], (D, D), D ** -0.5, 0.25)
    neighbours = draw_neighbours(jax.random.fold_in(jax.random.fold_in(arg_keys[8], part), 71), part)
    edge_weight = place_ends(jax.random.randint(part_keys[5], (NODES, K), 1, 9), jax.random.fold_in(part_keys[5], 1), 1, 8).astype(jnp.int32)
    fetch_block = draw_fetch_block(jax.random.fold_in(jax.random.fold_in(arg_keys[8], part), 71), part)
    fetch_count = draw_fetch_count(jax.random.fold_in(jax.random.fold_in(arg_keys[8], part), 71), part)
    return dict(features=features, upstream=upstream, weight_one=weight_one, weight_two=weight_two, neighbours=neighbours, edge_weight=edge_weight, fetch_block=fetch_block, fetch_count=fetch_count)


SELF_WEIGHT = 8.0

def gelu_tanh(values):
    return jax.nn.gelu(values, approximate=True)

def valid_weights(neighbours, edge_weight, fetch_block, fetch_count):
    node_ids = jnp.arange(NODES, dtype=jnp.int32)
    home_dev = node_ids // ROWS
    first_row = (home_dev * ROWS)[:, None]
    owner_dev = neighbours // ROWS
    in_band = (neighbours >= first_row - HALO) & (neighbours < first_row + ROWS + HALO)
    table_row = (home_dev[:, None] * N_NODE + owner_dev).astype(jnp.int32)
    listed = fetch_block[table_row]
    live_slot = jnp.arange(CAP, dtype=jnp.int32)[None, None, :] < fetch_count[table_row][..., None]
    target = (neighbours % ROWS // BLK)[..., None]
    found_slot = jnp.any((listed == target) & live_slot, axis=-1)
    return jnp.where(in_band | found_slot, edge_weight.astype(jnp.float32), jnp.float32(0.0))

def aggregate(values, neighbours, weight, row_total):

    def one_group(group_index):
        begin = (group_index * ROWS).astype(jnp.int32)
        nbr_rows = lax.dynamic_slice_in_dim(neighbours, begin, ROWS, 0)
        weights = lax.dynamic_slice_in_dim(weight, begin, ROWS, 0)
        own_rows = lax.dynamic_slice_in_dim(values, begin, ROWS, 0).astype(jnp.float32)
        gathered = values[nbr_rows].astype(jnp.float32)
        return SELF_WEIGHT * own_rows + jnp.einsum('rk,rkd->rd', weights, gathered)
    sums = lax.map(one_group, jnp.arange(N_NODE, dtype=jnp.int32)).reshape(NODES, D)
    return (sums / row_total[:, None]).astype(jnp.bfloat16)

def adjoint(cotangent, neighbours, weight):
    cot_float = cotangent.astype(jnp.float32)

    def add_group(group_index, accum):
        begin = (group_index * ROWS).astype(jnp.int32)
        nbr_rows = lax.dynamic_slice_in_dim(neighbours, begin, ROWS, 0)
        weights = lax.dynamic_slice_in_dim(weight, begin, ROWS, 0)
        cot_rows = lax.dynamic_slice_in_dim(cot_float, begin, ROWS, 0)
        terms = (weights[:, :, None] * cot_rows[:, None, :]).reshape(ROWS * K, D)
        return accum.at[nbr_rows.reshape(-1)].add(terms)
    return lax.fori_loop(0, N_NODE, add_group, SELF_WEIGHT * cot_float)

def reference(features, upstream, weight_one, weight_two, neighbours, edge_weight, fetch_block, fetch_count):
    weight = valid_weights(neighbours, edge_weight, fetch_block, fetch_count)
    row_total = SELF_WEIGHT + lax.optimization_barrier(jnp.sum(weight, axis=1))
    grad_scale = 1.0 / jnp.sqrt(jnp.float32(NODES))
    agg_one = aggregate(features, neighbours, weight, row_total)
    pre_one = jnp.dot(agg_one, weight_one, preferred_element_type=jnp.float32)
    hidden_f, gelu_back = jax.vjp(gelu_tanh, pre_one)
    hidden = hidden_f.astype(jnp.bfloat16)
    agg_two = aggregate(hidden, neighbours, weight, row_total)
    grad_two = jnp.dot(agg_two.T, upstream, preferred_element_type=jnp.float32) * grad_scale
    q_two = (jnp.dot(upstream, weight_two.T, preferred_element_type=jnp.float32) / row_total[:, None]).astype(jnp.bfloat16)
    back_hidden = adjoint(q_two, neighbours, weight)
    d_pre = gelu_back(back_hidden)[0].astype(jnp.bfloat16)
    grad_one = jnp.dot(agg_one.T, d_pre, preferred_element_type=jnp.float32) * grad_scale
    q_one = (jnp.dot(d_pre, weight_one.T, preferred_element_type=jnp.float32) / row_total[:, None]).astype(jnp.bfloat16)
    d_features = adjoint(q_one, neighbours, weight)
    return (d_features.astype(jnp.bfloat16), grad_one.astype(jnp.bfloat16), grad_two.astype(jnp.bfloat16))
```

```python
import functools
import math

import jax
import jax.numpy as jnp
from jax import lax
from jax.experimental import pallas as pl
from jax.experimental.pallas import tpu as pltpu
from jax.sharding import PartitionSpec as P

D = 512
K = 32
ROWS = 128
HALO = 32
BLK = 8
CAP = 2
SELF_WEIGHT = 8.0
SLOT = CAP * BLK
HALO_COL = ROWS
FAR_COL = 2 * ROWS
PLANE = 4

F32 = jnp.float32
BF16 = jnp.bfloat16
VMEM_LIMIT = 48 * 1024 * 1024


def nn(left, right):
    return jnp.dot(left, right, preferred_element_type=F32)


def nt(left, right):
    return lax.dot_general(left, right, (((1,), (1,)), ((), ())), preferred_element_type=F32)


def tn(left, right):
    return lax.dot_general(left, right, (((0,), (0,)), ((), ())), preferred_element_type=F32)


def iota(shape, dim):
    return lax.broadcasted_iota(jnp.int32, shape, dim)


def call(kernel, out_shape, scratch=()):
    return pl.pallas_call(
        kernel,
        out_shape=out_shape,
        scratch_shapes=list(scratch),
        compiler_params=pltpu.CompilerParams(vmem_limit_bytes=VMEM_LIMIT),
    )


def struct(shape, dtype):
    return jax.ShapeDtypeStruct(shape, dtype)


def prepare_kernel(
    count, nbr_ref, wgt_ref, tab_ref, cnt_ref, feat_ref, up_ref,
    mat_ref, own_ref, send_ref, fwd_ref, bwd_ref, rows_scr, at_scr,
):
    device = lax.axis_index("node")
    first = device * ROWS
    far = count * SLOT
    pairs = count * count
    rows_scr[...] = jnp.zeros_like(rows_scr)
    rows_scr[0:CAP, :] = tab_ref[...].astype(F32)
    rows_scr[CAP : CAP + 1, :] = cnt_ref[...].astype(F32)
    step = min(pairs, 256)
    listed = jnp.zeros((far, 8), F32)
    asked = jnp.zeros((far, 8), F32)
    peer_wide = iota((far, step), 0) // SLOT
    for at in range(0, pairs, step):
        pair = iota((far, step), 1) + at
        rows = rows_scr[:, at : at + step].astype(BF16)
        mine = jnp.where(pair == device * count + peer_wide, 1.0, 0.0).astype(BF16)
        theirs = jnp.where(pair == peer_wide * count + device, 1.0, 0.0).astype(BF16)
        listed = listed + nt(mine, rows)
        asked = asked + nt(theirs, rows)
    listed = listed.astype(jnp.int32)
    asked = asked.astype(jnp.int32)
    col = iota((far, 1), 0)
    slot = col // BLK % CAP
    inner = col % BLK
    block = jnp.where(slot == 0, listed[:, 0:1], listed[:, 1:2])
    node = col // SLOT * ROWS + block * BLK + inner
    in_band = (node >= first - HALO) & (node < first + ROWS + HALO)
    far_node = jnp.where((slot < listed[:, 2:3]) & jnp.logical_not(in_band), node, -1)
    asked_row = jnp.where(slot == 0, asked[:, 0:1], asked[:, 1:2]) * BLK + inner

    weight = wgt_ref[...].astype(F32)
    neighbour = nbr_ref[...]

    def counted(nodes, total):
        for k in range(K):
            total = total + jnp.where(neighbour[k : k + 1, :] == nodes, weight[k : k + 1, :], 0.0)
        return total

    square = (ROWS, ROWS)
    row = iota(square, 0)
    at_scr[0:ROWS, :] = counted(first + row, jnp.where(row == iota(square, 1), SELF_WEIGHT, 0.0))
    rim = iota((2 * HALO, ROWS), 0)
    rim_node = first + jnp.where(rim < HALO, rim - HALO, rim - HALO + ROWS)
    at_scr[HALO_COL : HALO_COL + 2 * HALO, :] = counted(rim_node, jnp.zeros((2 * HALO, ROWS), F32))
    at_scr[HALO_COL + 2 * HALO : FAR_COL, :] = jnp.zeros((FAR_COL - HALO_COL - 2 * HALO, ROWS), F32)
    for at in range(0, far, ROWS):
        nodes = jnp.broadcast_to(far_node[at : at + ROWS], square)
        at_scr[FAR_COL + at : FAR_COL + at + ROWS, :] = counted(nodes, jnp.zeros(square, F32))

    adj_mat = at_scr[...]
    matrix = adj_mat.T
    adj_mat = adj_mat.astype(BF16)
    total = jnp.sum(matrix, axis=1, keepdims=True)
    mat_ref[:, 0 : FAR_COL + far] = matrix.astype(BF16)
    pick = jnp.where(asked_row == iota((far, ROWS), 1), 1.0, 0.0)
    mat_ref[:, FAR_COL + far :] = pick.T.astype(BF16)

    scaled = (up_ref[...].astype(F32) / total).astype(BF16)
    features = feat_ref[...]
    own_ref[...] = nn(adj_mat[0:ROWS], scaled)
    rims = nn(adj_mat[HALO_COL : HALO_COL + 2 * HALO], scaled).astype(BF16)
    fwd_ref[0:HALO, :] = features[ROWS - HALO : ROWS]
    fwd_ref[HALO : 2 * HALO, :] = rims[HALO : 2 * HALO]
    bwd_ref[0:HALO, :] = features[0:HALO]
    bwd_ref[HALO : 2 * HALO, :] = rims[0:HALO]
    rows_out = nn(pick.astype(BF16), features).astype(BF16)
    send_ref[:, 0:SLOT, :] = rows_out.reshape(count, SLOT, D)
    terms = nn(adj_mat[FAR_COL:], scaled).astype(BF16)
    send_ref[:, SLOT : 2 * SLOT, :] = terms.reshape(count, SLOT, D)


def row_total(mat_ref, far):
    return jnp.sum(mat_ref[:, 0 : FAR_COL + far].astype(F32), axis=1, keepdims=True)


def layer_kernel(
    count, mat_ref, feat_ref, own_ref, recv_ref, left_ref, right_ref, w_one_ref, w_two_ref,
    *refs,
):
    plane, piece = PLANE, 2 * D // count
    groups = count // plane
    part_refs = refs[:plane]
    d_pre_ref, rim_scr, u_scr, hidden_scr, agg_scr = refs[plane:]
    device = lax.axis_index("node")
    group, place = device // plane, device % plane
    far = count * SLOT
    total = row_total(mat_ref, far)
    rim_scr[0:HALO, :] = left_ref[0:HALO, :]
    rim_scr[HALO : 2 * HALO, :] = right_ref[0:HALO, :]
    rim_scr[2 * HALO :, :] = jnp.zeros((ROWS - 2 * HALO, D), BF16)
    sums = nn(mat_ref[:, 0:ROWS], feat_ref[...])
    sums = sums + nn(mat_ref[:, HALO_COL:FAR_COL], rim_scr[...])
    sums = sums + nn(
        mat_ref[:, FAR_COL : FAR_COL + far], recv_ref[:, 0:SLOT, :].reshape(far, D)
    )
    agg = (sums / total).astype(BF16)
    agg_scr[...] = agg
    u_scr[...] = own_ref[...] + nn(
        mat_ref[:, FAR_COL + far :], recv_ref[:, SLOT : 2 * SLOT, :].reshape(far, D)
    )
    u_scr[0:HALO, :] += left_ref[HALO : 2 * HALO, :].astype(F32)
    u_scr[ROWS - HALO : ROWS, :] += right_ref[HALO : 2 * HALO, :].astype(F32)
    u = u_scr[...].astype(BF16)
    back = nt(u, w_two_ref[...])
    pre = nn(agg, w_one_ref[...])
    square = pre * pre
    bend = jnp.tanh(0.7978845608 * pre * (1.0 + 0.044715 * square))
    hidden_scr[...] = (0.5 * pre * (1.0 + bend)).astype(BF16)
    slope = 0.5 * (1.0 + bend) + 0.5 * pre * (1.0 - bend * bend) * (
        0.7978845608 * (1.0 + 3.0 * 0.044715 * square)
    )
    d_pre = (back * slope).astype(BF16)
    d_pre_ref[...] = d_pre
    wide = D // plane
    for v in range(plane):
        cols = pl.ds(pl.multiple_of((place ^ v) * wide, wide), wide)
        for half, (left, right) in enumerate(((hidden_scr, u), (agg_scr, d_pre))):
            part = tn(left[:, cols], right).astype(part_refs[v].dtype)
            for j in range(groups // 2):
                to = lax.rem(half * (groups // 2) + j + groups - group, groups)
                part_refs[v][pl.ds(pl.multiple_of(to * piece, piece), piece), :] = part[
                    j * piece : (j + 1) * piece
                ]


def back_kernel(count, mat_ref, d_pre_ref, w_one_ref, own_ref, send_ref, fwd_ref, bwd_ref):
    far = count * SLOT
    q = (nt(d_pre_ref[...], w_one_ref[...]) / row_total(mat_ref, far)).astype(BF16)
    own_ref[...] = tn(mat_ref[:, 0:ROWS], q)
    rims = tn(mat_ref[:, HALO_COL:FAR_COL], q).astype(BF16)
    bwd_ref[...] = rims[0:HALO]
    fwd_ref[...] = rims[HALO : 2 * HALO]
    terms = tn(mat_ref[:, FAR_COL : FAR_COL + far], q).astype(BF16)
    send_ref[...] = terms.reshape(count, SLOT, D)


def features_kernel(count, mat_ref, own_ref, recv_ref, left_ref, right_ref, out_ref, sum_scr):
    far = count * SLOT
    sum_scr[...] = own_ref[...] + nn(mat_ref[:, FAR_COL + far :], recv_ref[...].reshape(far, D))
    sum_scr[0:HALO, :] += left_ref[...].astype(F32)
    sum_scr[ROWS - HALO : ROWS, :] += right_ref[...].astype(F32)
    out_ref[...] = sum_scr[...].astype(BF16)


def plane_sum_kernel(piece, *refs):
    part_refs, out_refs = refs[:PLANE], refs[PLANE:]
    for k, out in enumerate(out_refs):
        rows = slice(k * piece, (k + 1) * piece)
        total = part_refs[0][rows, :].astype(F32)
        for ref in part_refs[1:]:
            total = total + ref[rows, :].astype(F32)
        out[...] = total.astype(out.dtype)


def group_sum_kernel(scale, *refs):
    total = refs[0][...]
    for ref in refs[1:-1]:
        total = total + ref[...].astype(F32)
    refs[-1][...] = (total * scale).astype(BF16)


def gather_kernel(count, *refs):
    piece, groups, wide = 2 * D // count, count // PLANE, D // PLANE
    device = lax.axis_index("node")
    group, place = device // PLANE, device % PLANE
    outs = refs[PLANE:]
    per = groups // 2
    for v in range(PLANE):
        row = (place ^ v) * wide
        for half in range(2):
            for j in range(per):
                at = lax.rem(group + 2 * groups - (half * per + j), groups)
                rows = refs[v][pl.ds(pl.multiple_of(at * piece, piece), piece), :]
                outs[half][pl.ds(pl.multiple_of(row + j * piece, piece), piece), :] = rows


def shards(
    features, upstream, weight_one, weight_two, neighbours, edge_weight, fetch_block, fetch_count
):
    count = lax.axis_size("node")
    groups = count // PLANE
    piece = 2 * D // count
    far = count * SLOT
    chain = FAR_COL + far
    up = [(i, i + 1) for i in range(count - 1)]
    down = [(i + 1, i) for i in range(count - 1)]

    def in_plane(value, v):
        return lax.ppermute(value, "node", [(i, i ^ v) for i in range(count)])

    def across(value, k):
        return lax.ppermute(
            value, "node", [(i, (i + k * PLANE) % count) for i in range(count)]
        )

    matrix, own, send, to_right, to_left = call(
        functools.partial(prepare_kernel, count),
        (
            struct((ROWS, chain + far), BF16),
            struct((ROWS, D), F32),
            struct((count, 2 * SLOT, D), BF16),
            struct((2 * HALO, D), BF16),
            struct((2 * HALO, D), BF16),
        ),
        (pltpu.VMEM((8, count * count), F32), pltpu.VMEM((chain, ROWS), F32)),
    )(
        neighbours.T, edge_weight.T, fetch_block.T, fetch_count.reshape(1, -1), features, upstream
    )
    from_left = lax.ppermute(to_right, "node", up)
    from_right = lax.ppermute(to_left, "node", down)
    received = lax.all_to_all(send, "node", split_axis=0, concat_axis=0, tiled=True)

    *parts, d_pre = call(
        functools.partial(layer_kernel, count),
        (
            struct((2 * D // PLANE, D), F32),
            *[struct((2 * D // PLANE, D), BF16)] * (PLANE - 1),
            struct((ROWS, D), BF16),
        ),
        (
            pltpu.VMEM((ROWS, D), BF16),
            pltpu.VMEM((ROWS, D), F32),
            pltpu.VMEM((ROWS, D), BF16),
            pltpu.VMEM((ROWS, D), BF16),
        ),
    )(matrix, features, own, received, from_left, from_right, weight_one, weight_two)
    plane_parts = [parts[0]] + [in_plane(parts[v], v) for v in range(1, PLANE)]

    own, send, to_right, to_left = call(
        functools.partial(back_kernel, count),
        (
            struct((ROWS, D), F32),
            struct((count, SLOT, D), BF16),
            struct((HALO, D), BF16),
            struct((HALO, D), BF16),
        ),
    )(matrix, d_pre, weight_one)
    from_left = lax.ppermute(to_right, "node", up)
    from_right = lax.ppermute(to_left, "node", down)
    received = lax.all_to_all(send, "node", split_axis=0, concat_axis=0, tiled=True)
    d_features = call(
        functools.partial(features_kernel, count),
        struct((ROWS, D), BF16),
        (pltpu.VMEM((ROWS, D), F32),),
    )(matrix, own, received, from_left, from_right)

    sums = call(
        functools.partial(plane_sum_kernel, piece),
        (struct((piece, D), F32), *[struct((piece, D), BF16)] * (groups - 1)),
    )(*plane_parts)
    shared = [sums[0]] + [across(sums[k], k) for k in range(1, groups)]
    total = call(
        functools.partial(group_sum_kernel, 1.0 / math.sqrt(ROWS * count)),
        struct((piece, D), BF16),
    )(*shared)
    chunk = jnp.concatenate([total] + [across(total, k) for k in range(1, groups)], axis=0)
    chunks = [chunk] + [in_plane(chunk, v) for v in range(1, PLANE)]
    grad_two, grad_one = call(
        functools.partial(gather_kernel, count),
        (struct((D, D), BF16), struct((D, D), BF16)),
    )(*chunks)
    return d_features, grad_one, grad_two


def solution(mesh):
    placed = (
        P(("rep", "node"), None),
        P(("rep", "node"), None),
        P(),
        P(),
        P(("rep", "node"), None),
        P(("rep", "node"), None),
        P("rep", None),
        P("rep"),
    )
    return jax.shard_map(
        shards,
        mesh=mesh,
        in_specs=placed,
        out_specs=(P(("rep", "node"), None), P("rep", None), P("rep", None)),
        check_vma=False,
    )
```

```python
import functools
import math

import jax
import jax.numpy as jnp
from jax import lax
from jax.experimental import pallas as pl
from jax.experimental.pallas import tpu as pltpu
from jax.sharding import PartitionSpec as P

D = 512
K = 32
ROWS = 128
HALO = 32
BLK = 8
CAP = 2
SELF_WEIGHT = 8.0
SLOT = CAP * BLK
HALO_COL = ROWS
FAR_COL = 2 * ROWS
PLANE = 4

F32 = jnp.float32
BF16 = jnp.bfloat16
VMEM_LIMIT = 48 * 1024 * 1024


def nn(left, right):
    return jnp.dot(left, right, preferred_element_type=F32)


def nt(left, right):
    return lax.dot_general(left, right, (((1,), (1,)), ((), ())), preferred_element_type=F32)


def tn(left, right):
    return lax.dot_general(left, right, (((0,), (0,)), ((), ())), preferred_element_type=F32)


def iota(shape, dim):
    return lax.broadcasted_iota(jnp.int32, shape, dim)


def call(kernel, out_shape, scratch=(), **specs):
    return pl.pallas_call(
        kernel,
        out_shape=out_shape,
        **specs,
        scratch_shapes=list(scratch),
        compiler_params=pltpu.CompilerParams(vmem_limit_bytes=VMEM_LIMIT),
    )


def struct(shape, dtype):
    return jax.ShapeDtypeStruct(shape, dtype)


def prepare_kernel(
    count, nbr_hbm, wgt_hbm, tab_hbm, cnt_hbm, feat_hbm, up_hbm,
    mat_ref, own_ref, send_ref, fwd_ref, bwd_ref,
    nbr_ref, wgt_ref, tab_ref, cnt_ref, feat_ref, up_ref, sems, rows_scr, at_scr,
):
    inputs = (
        (tab_hbm, tab_ref), (cnt_hbm, cnt_ref), (nbr_hbm, nbr_ref),
        (wgt_hbm, wgt_ref), (up_hbm, up_ref), (feat_hbm, feat_ref),
    )
    copies = [
        pltpu.make_async_copy(src, dst, sems.at[i]) for i, (src, dst) in enumerate(inputs)
    ]
    for copy in copies:
        copy.start()
    copies[0].wait()
    copies[1].wait()
    device = lax.axis_index("node")
    first = device * ROWS
    far = count * SLOT
    pairs = count * count
    rows_scr[...] = jnp.zeros_like(rows_scr)
    rows_scr[0:CAP, :] = tab_ref[...].astype(F32)
    rows_scr[CAP : CAP + 1, :] = cnt_ref[...].astype(F32)
    step = min(pairs, 256)
    listed = jnp.zeros((far, 8), F32)
    asked = jnp.zeros((far, 8), F32)
    peer_wide = iota((far, step), 0) // SLOT
    for at in range(0, pairs, step):
        pair = iota((far, step), 1) + at
        rows = rows_scr[:, at : at + step].astype(BF16)
        mine = jnp.where(pair == device * count + peer_wide, 1.0, 0.0).astype(BF16)
        theirs = jnp.where(pair == peer_wide * count + device, 1.0, 0.0).astype(BF16)
        listed = listed + nt(mine, rows)
        asked = asked + nt(theirs, rows)
    listed = listed.astype(jnp.int32)
    asked = asked.astype(jnp.int32)
    col = iota((far, 1), 0)
    slot = col // BLK % CAP
    inner = col % BLK
    block = jnp.where(slot == 0, listed[:, 0:1], listed[:, 1:2])
    node = col // SLOT * ROWS + block * BLK + inner
    in_band = (node >= first - HALO) & (node < first + ROWS + HALO)
    far_node = jnp.where((slot < listed[:, 2:3]) & jnp.logical_not(in_band), node, -1)
    asked_row = jnp.where(slot == 0, asked[:, 0:1], asked[:, 1:2]) * BLK + inner

    copies[2].wait()
    copies[3].wait()
    weight = wgt_ref[...].astype(F32)
    neighbour = nbr_ref[...]

    def counted(nodes, total):
        for k in range(K):
            total = total + jnp.where(neighbour[k : k + 1, :] == nodes, weight[k : k + 1, :], 0.0)
        return total

    square = (ROWS, ROWS)
    row = iota(square, 0)
    at_scr[0:ROWS, :] = counted(first + row, jnp.where(row == iota(square, 1), SELF_WEIGHT, 0.0))
    rim = iota((2 * HALO, ROWS), 0)
    rim_node = first + jnp.where(rim < HALO, rim - HALO, rim - HALO + ROWS)
    at_scr[HALO_COL : HALO_COL + 2 * HALO, :] = counted(rim_node, jnp.zeros((2 * HALO, ROWS), F32))
    at_scr[HALO_COL + 2 * HALO : FAR_COL, :] = jnp.zeros((FAR_COL - HALO_COL - 2 * HALO, ROWS), F32)
    for at in range(0, far, ROWS):
        nodes = jnp.broadcast_to(far_node[at : at + ROWS], square)
        at_scr[FAR_COL + at : FAR_COL + at + ROWS, :] = counted(nodes, jnp.zeros(square, F32))

    adj_mat = at_scr[...]
    matrix = adj_mat.T
    adj_mat = adj_mat.astype(BF16)
    total = jnp.sum(matrix, axis=1, keepdims=True)
    mat_ref[:, 0 : FAR_COL + far] = matrix.astype(BF16)
    pick = jnp.where(asked_row == iota((far, ROWS), 1), 1.0, 0.0)
    mat_ref[:, FAR_COL + far :] = pick.T.astype(BF16)

    copies[4].wait()
    scaled = (up_ref[...].astype(F32) / total).astype(BF16)
    copies[5].wait()
    features = feat_ref[...]
    own_ref[...] = nn(adj_mat[0:ROWS], scaled)
    rims = nn(adj_mat[HALO_COL : HALO_COL + 2 * HALO], scaled).astype(BF16)
    fwd_ref[0:HALO, :] = features[ROWS - HALO : ROWS]
    fwd_ref[HALO : 2 * HALO, :] = rims[HALO : 2 * HALO]
    bwd_ref[0:HALO, :] = features[0:HALO]
    bwd_ref[HALO : 2 * HALO, :] = rims[0:HALO]
    rows_out = nn(pick.astype(BF16), features).astype(BF16)
    send_ref[:, 0:SLOT, :] = rows_out.reshape(count, SLOT, D)
    terms = nn(adj_mat[FAR_COL:], scaled).astype(BF16)
    send_ref[:, SLOT : 2 * SLOT, :] = terms.reshape(count, SLOT, D)


def row_total(mat_ref, far):
    return jnp.sum(mat_ref[:, 0 : FAR_COL + far].astype(F32), axis=1, keepdims=True)


def layer_kernel(
    count, mat_ref, feat_ref, own_ref, recv_ref, left_ref, right_ref, w_one_ref, w_two_ref,
    *refs,
):
    plane, piece = PLANE, 2 * D // count
    groups = count // plane
    part_refs = refs[:plane]
    d_pre_ref, rim_scr, u_scr, hidden_scr, agg_scr = refs[plane:]
    device = lax.axis_index("node")
    group, place = device // plane, device % plane
    far = count * SLOT
    total = row_total(mat_ref, far)
    rim_scr[0:HALO, :] = left_ref[0:HALO, :]
    rim_scr[HALO : 2 * HALO, :] = right_ref[0:HALO, :]
    rim_scr[2 * HALO :, :] = jnp.zeros((ROWS - 2 * HALO, D), BF16)
    sums = nn(mat_ref[:, 0:ROWS], feat_ref[...])
    sums = sums + nn(mat_ref[:, HALO_COL:FAR_COL], rim_scr[...])
    sums = sums + nn(
        mat_ref[:, FAR_COL : FAR_COL + far], recv_ref[:, 0:SLOT, :].reshape(far, D)
    )
    agg = (sums / total).astype(BF16)
    agg_scr[...] = agg
    u_scr[...] = own_ref[...] + nn(
        mat_ref[:, FAR_COL + far :], recv_ref[:, SLOT : 2 * SLOT, :].reshape(far, D)
    )
    u_scr[0:HALO, :] += left_ref[HALO : 2 * HALO, :].astype(F32)
    u_scr[ROWS - HALO : ROWS, :] += right_ref[HALO : 2 * HALO, :].astype(F32)
    u = u_scr[...].astype(BF16)
    back = nt(u, w_two_ref[...])
    pre = nn(agg, w_one_ref[...])
    square = pre * pre
    bend = jnp.tanh(0.7978845608 * pre * (1.0 + 0.044715 * square))
    hidden_scr[...] = (0.5 * pre * (1.0 + bend)).astype(BF16)
    slope = 0.5 * (1.0 + bend) + 0.5 * pre * (1.0 - bend * bend) * (
        0.7978845608 * (1.0 + 3.0 * 0.044715 * square)
    )
    d_pre = (back * slope).astype(BF16)
    d_pre_ref[...] = d_pre
    wide = D // plane
    for v in range(plane):
        cols = pl.ds(pl.multiple_of((place ^ v) * wide, wide), wide)
        for half, (left, right) in enumerate(((hidden_scr, u), (agg_scr, d_pre))):
            part = tn(left[:, cols], right).astype(part_refs[v].dtype)
            for j in range(groups // 2):
                to = lax.rem(half * (groups // 2) + j + groups - group, groups)
                part_refs[v][pl.ds(pl.multiple_of(to * piece, piece), piece), :] = part[
                    j * piece : (j + 1) * piece
                ]


def back_kernel(count, mat_ref, d_pre_ref, w_one_ref, own_ref, *refs):
    groups = count // PLANE
    across_refs, (left_ref, right_ref, block_scr) = refs[:groups], refs[groups:]
    device = lax.axis_index("node")
    group, place = device // PLANE, device % PLANE
    far = count * SLOT
    q = (nt(d_pre_ref[...], w_one_ref[...]) / row_total(mat_ref, far)).astype(BF16)
    own_ref[...] = tn(mat_ref[:, 0:ROWS], q)
    rims = tn(mat_ref[:, HALO_COL:FAR_COL], q).astype(BF16)
    left_ref[...] = rims[0:HALO]
    right_ref[...] = rims[HALO : 2 * HALO]
    terms = tn(mat_ref[:, FAR_COL : FAR_COL + far], q).astype(BF16).reshape(count, SLOT, D)
    for peer in range(count):
        k = lax.rem(peer // PLANE + groups - group, groups)
        block_scr[k * PLANE + ((peer % PLANE) ^ place)] = terms[peer]
    size = PLANE * SLOT
    for k, ref in enumerate(across_refs):
        ref[0:size, :] = block_scr[k * PLANE : (k + 1) * PLANE].reshape(size, D)
        if k == 1:
            ref[size:, :] = rims[HALO : 2 * HALO]
        if k == groups - 1:
            ref[size:, :] = rims[0:HALO]


def turn_kernel(count, *refs):
    groups = count // PLANE
    across_refs, (left_ref, right_ref), plane_refs = (
        refs[:groups], refs[groups : groups + 2], refs[groups + 2 :],
    )
    place = lax.axis_index("node") % PLANE
    size = groups * SLOT
    for v, ref in enumerate(plane_refs):
        for k in range(groups):
            ref[k * SLOT : (k + 1) * SLOT, :] = across_refs[k][v * SLOT : (v + 1) * SLOT, :]
    left, right = left_ref[...], right_ref[...]
    from_below = across_refs[1][PLANE * SLOT :, :]
    from_above = across_refs[groups - 1][PLANE * SLOT :, :]
    plane_refs[1][size:, :] = jnp.where(place % 2 == 0, right, left)
    plane_refs[3][size:, :] = jnp.where(
        place == 0,
        from_above,
        jnp.where(place == 1, right, jnp.where(place == 2, left, from_below)),
    )


def features_kernel(count, mat_ref, own_ref, *refs):
    plane_refs, (out_ref, sum_scr, block_scr) = refs[:PLANE], refs[PLANE:]
    groups = count // PLANE
    device = lax.axis_index("node")
    group, place = device // PLANE, device % PLANE
    far = count * SLOT
    size = groups * SLOT
    for v, ref in enumerate(plane_refs):
        for k in range(groups):
            peer = lax.rem(group + groups - k, groups) * PLANE + (place ^ v)
            block_scr[peer] = ref[k * SLOT : (k + 1) * SLOT, :]
    sum_scr[...] = own_ref[...] + nn(mat_ref[:, FAR_COL + far :], block_scr[...].reshape(far, D))
    one, three = plane_refs[1][size:, :].astype(F32), plane_refs[3][size:, :].astype(F32)
    even = place % 2 == 0
    sum_scr[0:HALO, :] += jnp.where(even, three, one)
    sum_scr[ROWS - HALO : ROWS, :] += jnp.where(even, one, three)
    out_ref[...] = sum_scr[...].astype(BF16)


def plane_sum_kernel(piece, *refs):
    part_refs, out_refs = refs[:PLANE], refs[PLANE:]
    for k, out in enumerate(out_refs):
        rows = slice(k * piece, (k + 1) * piece)
        total = part_refs[0][rows, :].astype(F32)
        for ref in part_refs[1:]:
            total = total + ref[rows, :].astype(F32)
        out[...] = total.astype(out.dtype)


def group_sum_kernel(scale, *refs):
    total = refs[0][...]
    for ref in refs[1:-1]:
        total = total + ref[...].astype(F32)
    refs[-1][...] = (total * scale).astype(BF16)


def gather_kernel(count, *refs):
    piece, groups, wide = 2 * D // count, count // PLANE, D // PLANE
    device = lax.axis_index("node")
    group, place = device // PLANE, device % PLANE
    outs = refs[PLANE:]
    per = groups // 2
    for v in range(PLANE):
        row = (place ^ v) * wide
        for half in range(2):
            for j in range(per):
                at = lax.rem(group + 2 * groups - (half * per + j), groups)
                rows = refs[v][pl.ds(pl.multiple_of(at * piece, piece), piece), :]
                outs[half][pl.ds(pl.multiple_of(row + j * piece, piece), piece), :] = rows


def shards(
    features, upstream, weight_one, weight_two, neighbours, edge_weight, fetch_block, fetch_count
):
    count = lax.axis_size("node")
    groups = count // PLANE
    piece = 2 * D // count
    far = count * SLOT
    chain = FAR_COL + far
    up = [(i, i + 1) for i in range(count - 1)]
    down = [(i + 1, i) for i in range(count - 1)]

    def in_plane(value, v):
        return lax.ppermute(value, "node", [(i, i ^ v) for i in range(count)])

    def across(value, k):
        return lax.ppermute(
            value, "node", [(i, (i + k * PLANE) % count) for i in range(count)]
        )

    matrix, own, send, to_right, to_left = call(
        functools.partial(prepare_kernel, count),
        (
            struct((ROWS, chain + far), BF16),
            struct((ROWS, D), F32),
            struct((count, 2 * SLOT, D), BF16),
            struct((2 * HALO, D), BF16),
            struct((2 * HALO, D), BF16),
        ),
        (
            pltpu.VMEM((K, ROWS), jnp.int32),
            pltpu.VMEM((K, ROWS), jnp.int32),
            pltpu.VMEM((CAP, count * count), jnp.int32),
            pltpu.VMEM((1, count * count), jnp.int32),
            pltpu.VMEM((ROWS, D), BF16),
            pltpu.VMEM((ROWS, D), BF16),
            pltpu.SemaphoreType.DMA((6,)),
            pltpu.VMEM((8, count * count), F32),
            pltpu.VMEM((chain, ROWS), F32),
        ),
        in_specs=[pl.BlockSpec(memory_space=pl.ANY)] * 6,
    )(
        neighbours.T, edge_weight.T, fetch_block.T, fetch_count.reshape(1, -1), features, upstream
    )
    from_left = lax.ppermute(to_right, "node", up)
    from_right = lax.ppermute(to_left, "node", down)
    received = lax.all_to_all(send, "node", split_axis=0, concat_axis=0, tiled=True)

    *parts, d_pre = call(
        functools.partial(layer_kernel, count),
        (
            struct((2 * D // PLANE, D), F32),
            *[struct((2 * D // PLANE, D), BF16)] * (PLANE - 1),
            struct((ROWS, D), BF16),
        ),
        (
            pltpu.VMEM((ROWS, D), BF16),
            pltpu.VMEM((ROWS, D), F32),
            pltpu.VMEM((ROWS, D), BF16),
            pltpu.VMEM((ROWS, D), BF16),
        ),
    )(matrix, features, own, received, from_left, from_right, weight_one, weight_two)
    plane_parts = [parts[0]] + [in_plane(parts[v], v) for v in range(1, PLANE)]

    across_rows = [PLANE * SLOT + HALO * (k in (1, groups - 1)) for k in range(groups)]
    plane_rows = [groups * SLOT + HALO * (v in (1, 3)) for v in range(PLANE)]
    own, *blocks, to_left, to_right = call(
        functools.partial(back_kernel, count),
        (
            struct((ROWS, D), F32),
            *[struct((rows, D), BF16) for rows in across_rows],
            struct((HALO, D), BF16),
            struct((HALO, D), BF16),
        ),
        (pltpu.VMEM((count, SLOT, D), BF16),),
    )(matrix, d_pre, weight_one)
    blocks = [blocks[0]] + [across(blocks[k], k) for k in range(1, groups)]
    plane_parts, blocks = lax.optimization_barrier((plane_parts, blocks))

    sums = call(
        functools.partial(plane_sum_kernel, piece),
        (struct((piece, D), F32), *[struct((piece, D), BF16)] * (groups - 1)),
    )(*plane_parts)
    blocks = call(
        functools.partial(turn_kernel, count),
        tuple(struct((rows, D), BF16) for rows in plane_rows),
    )(*blocks, to_left, to_right)
    sums, blocks = lax.optimization_barrier((sums, blocks))
    shared = [sums[0]] + [across(sums[k], k) for k in range(1, groups)]
    blocks = [blocks[0]] + [in_plane(blocks[v], v) for v in range(1, PLANE)]
    shared, blocks = lax.optimization_barrier((shared, blocks))
    total = call(
        functools.partial(group_sum_kernel, 1.0 / math.sqrt(ROWS * count)),
        struct((piece, D), BF16),
    )(*shared)
    d_features = call(
        functools.partial(features_kernel, count),
        struct((ROWS, D), BF16),
        (pltpu.VMEM((ROWS, D), F32), pltpu.VMEM((count, SLOT, D), BF16)),
    )(matrix, own, *blocks)
    chunk = jnp.concatenate([total] + [across(total, k) for k in range(1, groups)], axis=0)
    chunks = [chunk] + [in_plane(chunk, v) for v in range(1, PLANE)]
    grad_two, grad_one = call(
        functools.partial(gather_kernel, count),
        (struct((D, D), BF16), struct((D, D), BF16)),
    )(*chunks)
    return d_features, grad_one, grad_two


def solution(mesh):
    placed = (
        P(("rep", "node"), None),
        P(("rep", "node"), None),
        P(),
        P(),
        P(("rep", "node"), None),
        P(("rep", "node"), None),
        P("rep", None),
        P("rep"),
    )
    return jax.shard_map(
        shards,
        mesh=mesh,
        in_specs=placed,
        out_specs=(P(("rep", "node"), None), P("rep", None), P("rep", None)),
        check_vma=False,
    )
```

```python
import functools
import math

import jax
import jax.numpy as jnp
from jax import lax
from jax.experimental import pallas as pl
from jax.experimental.pallas import tpu as pltpu
from jax.sharding import PartitionSpec as P

D = 512
K = 32
ROWS = 128
HALO = 32
BLK = 8
CAP = 2
SELF_WEIGHT = 8.0
SLOT = CAP * BLK
HALO_COL = ROWS
FAR_COL = 2 * ROWS
PLANE = 4

F32 = jnp.float32
BF16 = jnp.bfloat16
VMEM_LIMIT = 48 * 1024 * 1024


def nn(left, right):
    return jnp.dot(left, right, preferred_element_type=F32)


def nt(left, right):
    return lax.dot_general(left, right, (((1,), (1,)), ((), ())), preferred_element_type=F32)


def tn(left, right):
    return lax.dot_general(left, right, (((0,), (0,)), ((), ())), preferred_element_type=F32)


def iota(shape, dim):
    return lax.broadcasted_iota(jnp.int32, shape, dim)


def call(kernel, out_shape, scratch=(), **specs):
    return pl.pallas_call(
        kernel,
        out_shape=out_shape,
        **specs,
        scratch_shapes=list(scratch),
        compiler_params=pltpu.CompilerParams(vmem_limit_bytes=VMEM_LIMIT),
    )


def struct(shape, dtype):
    return jax.ShapeDtypeStruct(shape, dtype)


def prepare_kernel(
    count, nbr_hbm, wgt_hbm, tab_hbm, cnt_hbm, feat_hbm, up_hbm,
    mat_ref, own_ref, send_ref, fwd_ref, bwd_ref,
    nbr_ref, wgt_ref, tab_ref, cnt_ref, feat_ref, up_ref, sems, rows_scr, at_scr,
):
    inputs = (
        (tab_hbm, tab_ref), (cnt_hbm, cnt_ref), (nbr_hbm, nbr_ref),
        (wgt_hbm, wgt_ref), (up_hbm, up_ref), (feat_hbm, feat_ref),
    )
    copies = [
        pltpu.make_async_copy(src, dst, sems.at[i]) for i, (src, dst) in enumerate(inputs)
    ]
    for copy in copies:
        copy.start()
    copies[0].wait()
    copies[1].wait()
    device = lax.axis_index("node")
    first = device * ROWS
    far = count * SLOT
    pairs = count * count
    rows_scr[...] = jnp.zeros_like(rows_scr)
    rows_scr[0:CAP, :] = tab_ref[...].astype(F32)
    rows_scr[CAP : CAP + 1, :] = cnt_ref[...].astype(F32)
    step = min(pairs, 256)
    listed = jnp.zeros((far, 8), F32)
    asked = jnp.zeros((far, 8), F32)
    peer_wide = iota((far, step), 0) // SLOT
    for at in range(0, pairs, step):
        pair = iota((far, step), 1) + at
        rows = rows_scr[:, at : at + step].astype(BF16)
        mine = jnp.where(pair == device * count + peer_wide, 1.0, 0.0).astype(BF16)
        theirs = jnp.where(pair == peer_wide * count + device, 1.0, 0.0).astype(BF16)
        listed = listed + nt(mine, rows)
        asked = asked + nt(theirs, rows)
    listed = listed.astype(jnp.int32)
    asked = asked.astype(jnp.int32)
    col = iota((far, 1), 0)
    slot = col // BLK % CAP
    inner = col % BLK
    block = jnp.where(slot == 0, listed[:, 0:1], listed[:, 1:2])
    node = col // SLOT * ROWS + block * BLK + inner
    in_band = (node >= first - HALO) & (node < first + ROWS + HALO)
    far_node = jnp.where((slot < listed[:, 2:3]) & jnp.logical_not(in_band), node, -1)
    asked_row = jnp.where(slot == 0, asked[:, 0:1], asked[:, 1:2]) * BLK + inner

    copies[2].wait()
    copies[3].wait()
    weight = wgt_ref[...].astype(F32)
    neighbour = nbr_ref[...]

    def counted(nodes, total):
        for k in range(K):
            total = total + jnp.where(neighbour[k : k + 1, :] == nodes, weight[k : k + 1, :], 0.0)
        return total

    square = (ROWS, ROWS)
    row = iota(square, 0)
    at_scr[0:ROWS, :] = counted(first + row, jnp.where(row == iota(square, 1), SELF_WEIGHT, 0.0))
    rim = iota((2 * HALO, ROWS), 0)
    rim_node = first + jnp.where(rim < HALO, rim - HALO, rim - HALO + ROWS)
    at_scr[HALO_COL : HALO_COL + 2 * HALO, :] = counted(rim_node, jnp.zeros((2 * HALO, ROWS), F32))
    at_scr[HALO_COL + 2 * HALO : FAR_COL, :] = jnp.zeros((FAR_COL - HALO_COL - 2 * HALO, ROWS), F32)
    for at in range(0, far, ROWS):
        nodes = jnp.broadcast_to(far_node[at : at + ROWS], square)
        at_scr[FAR_COL + at : FAR_COL + at + ROWS, :] = counted(nodes, jnp.zeros(square, F32))

    adj_mat = at_scr[...]
    matrix = adj_mat.T
    adj_mat = adj_mat.astype(BF16)
    total = jnp.sum(matrix, axis=1, keepdims=True)
    mat_ref[:, 0 : FAR_COL + far] = matrix.astype(BF16)
    pick = jnp.where(asked_row == iota((far, ROWS), 1), 1.0, 0.0)
    mat_ref[:, FAR_COL + far :] = pick.T.astype(BF16)

    copies[4].wait()
    scaled = (up_ref[...].astype(F32) / total).astype(BF16)
    copies[5].wait()
    features = feat_ref[...]
    own_ref[...] = nn(adj_mat[0:ROWS], scaled)
    rims = nn(adj_mat[HALO_COL : HALO_COL + 2 * HALO], scaled).astype(BF16)
    fwd_ref[0:HALO, :] = features[ROWS - HALO : ROWS]
    fwd_ref[HALO : 2 * HALO, :] = rims[HALO : 2 * HALO]
    bwd_ref[0:HALO, :] = features[0:HALO]
    bwd_ref[HALO : 2 * HALO, :] = rims[0:HALO]
    rows_out = nn(pick.astype(BF16), features).astype(BF16)
    send_ref[:, 0:SLOT, :] = rows_out.reshape(count, SLOT, D)
    terms = nn(adj_mat[FAR_COL:], scaled).astype(BF16)
    send_ref[:, SLOT : 2 * SLOT, :] = terms.reshape(count, SLOT, D)


def row_total(mat_ref, far):
    return jnp.sum(mat_ref[:, 0 : FAR_COL + far].astype(F32), axis=1, keepdims=True)


def layer_kernel(
    count, mat_ref, feat_ref, own_ref, recv_ref, left_ref, right_ref, w_one_ref, w_two_ref,
    *refs,
):
    plane, piece = PLANE, 2 * D // count
    groups = count // plane
    part_refs = refs[:plane]
    d_pre_ref, rim_scr, u_scr, hidden_scr, agg_scr = refs[plane:]
    device = lax.axis_index("node")
    group, place = device // plane, device % plane
    far = count * SLOT
    total = row_total(mat_ref, far)
    rim_scr[0:HALO, :] = left_ref[0:HALO, :]
    rim_scr[HALO : 2 * HALO, :] = right_ref[0:HALO, :]
    rim_scr[2 * HALO :, :] = jnp.zeros((ROWS - 2 * HALO, D), BF16)
    sums = nn(mat_ref[:, 0:ROWS], feat_ref[...])
    sums = sums + nn(mat_ref[:, HALO_COL:FAR_COL], rim_scr[...])
    sums = sums + nn(
        mat_ref[:, FAR_COL : FAR_COL + far], recv_ref[:, 0:SLOT, :].reshape(far, D)
    )
    agg = (sums / total).astype(BF16)
    agg_scr[...] = agg
    u_scr[...] = own_ref[...] + nn(
        mat_ref[:, FAR_COL + far :], recv_ref[:, SLOT : 2 * SLOT, :].reshape(far, D)
    )
    u_scr[0:HALO, :] += left_ref[HALO : 2 * HALO, :].astype(F32)
    u_scr[ROWS - HALO : ROWS, :] += right_ref[HALO : 2 * HALO, :].astype(F32)
    u = u_scr[...].astype(BF16)
    back = nt(u, w_two_ref[...])
    pre = nn(agg, w_one_ref[...])
    square = pre * pre
    bend = jnp.tanh(0.7978845608 * pre * (1.0 + 0.044715 * square))
    hidden_scr[...] = (0.5 * pre * (1.0 + bend)).astype(BF16)
    slope = 0.5 * (1.0 + bend) + 0.5 * pre * (1.0 - bend * bend) * (
        0.7978845608 * (1.0 + 3.0 * 0.044715 * square)
    )
    d_pre = (back * slope).astype(BF16)
    d_pre_ref[...] = d_pre
    wide = D // plane
    for v in range(plane):
        cols = pl.ds(pl.multiple_of((place ^ v) * wide, wide), wide)
        for half, (left, right) in enumerate(((hidden_scr, u), (agg_scr, d_pre))):
            part = tn(left[:, cols], right).astype(part_refs[v].dtype)
            for j in range(groups // 2):
                to = lax.rem(half * (groups // 2) + j + groups - group, groups)
                part_refs[v][pl.ds(pl.multiple_of(to * piece, piece), piece), :] = part[
                    j * piece : (j + 1) * piece
                ]


def hop_bits(count):
    bits = [b for b in range(count.bit_length() - 1)]
    return [bits[2], bits[0], bits[1]] + bits[3:]


def hop_rows(count, bit):
    return count // 2 * SLOT + HALO * (2 if bit == 0 else 1)


def right_moves(device, bit):
    if bit == 2:
        return device % 4 == 3
    return device % (1 << bit) == 0


def pack_hop(count, bit, held_ref, left, right, out_ref):
    device = lax.axis_index("node")
    chosen = [r for r in range(count) if r >> bit & 1]
    for at, r in enumerate(chosen):
        out_ref[at * SLOT : (at + 1) * SLOT, :] = held_ref[r]
    size = len(chosen) * SLOT
    if bit == 0:
        out_ref[size : size + HALO, :] = left
        out_ref[size + HALO :, :] = right
    else:
        out_ref[size:, :] = jnp.where(right_moves(device, bit), right, left)


def unpack_hop(count, bit, got_ref, held_ref, left, right):
    device = lax.axis_index("node")
    chosen = [r for r in range(count) if r >> bit & 1]
    for at, r in enumerate(chosen):
        held_ref[r] = got_ref[at * SLOT : (at + 1) * SLOT, :]
    size = len(chosen) * SLOT
    if bit == 0:
        return got_ref[size : size + HALO, :], got_ref[size + HALO :, :]
    got = got_ref[size:, :]
    if bit == 2:
        moves = device % 4 == 0
    else:
        moves = device % (1 << bit) == (1 << bit) - 1
    return jnp.where(moves, got, left), jnp.where(right_moves(device, bit), got, right)


def back_kernel(
    count, bit, mat_ref, d_pre_ref, w_one_ref, own_ref, held_ref, left_ref, right_ref, out_ref
):
    device = lax.axis_index("node")
    far = count * SLOT
    q = (nt(d_pre_ref[...], w_one_ref[...]) / row_total(mat_ref, far)).astype(BF16)
    rims = tn(mat_ref[:, HALO_COL:FAR_COL], q).astype(BF16)
    left_ref[...] = rims[0:HALO]
    right_ref[...] = rims[HALO : 2 * HALO]
    terms = tn(mat_ref[:, FAR_COL : FAR_COL + far], q).astype(BF16).reshape(count, SLOT, D)
    for peer in range(count):
        held_ref[device ^ peer] = terms[peer]
    pack_hop(count, bit, held_ref, rims[0:HALO], rims[HALO : 2 * HALO], out_ref)
    own_ref[...] = tn(mat_ref[:, 0:ROWS], q)


def hop_kernel(
    count, last, bit, got_ref, was_ref, was_left_ref, was_right_ref,
    held_ref, left_ref, right_ref, out_ref,
):
    held_ref[...] = was_ref[...]
    left, right = unpack_hop(
        count, last, got_ref, held_ref, was_left_ref[...], was_right_ref[...]
    )
    left_ref[...] = left
    right_ref[...] = right
    pack_hop(count, bit, held_ref, left, right, out_ref)


def features_kernel(
    count, last, mat_ref, own_ref, got_ref, was_ref, was_left_ref, was_right_ref,
    out_ref, sum_scr, held_scr, block_scr,
):
    device = lax.axis_index("node")
    far = count * SLOT
    held_scr[...] = was_ref[...]
    left, right = unpack_hop(
        count, last, got_ref, held_scr, was_left_ref[...], was_right_ref[...]
    )
    for r in range(count):
        block_scr[device ^ r] = held_scr[r]
    sum_scr[...] = own_ref[...] + nn(mat_ref[:, FAR_COL + far :], block_scr[...].reshape(far, D))
    sum_scr[0:HALO, :] += right.astype(F32)
    sum_scr[ROWS - HALO : ROWS, :] += left.astype(F32)
    out_ref[...] = sum_scr[...].astype(BF16)


def plane_sum_kernel(piece, *refs):
    part_refs, out_refs = refs[:PLANE], refs[PLANE:]
    for k, out in enumerate(out_refs):
        rows = slice(k * piece, (k + 1) * piece)
        total = part_refs[0][rows, :].astype(F32)
        for ref in part_refs[1:]:
            total = total + ref[rows, :].astype(F32)
        out[...] = total.astype(out.dtype)


def group_sum_kernel(scale, *refs):
    total = refs[0][...]
    for ref in refs[1:-1]:
        total = total + ref[...].astype(F32)
    refs[-1][...] = (total * scale).astype(BF16)


def gather_kernel(count, *refs):
    piece, groups, wide = 2 * D // count, count // PLANE, D // PLANE
    device = lax.axis_index("node")
    group, place = device // PLANE, device % PLANE
    outs = refs[PLANE:]
    per = groups // 2
    for v in range(PLANE):
        row = (place ^ v) * wide
        for half in range(2):
            for j in range(per):
                at = lax.rem(group + 2 * groups - (half * per + j), groups)
                rows = refs[v][pl.ds(pl.multiple_of(at * piece, piece), piece), :]
                outs[half][pl.ds(pl.multiple_of(row + j * piece, piece), piece), :] = rows


def shards(
    features, upstream, weight_one, weight_two, neighbours, edge_weight, fetch_block, fetch_count
):
    count = lax.axis_size("node")
    groups = count // PLANE
    piece = 2 * D // count
    far = count * SLOT
    chain = FAR_COL + far
    up = [(i, i + 1) for i in range(count - 1)]
    down = [(i + 1, i) for i in range(count - 1)]

    def in_plane(value, v):
        return lax.ppermute(value, "node", [(i, i ^ v) for i in range(count)])

    def across(value, k):
        return lax.ppermute(
            value, "node", [(i, (i + k * PLANE) % count) for i in range(count)]
        )

    matrix, own, send, to_right, to_left = call(
        functools.partial(prepare_kernel, count),
        (
            struct((ROWS, chain + far), BF16),
            struct((ROWS, D), F32),
            struct((count, 2 * SLOT, D), BF16),
            struct((2 * HALO, D), BF16),
            struct((2 * HALO, D), BF16),
        ),
        (
            pltpu.VMEM((K, ROWS), jnp.int32),
            pltpu.VMEM((K, ROWS), jnp.int32),
            pltpu.VMEM((CAP, count * count), jnp.int32),
            pltpu.VMEM((1, count * count), jnp.int32),
            pltpu.VMEM((ROWS, D), BF16),
            pltpu.VMEM((ROWS, D), BF16),
            pltpu.SemaphoreType.DMA((6,)),
            pltpu.VMEM((8, count * count), F32),
            pltpu.VMEM((chain, ROWS), F32),
        ),
        in_specs=[pl.BlockSpec(memory_space=pltpu.HBM)] * 6,
    )(
        neighbours.T, edge_weight.T, fetch_block.T, fetch_count.reshape(1, -1), features, upstream
    )
    from_left = lax.ppermute(to_right, "node", up)
    from_right = lax.ppermute(to_left, "node", down)
    received = lax.all_to_all(send, "node", split_axis=0, concat_axis=0, tiled=True)

    *parts, d_pre = call(
        functools.partial(layer_kernel, count),
        (
            struct((2 * D // PLANE, D), F32),
            *[struct((2 * D // PLANE, D), BF16)] * (PLANE - 1),
            struct((ROWS, D), BF16),
        ),
        (
            pltpu.VMEM((ROWS, D), BF16),
            pltpu.VMEM((ROWS, D), F32),
            pltpu.VMEM((ROWS, D), BF16),
            pltpu.VMEM((ROWS, D), BF16),
        ),
    )(matrix, features, own, received, from_left, from_right, weight_one, weight_two)
    plane_parts = [parts[0]] + [in_plane(parts[v], v) for v in range(1, PLANE)]

    bits = hop_bits(count)
    carried = (
        struct((count, SLOT, D), BF16),
        struct((HALO, D), BF16),
        struct((HALO, D), BF16),
    )

    def message(bit):
        return struct((hop_rows(count, bit), D), BF16)

    def swap(value, bit):
        return lax.ppermute(value, "node", [(i, i ^ (1 << bit)) for i in range(count)])

    def next_hop(at, got, held):
        *held, out = call(
            functools.partial(hop_kernel, count, bits[at - 1], bits[at]),
            (*carried, message(bits[at])),
        )(got, *held)
        return out, held

    own, *held, out = call(
        functools.partial(back_kernel, count, bits[0]),
        (struct((ROWS, D), F32), *carried, message(bits[0])),
    )(matrix, d_pre, weight_one)
    plane_parts, got = lax.optimization_barrier((plane_parts, swap(out, bits[0])))

    sums = call(
        functools.partial(plane_sum_kernel, piece),
        (struct((piece, D), F32), *[struct((piece, D), BF16)] * (groups - 1)),
    )(*plane_parts)
    out, held = next_hop(1, got, held)
    sums, out = lax.optimization_barrier((sums, out))
    shared = [sums[0]] + [across(sums[k], k) for k in range(1, groups)]
    shared, got = lax.optimization_barrier((shared, swap(out, bits[1])))

    total = call(
        functools.partial(group_sum_kernel, 1.0 / math.sqrt(ROWS * count)),
        struct((piece, D), BF16),
    )(*shared)
    out, held = next_hop(2, got, held)
    total, out = lax.optimization_barrier((total, out))
    pieces = [total] + [across(total, k) for k in range(1, groups)]
    pieces, got = lax.optimization_barrier((pieces, swap(out, bits[2])))

    chunk = jnp.concatenate(pieces, axis=0)
    out, held = next_hop(3, got, held)
    chunk, out = lax.optimization_barrier((chunk, out))
    chunks = [chunk] + [in_plane(chunk, v) for v in range(1, PLANE)]
    got = swap(out, bits[3])
    for at in range(4, len(bits)):
        out, held = next_hop(at, got, held)
        got = swap(out, bits[at])
    d_features = call(
        functools.partial(features_kernel, count, bits[-1]),
        struct((ROWS, D), BF16),
        (
            pltpu.VMEM((ROWS, D), F32),
            pltpu.VMEM((count, SLOT, D), BF16),
            pltpu.VMEM((count, SLOT, D), BF16),
        ),
    )(matrix, own, got, *held)
    grad_two, grad_one = call(
        functools.partial(gather_kernel, count),
        (struct((D, D), BF16), struct((D, D), BF16)),
    )(*chunks)
    return d_features, grad_one, grad_two


def solution(mesh):
    placed = (
        P(("rep", "node"), None),
        P(("rep", "node"), None),
        P(),
        P(),
        P(("rep", "node"), None),
        P(("rep", "node"), None),
        P("rep", None),
        P("rep"),
    )
    return jax.shard_map(
        shards,
        mesh=mesh,
        in_specs=placed,
        out_specs=(P(("rep", "node"), None), P("rep", None), P("rep", None)),
        check_vma=False,
    )
```

```python
import functools
import math

import jax
import jax.numpy as jnp
from jax import lax
from jax.experimental import pallas as pl
from jax.experimental.pallas import tpu as pltpu
from jax.sharding import PartitionSpec as P

D = 512
K = 32
ROWS = 128
HALO = 32
BLK = 8
CAP = 2
SELF_WEIGHT = 8.0
SLOT = CAP * BLK
HALO_COL = ROWS
FAR_COL = 2 * ROWS
PLANE = 4

F32 = jnp.float32
BF16 = jnp.bfloat16
VMEM_LIMIT = 48 * 1024 * 1024


def nn(left, right):
    return jnp.dot(left, right, preferred_element_type=F32)


def nt(left, right):
    return lax.dot_general(left, right, (((1,), (1,)), ((), ())), preferred_element_type=F32)


def tn(left, right):
    return lax.dot_general(left, right, (((0,), (0,)), ((), ())), preferred_element_type=F32)


def iota(shape, dim):
    return lax.broadcasted_iota(jnp.int32, shape, dim)


def call(kernel, out_shape, scratch=(), **specs):
    return pl.pallas_call(
        kernel,
        out_shape=out_shape,
        **specs,
        scratch_shapes=list(scratch),
        compiler_params=pltpu.CompilerParams(vmem_limit_bytes=VMEM_LIMIT),
    )


def struct(shape, dtype):
    return jax.ShapeDtypeStruct(shape, dtype)


def prepare_kernel(
    count, nbr_hbm, wgt_hbm, tab_hbm, cnt_hbm, feat_hbm, up_hbm,
    mat_ref, own_ref, send_ref, fwd_ref, bwd_ref,
    nbr_ref, wgt_ref, tab_ref, cnt_ref, feat_ref, up_ref, sems, rows_scr, at_scr,
):
    inputs = (
        (tab_hbm, tab_ref), (cnt_hbm, cnt_ref), (nbr_hbm, nbr_ref),
        (wgt_hbm, wgt_ref), (up_hbm, up_ref), (feat_hbm, feat_ref),
    )
    copies = [
        pltpu.make_async_copy(src, dst, sems.at[i]) for i, (src, dst) in enumerate(inputs)
    ]
    for copy in copies:
        copy.start()
    copies[0].wait()
    copies[1].wait()
    device = lax.axis_index("node")
    first = device * ROWS
    far = count * SLOT
    pairs = count * count
    rows_scr[...] = jnp.zeros_like(rows_scr)
    rows_scr[0:CAP, :] = tab_ref[...].astype(F32)
    rows_scr[CAP : CAP + 1, :] = cnt_ref[...].astype(F32)
    step = min(pairs, 256)
    listed = jnp.zeros((far, 8), F32)
    asked = jnp.zeros((far, 8), F32)
    peer_wide = iota((far, step), 0) // SLOT
    for at in range(0, pairs, step):
        pair = iota((far, step), 1) + at
        rows = rows_scr[:, at : at + step].astype(BF16)
        mine = jnp.where(pair == device * count + peer_wide, 1.0, 0.0).astype(BF16)
        theirs = jnp.where(pair == peer_wide * count + device, 1.0, 0.0).astype(BF16)
        listed = listed + nt(mine, rows)
        asked = asked + nt(theirs, rows)
    listed = listed.astype(jnp.int32)
    asked = asked.astype(jnp.int32)
    col = iota((far, 1), 0)
    slot = col // BLK % CAP
    inner = col % BLK
    block = jnp.where(slot == 0, listed[:, 0:1], listed[:, 1:2])
    node = col // SLOT * ROWS + block * BLK + inner
    in_band = (node >= first - HALO) & (node < first + ROWS + HALO)
    far_node = jnp.where((slot < listed[:, 2:3]) & jnp.logical_not(in_band), node, -1)
    asked_row = jnp.where(slot == 0, asked[:, 0:1], asked[:, 1:2]) * BLK + inner

    copies[2].wait()
    copies[3].wait()
    weight = wgt_ref[...].astype(F32)
    neighbour = nbr_ref[...]

    def counted(nodes, total):
        for k in range(K):
            total = total + jnp.where(neighbour[k : k + 1, :] == nodes, weight[k : k + 1, :], 0.0)
        return total

    square = (ROWS, ROWS)
    row = iota(square, 0)
    at_scr[0:ROWS, :] = counted(first + row, jnp.where(row == iota(square, 1), SELF_WEIGHT, 0.0))
    rim = iota((2 * HALO, ROWS), 0)
    rim_node = first + jnp.where(rim < HALO, rim - HALO, rim - HALO + ROWS)
    at_scr[HALO_COL : HALO_COL + 2 * HALO, :] = counted(rim_node, jnp.zeros((2 * HALO, ROWS), F32))
    at_scr[HALO_COL + 2 * HALO : FAR_COL, :] = jnp.zeros((FAR_COL - HALO_COL - 2 * HALO, ROWS), F32)
    for at in range(0, far, ROWS):
        nodes = jnp.broadcast_to(far_node[at : at + ROWS], square)
        at_scr[FAR_COL + at : FAR_COL + at + ROWS, :] = counted(nodes, jnp.zeros(square, F32))

    adj_mat = at_scr[...]
    matrix = adj_mat.T
    adj_mat = adj_mat.astype(BF16)
    total = jnp.sum(matrix, axis=1, keepdims=True)
    mat_ref[:, 0 : FAR_COL + far] = matrix.astype(BF16)
    pick = jnp.where(asked_row == iota((far, ROWS), 1), 1.0, 0.0)
    mat_ref[:, FAR_COL + far :] = pick.T.astype(BF16)

    copies[4].wait()
    scaled = (up_ref[...].astype(F32) / total).astype(BF16)
    copies[5].wait()
    features = feat_ref[...]
    own_ref[...] = nn(adj_mat[0:ROWS], scaled)
    rims = nn(adj_mat[HALO_COL : HALO_COL + 2 * HALO], scaled).astype(BF16)
    fwd_ref[0:HALO, :] = features[ROWS - HALO : ROWS]
    fwd_ref[HALO : 2 * HALO, :] = rims[HALO : 2 * HALO]
    bwd_ref[0:HALO, :] = features[0:HALO]
    bwd_ref[HALO : 2 * HALO, :] = rims[0:HALO]
    rows_out = nn(pick.astype(BF16), features).astype(BF16)
    send_ref[:, 0:SLOT, :] = rows_out.reshape(count, SLOT, D)
    terms = nn(adj_mat[FAR_COL:], scaled).astype(BF16)
    send_ref[:, SLOT : 2 * SLOT, :] = terms.reshape(count, SLOT, D)


def row_total(mat_ref, far):
    return jnp.sum(mat_ref[:, 0 : FAR_COL + far].astype(F32), axis=1, keepdims=True)


def layer_kernel(
    count, mat_ref, feat_ref, own_ref, recv_ref, left_ref, right_ref, w_one_ref, w_two_ref,
    *refs,
):
    plane, piece = PLANE, 2 * D // count
    groups = count // plane
    part_refs = refs[:plane]
    d_pre_ref, rim_scr, u_scr, hidden_scr, agg_scr = refs[plane:]
    device = lax.axis_index("node")
    group, place = device // plane, device % plane
    far = count * SLOT
    total = row_total(mat_ref, far)
    rim_scr[0:HALO, :] = left_ref[0:HALO, :]
    rim_scr[HALO : 2 * HALO, :] = right_ref[0:HALO, :]
    rim_scr[2 * HALO :, :] = jnp.zeros((ROWS - 2 * HALO, D), BF16)
    sums = nn(mat_ref[:, 0:ROWS], feat_ref[...])
    sums = sums + nn(mat_ref[:, HALO_COL:FAR_COL], rim_scr[...])
    sums = sums + nn(
        mat_ref[:, FAR_COL : FAR_COL + far], recv_ref[:, 0:SLOT, :].reshape(far, D)
    )
    agg = (sums / total).astype(BF16)
    agg_scr[...] = agg
    u_scr[...] = own_ref[...] + nn(
        mat_ref[:, FAR_COL + far :], recv_ref[:, SLOT : 2 * SLOT, :].reshape(far, D)
    )
    u_scr[0:HALO, :] += left_ref[HALO : 2 * HALO, :].astype(F32)
    u_scr[ROWS - HALO : ROWS, :] += right_ref[HALO : 2 * HALO, :].astype(F32)
    u = u_scr[...].astype(BF16)
    back = nt(u, w_two_ref[...])
    pre = nn(agg, w_one_ref[...])
    square = pre * pre
    bend = jnp.tanh(0.7978845608 * pre * (1.0 + 0.044715 * square))
    hidden_scr[...] = (0.5 * pre * (1.0 + bend)).astype(BF16)
    slope = 0.5 * (1.0 + bend) + 0.5 * pre * (1.0 - bend * bend) * (
        0.7978845608 * (1.0 + 3.0 * 0.044715 * square)
    )
    d_pre = (back * slope).astype(BF16)
    d_pre_ref[...] = d_pre
    wide = D // plane
    for v in range(plane):
        cols = pl.ds(pl.multiple_of((place ^ v) * wide, wide), wide)
        for half, (left, right) in enumerate(((hidden_scr, u), (agg_scr, d_pre))):
            part = tn(left[:, cols], right).astype(part_refs[v].dtype)
            for j in range(groups // 2):
                to = lax.rem(half * (groups // 2) + j + groups - group, groups)
                part_refs[v][pl.ds(pl.multiple_of(to * piece, piece), piece), :] = part[
                    j * piece : (j + 1) * piece
                ]


def hop_bits(count):
    bits = [b for b in range(count.bit_length() - 1)]
    return [bits[2], bits[0], bits[1]] + bits[3:]


def hop_rows(count, bit):
    return count // 2 * SLOT + HALO * (2 if bit == 0 else 1)


def right_moves(device, bit):
    if bit == 2:
        return device % 4 == 3
    return device % (1 << bit) == 0


def pack_hop(count, bit, held_ref, left, right, out_ref):
    device = lax.axis_index("node")
    chosen = [r for r in range(count) if r >> bit & 1]
    for at, r in enumerate(chosen):
        out_ref[at * SLOT : (at + 1) * SLOT, :] = held_ref[r]
    size = len(chosen) * SLOT
    if bit == 0:
        out_ref[size : size + HALO, :] = left
        out_ref[size + HALO :, :] = right
    else:
        out_ref[size:, :] = jnp.where(right_moves(device, bit), right, left)


def unpack_hop(count, bit, got_ref, held_ref, left, right):
    device = lax.axis_index("node")
    chosen = [r for r in range(count) if r >> bit & 1]
    for at, r in enumerate(chosen):
        held_ref[r] = got_ref[at * SLOT : (at + 1) * SLOT, :]
    size = len(chosen) * SLOT
    if bit == 0:
        return got_ref[size : size + HALO, :], got_ref[size + HALO :, :]
    got = got_ref[size:, :]
    if bit == 2:
        moves = device % 4 == 0
    else:
        moves = device % (1 << bit) == (1 << bit) - 1
    return jnp.where(moves, got, left), jnp.where(right_moves(device, bit), got, right)


def back_kernel(
    count, bit, mat_ref, d_pre_ref, w_one_ref, own_ref, held_ref, left_ref, right_ref, out_ref
):
    device = lax.axis_index("node")
    far = count * SLOT
    q = (nt(d_pre_ref[...], w_one_ref[...]) / row_total(mat_ref, far)).astype(BF16)
    rims = tn(mat_ref[:, HALO_COL:FAR_COL], q).astype(BF16)
    left_ref[...] = rims[0:HALO]
    right_ref[...] = rims[HALO : 2 * HALO]
    terms = tn(mat_ref[:, FAR_COL : FAR_COL + far], q).astype(BF16).reshape(count, SLOT, D)
    for peer in range(count):
        held_ref[device ^ peer] = terms[peer]
    pack_hop(count, bit, held_ref, rims[0:HALO], rims[HALO : 2 * HALO], out_ref)
    own_ref[...] = tn(mat_ref[:, 0:ROWS], q)


def hop_kernel(
    count, last, bit, got_ref, was_ref, was_left_ref, was_right_ref,
    held_ref, left_ref, right_ref, out_ref,
):
    held_ref[...] = was_ref[...]
    left, right = unpack_hop(
        count, last, got_ref, held_ref, was_left_ref[...], was_right_ref[...]
    )
    left_ref[...] = left
    right_ref[...] = right
    pack_hop(count, bit, held_ref, left, right, out_ref)


def features_kernel(
    count, last, mat_ref, own_ref, got_ref, was_ref, was_left_ref, was_right_ref,
    out_ref, sum_scr, held_scr, block_scr,
):
    device = lax.axis_index("node")
    far = count * SLOT
    held_scr[...] = was_ref[...]
    left, right = unpack_hop(
        count, last, got_ref, held_scr, was_left_ref[...], was_right_ref[...]
    )
    for r in range(count):
        block_scr[device ^ r] = held_scr[r]
    sum_scr[...] = own_ref[...] + nn(mat_ref[:, FAR_COL + far :], block_scr[...].reshape(far, D))
    sum_scr[0:HALO, :] += right.astype(F32)
    sum_scr[ROWS - HALO : ROWS, :] += left.astype(F32)
    out_ref[...] = sum_scr[...].astype(BF16)


def plane_sum_kernel(piece, *refs):
    part_refs, out_refs = refs[:PLANE], refs[PLANE:]
    for k, out in enumerate(out_refs):
        rows = slice(k * piece, (k + 1) * piece)
        total = part_refs[0][rows, :].astype(F32)
        for ref in part_refs[1:]:
            total = total + ref[rows, :].astype(F32)
        out[...] = total.astype(out.dtype)


def group_sum_kernel(scale, *refs):
    total = refs[0][...]
    for ref in refs[1:-1]:
        total = total + ref[...].astype(F32)
    refs[-1][...] = (total * scale).astype(BF16)


def gather_kernel(count, *refs):
    piece, groups, wide = 2 * D // count, count // PLANE, D // PLANE
    device = lax.axis_index("node")
    group, place = device // PLANE, device % PLANE
    outs = refs[PLANE:]
    per = groups // 2
    for v in range(PLANE):
        row = (place ^ v) * wide
        for half in range(2):
            for j in range(per):
                at = lax.rem(group + 2 * groups - (half * per + j), groups)
                rows = refs[v][pl.ds(pl.multiple_of(at * piece, piece), piece), :]
                outs[half][pl.ds(pl.multiple_of(row + j * piece, piece), piece), :] = rows


def shards(
    features, upstream, weight_one, weight_two, neighbours, edge_weight, fetch_block, fetch_count
):
    count = lax.axis_size("node")
    groups = count // PLANE
    piece = 2 * D // count
    far = count * SLOT
    chain = FAR_COL + far
    up = [(i, i + 1) for i in range(count - 1)]
    down = [(i + 1, i) for i in range(count - 1)]

    def in_plane(value, v):
        return lax.ppermute(value, "node", [(i, i ^ v) for i in range(count)])

    def across(value, k):
        return lax.ppermute(
            value, "node", [(i, (i + k * PLANE) % count) for i in range(count)]
        )

    matrix, own, send, to_right, to_left = call(
        functools.partial(prepare_kernel, count),
        (
            struct((ROWS, chain + far), BF16),
            struct((ROWS, D), F32),
            struct((count, 2 * SLOT, D), BF16),
            struct((2 * HALO, D), BF16),
            struct((2 * HALO, D), BF16),
        ),
        (
            pltpu.VMEM((K, ROWS), jnp.int32),
            pltpu.VMEM((K, ROWS), jnp.int32),
            pltpu.VMEM((CAP, count * count), jnp.int32),
            pltpu.VMEM((1, count * count), jnp.int32),
            pltpu.VMEM((ROWS, D), BF16),
            pltpu.VMEM((ROWS, D), BF16),
            pltpu.SemaphoreType.DMA((6,)),
            pltpu.VMEM((8, count * count), F32),
            pltpu.VMEM((chain, ROWS), F32),
        ),
        in_specs=[pl.BlockSpec(memory_space=pltpu.HBM)] * 6,
    )(
        *(
            pltpu.with_memory_space_constraint(value, pltpu.HBM)
            for value in (
                neighbours.T, edge_weight.T, fetch_block.T, fetch_count.reshape(1, -1),
                features, upstream,
            )
        )
    )
    from_left = lax.ppermute(to_right, "node", up)
    from_right = lax.ppermute(to_left, "node", down)
    received = lax.all_to_all(send, "node", split_axis=0, concat_axis=0, tiled=True)

    *parts, d_pre = call(
        functools.partial(layer_kernel, count),
        (
            struct((2 * D // PLANE, D), F32),
            *[struct((2 * D // PLANE, D), BF16)] * (PLANE - 1),
            struct((ROWS, D), BF16),
        ),
        (
            pltpu.VMEM((ROWS, D), BF16),
            pltpu.VMEM((ROWS, D), F32),
            pltpu.VMEM((ROWS, D), BF16),
            pltpu.VMEM((ROWS, D), BF16),
        ),
    )(matrix, features, own, received, from_left, from_right, weight_one, weight_two)
    plane_parts = [parts[0]] + [in_plane(parts[v], v) for v in range(1, PLANE)]

    bits = hop_bits(count)
    carried = (
        struct((count, SLOT, D), BF16),
        struct((HALO, D), BF16),
        struct((HALO, D), BF16),
    )

    def message(bit):
        return struct((hop_rows(count, bit), D), BF16)

    def swap(value, bit):
        return lax.ppermute(value, "node", [(i, i ^ (1 << bit)) for i in range(count)])

    def next_hop(at, got, held):
        *held, out = call(
            functools.partial(hop_kernel, count, bits[at - 1], bits[at]),
            (*carried, message(bits[at])),
        )(got, *held)
        return out, held

    own, *held, out = call(
        functools.partial(back_kernel, count, bits[0]),
        (struct((ROWS, D), F32), *carried, message(bits[0])),
    )(matrix, d_pre, weight_one)
    plane_parts, got = lax.optimization_barrier((plane_parts, swap(out, bits[0])))

    sums = call(
        functools.partial(plane_sum_kernel, piece),
        (struct((piece, D), F32), *[struct((piece, D), BF16)] * (groups - 1)),
    )(*plane_parts)
    out, held = next_hop(1, got, held)
    sums, out = lax.optimization_barrier((sums, out))
    shared = [sums[0]] + [across(sums[k], k) for k in range(1, groups)]
    shared, got = lax.optimization_barrier((shared, swap(out, bits[1])))

    total = call(
        functools.partial(group_sum_kernel, 1.0 / math.sqrt(ROWS * count)),
        struct((piece, D), BF16),
    )(*shared)
    out, held = next_hop(2, got, held)
    total, out = lax.optimization_barrier((total, out))
    pieces = [total] + [across(total, k) for k in range(1, groups)]
    pieces, got = lax.optimization_barrier((pieces, swap(out, bits[2])))

    chunk = jnp.concatenate(pieces, axis=0)
    out, held = next_hop(3, got, held)
    chunk, out = lax.optimization_barrier((chunk, out))
    chunks = [chunk] + [in_plane(chunk, v) for v in range(1, PLANE)]
    got = swap(out, bits[3])
    for at in range(4, len(bits)):
        out, held = next_hop(at, got, held)
        got = swap(out, bits[at])
    d_features = call(
        functools.partial(features_kernel, count, bits[-1]),
        struct((ROWS, D), BF16),
        (
            pltpu.VMEM((ROWS, D), F32),
            pltpu.VMEM((count, SLOT, D), BF16),
            pltpu.VMEM((count, SLOT, D), BF16),
        ),
    )(matrix, own, got, *held)
    grad_two, grad_one = call(
        functools.partial(gather_kernel, count),
        (struct((D, D), BF16), struct((D, D), BF16)),
    )(*chunks)
    return d_features, grad_one, grad_two


def solution(mesh):
    placed = (
        P(("rep", "node"), None),
        P(("rep", "node"), None),
        P(),
        P(),
        P(("rep", "node"), None),
        P(("rep", "node"), None),
        P("rep", None),
        P("rep"),
    )
    return jax.shard_map(
        shards,
        mesh=mesh,
        in_specs=placed,
        out_specs=(P(("rep", "node"), None), P("rep", None), P("rep", None)),
        check_vma=False,
    )
```

```python
import functools
import math

import jax
import jax.numpy as jnp
from jax import lax
from jax.experimental import pallas as pl
from jax.experimental.pallas import tpu as pltpu
from jax.sharding import PartitionSpec as P

D = 512
K = 32
ROWS = 128
HALO = 32
BLK = 8
CAP = 2
SELF_WEIGHT = 8.0
SLOT = CAP * BLK
HALO_COL = ROWS
FAR_COL = 2 * ROWS
PLANE = 4

F32 = jnp.float32
BF16 = jnp.bfloat16
VMEM_LIMIT = 48 * 1024 * 1024


def nn(left, right):
    return jnp.dot(left, right, preferred_element_type=F32)


def nt(left, right):
    return lax.dot_general(left, right, (((1,), (1,)), ((), ())), preferred_element_type=F32)


def tn(left, right):
    return lax.dot_general(left, right, (((0,), (0,)), ((), ())), preferred_element_type=F32)


def iota(shape, dim):
    return lax.broadcasted_iota(jnp.int32, shape, dim)


def call(kernel, out_shape, scratch=(), **specs):
    return pl.pallas_call(
        kernel,
        out_shape=out_shape,
        **specs,
        scratch_shapes=list(scratch),
        compiler_params=pltpu.CompilerParams(vmem_limit_bytes=VMEM_LIMIT),
    )


def struct(shape, dtype):
    return jax.ShapeDtypeStruct(shape, dtype)


def prepare_kernel(
    count, nbr_hbm, wgt_hbm, tab_hbm, cnt_hbm, feat_hbm, up_hbm,
    mat_ref, own_ref, send_ref, near_ref, next_ref,
    nbr_ref, wgt_ref, tab_ref, cnt_ref, feat_ref, up_ref, sems, rows_scr, at_scr,
):
    inputs = (
        (tab_hbm, tab_ref), (cnt_hbm, cnt_ref), (nbr_hbm, nbr_ref),
        (wgt_hbm, wgt_ref), (up_hbm, up_ref), (feat_hbm, feat_ref),
    )
    copies = [
        pltpu.make_async_copy(src, dst, sems.at[i]) for i, (src, dst) in enumerate(inputs)
    ]
    for copy in copies:
        copy.start()
    copies[0].wait()
    copies[1].wait()
    device = lax.axis_index("node")
    first = device * ROWS
    far = count * SLOT
    pairs = count * count
    rows_scr[...] = jnp.zeros_like(rows_scr)
    rows_scr[0:CAP, :] = tab_ref[...].astype(F32)
    rows_scr[CAP : CAP + 1, :] = cnt_ref[...].astype(F32)
    step = min(pairs, 256)
    listed = jnp.zeros((far, 8), F32)
    asked = jnp.zeros((far, 8), F32)
    peer_wide = iota((far, step), 0) // SLOT
    for at in range(0, pairs, step):
        pair = iota((far, step), 1) + at
        rows = rows_scr[:, at : at + step].astype(BF16)
        mine = jnp.where(pair == device * count + peer_wide, 1.0, 0.0).astype(BF16)
        theirs = jnp.where(pair == peer_wide * count + device, 1.0, 0.0).astype(BF16)
        listed = listed + nt(mine, rows)
        asked = asked + nt(theirs, rows)
    listed = listed.astype(jnp.int32)
    asked = asked.astype(jnp.int32)
    col = iota((far, 1), 0)
    slot = col // BLK % CAP
    inner = col % BLK
    block = jnp.where(slot == 0, listed[:, 0:1], listed[:, 1:2])
    node = col // SLOT * ROWS + block * BLK + inner
    in_band = (node >= first - HALO) & (node < first + ROWS + HALO)
    far_node = jnp.where((slot < listed[:, 2:3]) & jnp.logical_not(in_band), node, -1)
    asked_row = jnp.where(slot == 0, asked[:, 0:1], asked[:, 1:2]) * BLK + inner

    copies[2].wait()
    copies[3].wait()
    weight = wgt_ref[...].astype(F32)
    neighbour = nbr_ref[...]

    def counted(nodes, total):
        for k in range(K):
            total = total + jnp.where(neighbour[k : k + 1, :] == nodes, weight[k : k + 1, :], 0.0)
        return total

    square = (ROWS, ROWS)
    row = iota(square, 0)
    at_scr[0:ROWS, :] = counted(first + row, jnp.where(row == iota(square, 1), SELF_WEIGHT, 0.0))
    rim = iota((2 * HALO, ROWS), 0)
    rim_node = first + jnp.where(rim < HALO, rim - HALO, rim - HALO + ROWS)
    at_scr[HALO_COL : HALO_COL + 2 * HALO, :] = counted(rim_node, jnp.zeros((2 * HALO, ROWS), F32))
    at_scr[HALO_COL + 2 * HALO : FAR_COL, :] = jnp.zeros((FAR_COL - HALO_COL - 2 * HALO, ROWS), F32)
    for at in range(0, far, ROWS):
        nodes = jnp.broadcast_to(far_node[at : at + ROWS], square)
        at_scr[FAR_COL + at : FAR_COL + at + ROWS, :] = counted(nodes, jnp.zeros(square, F32))

    adj_mat = at_scr[...]
    matrix = adj_mat.T
    adj_mat = adj_mat.astype(BF16)
    total = jnp.sum(matrix, axis=1, keepdims=True)
    mat_ref[:, 0 : FAR_COL + far] = matrix.astype(BF16)
    pick = jnp.where(asked_row == iota((far, ROWS), 1), 1.0, 0.0)
    mat_ref[:, FAR_COL + far :] = pick.T.astype(BF16)

    copies[4].wait()
    scaled = (up_ref[...].astype(F32) / total).astype(BF16)
    copies[5].wait()
    features = feat_ref[...]
    own_ref[...] = nn(adj_mat[0:ROWS], scaled)
    rims = nn(adj_mat[HALO_COL : HALO_COL + 2 * HALO], scaled).astype(BF16)
    even = device % 2 == 0
    low, high = features[0:HALO], features[ROWS - HALO : ROWS]
    near_ref[0:HALO, :] = jnp.where(even, high, low)
    near_ref[HALO:, :] = jnp.where(even, rims[HALO:], rims[0:HALO])
    next_ref[0:HALO, :] = jnp.where(even, low, high)
    next_ref[HALO:, :] = jnp.where(even, rims[0:HALO], rims[HALO:])
    rows_out = nn(pick.astype(BF16), features).astype(BF16)
    send_ref[:, 0:SLOT, :] = rows_out.reshape(count, SLOT, D)
    terms = nn(adj_mat[FAR_COL:], scaled).astype(BF16)
    send_ref[:, SLOT : 2 * SLOT, :] = terms.reshape(count, SLOT, D)


def row_total(mat_ref, far):
    return jnp.sum(mat_ref[:, 0 : FAR_COL + far].astype(F32), axis=1, keepdims=True)


def layer_kernel(
    count, mat_ref, feat_ref, own_ref, recv_ref, near_ref, next_ref, w_one_ref, w_two_ref,
    *refs,
):
    part_refs = refs[:PLANE]
    d_pre_ref, rim_scr, u_scr, hidden_scr, agg_scr = refs[PLANE:]
    device = lax.axis_index("node")
    place, side = device % PLANE, device // PLANE % 2
    even = device % 2 == 0
    left = jnp.where(even, next_ref[...], near_ref[...])
    right = jnp.where(even, near_ref[...], next_ref[...])
    far = count * SLOT
    total = row_total(mat_ref, far)
    rim_scr[0:HALO, :] = left[0:HALO]
    rim_scr[HALO : 2 * HALO, :] = right[0:HALO]
    rim_scr[2 * HALO :, :] = jnp.zeros((ROWS - 2 * HALO, D), BF16)
    sums = nn(mat_ref[:, 0:ROWS], feat_ref[...])
    sums = sums + nn(mat_ref[:, HALO_COL:FAR_COL], rim_scr[...])
    sums = sums + nn(
        mat_ref[:, FAR_COL : FAR_COL + far], recv_ref[:, 0:SLOT, :].reshape(far, D)
    )
    agg = (sums / total).astype(BF16)
    agg_scr[...] = agg
    u_scr[...] = own_ref[...] + nn(
        mat_ref[:, FAR_COL + far :], recv_ref[:, SLOT : 2 * SLOT, :].reshape(far, D)
    )
    u_scr[0:HALO, :] += left[HALO:].astype(F32)
    u_scr[ROWS - HALO : ROWS, :] += right[HALO:].astype(F32)
    u = u_scr[...].astype(BF16)
    back = nt(u, w_two_ref[...])
    pre = nn(agg, w_one_ref[...])
    square = pre * pre
    bend = jnp.tanh(0.7978845608 * pre * (1.0 + 0.044715 * square))
    hidden_scr[...] = (0.5 * pre * (1.0 + bend)).astype(BF16)
    slope = 0.5 * (1.0 + bend) + 0.5 * pre * (1.0 - bend * bend) * (
        0.7978845608 * (1.0 + 3.0 * 0.044715 * square)
    )
    d_pre = (back * slope).astype(BF16)
    d_pre_ref[...] = d_pre
    wide = D // PLANE
    for v in range(PLANE):
        cols = pl.ds(pl.multiple_of((place ^ v) * wide, wide), wide)
        for half, (first, second) in enumerate(((hidden_scr, u), (agg_scr, d_pre))):
            rows = pl.ds(pl.multiple_of((side ^ half) * wide, wide), wide)
            part_refs[v][rows, :] = tn(first[:, cols], second).astype(part_refs[v].dtype)


def hop_bits(count):
    bits = [b for b in range(count.bit_length() - 1)]
    return [bits[2], bits[0], bits[1]] + bits[3:]


def hop_rows(count, bit):
    return count // 2 * SLOT + HALO * (2 if bit == 0 else 1)


def right_moves(device, bit):
    if bit == 2:
        return device % 4 == 3
    return device % (1 << bit) == 0


def pack_hop(count, bit, held_ref, left, right, out_ref):
    device = lax.axis_index("node")
    chosen = [r for r in range(count) if r >> bit & 1]
    for at, r in enumerate(chosen):
        out_ref[at * SLOT : (at + 1) * SLOT, :] = held_ref[r]
    size = len(chosen) * SLOT
    if bit == 0:
        out_ref[size : size + HALO, :] = left
        out_ref[size + HALO :, :] = right
    else:
        out_ref[size:, :] = jnp.where(right_moves(device, bit), right, left)


def unpack_hop(count, bit, got_ref, held_ref, left, right):
    device = lax.axis_index("node")
    chosen = [r for r in range(count) if r >> bit & 1]
    for at, r in enumerate(chosen):
        held_ref[r] = got_ref[at * SLOT : (at + 1) * SLOT, :]
    size = len(chosen) * SLOT
    if bit == 0:
        return got_ref[size : size + HALO, :], got_ref[size + HALO :, :]
    got = got_ref[size:, :]
    if bit == 2:
        moves = device % 4 == 0
    else:
        moves = device % (1 << bit) == (1 << bit) - 1
    return jnp.where(moves, got, left), jnp.where(right_moves(device, bit), got, right)


def back_kernel(
    count, bit, mat_ref, d_pre_ref, w_one_ref, own_ref, held_ref, left_ref, right_ref, out_ref
):
    device = lax.axis_index("node")
    far = count * SLOT
    q = (nt(d_pre_ref[...], w_one_ref[...]) / row_total(mat_ref, far)).astype(BF16)
    rims = tn(mat_ref[:, HALO_COL:FAR_COL], q).astype(BF16)
    left_ref[...] = rims[0:HALO]
    right_ref[...] = rims[HALO : 2 * HALO]
    terms = tn(mat_ref[:, FAR_COL : FAR_COL + far], q).astype(BF16).reshape(count, SLOT, D)
    for peer in range(count):
        held_ref[device ^ peer] = terms[peer]
    pack_hop(count, bit, held_ref, rims[0:HALO], rims[HALO : 2 * HALO], out_ref)
    own_ref[...] = tn(mat_ref[:, 0:ROWS], q)


def hop_kernel(
    count, last, bit, got_ref, was_ref, was_left_ref, was_right_ref,
    held_ref, left_ref, right_ref, out_ref,
):
    held_ref[...] = was_ref[...]
    left, right = unpack_hop(
        count, last, got_ref, held_ref, was_left_ref[...], was_right_ref[...]
    )
    left_ref[...] = left
    right_ref[...] = right
    pack_hop(count, bit, held_ref, left, right, out_ref)


def features_kernel(
    count, last, mat_ref, own_ref, got_ref, was_ref, was_left_ref, was_right_ref,
    out_ref, sum_scr, held_scr, block_scr,
):
    device = lax.axis_index("node")
    far = count * SLOT
    held_scr[...] = was_ref[...]
    left, right = unpack_hop(
        count, last, got_ref, held_scr, was_left_ref[...], was_right_ref[...]
    )
    for r in range(count):
        block_scr[device ^ r] = held_scr[r]
    sum_scr[...] = own_ref[...] + nn(mat_ref[:, FAR_COL + far :], block_scr[...].reshape(far, D))
    sum_scr[0:HALO, :] += right.astype(F32)
    sum_scr[ROWS - HALO : ROWS, :] += left.astype(F32)
    out_ref[...] = sum_scr[...].astype(BF16)


def sum_refs(refs, rows=slice(None)):
    total = refs[0][rows, :].astype(F32)
    for ref in refs[1:]:
        total = total + ref[rows, :].astype(F32)
    return total


def plane_sum_kernel(*refs):
    part_refs, (keep_ref, give_ref) = refs[:PLANE], refs[PLANE:]
    wide = D // PLANE
    keep_ref[...] = sum_refs(part_refs, slice(0, wide))
    give_ref[...] = sum_refs(part_refs, slice(wide, 2 * wide)).astype(BF16)


def pair_sum_kernel(scale, one_ref, two_ref, out_ref):
    total = one_ref[...].astype(F32) + two_ref[...].astype(F32)
    out_ref[...] = (total * scale).astype(BF16)


def gather_kernel(*refs):
    chunk_refs, out_refs = refs[:PLANE], refs[PLANE:]
    wide = D // PLANE
    device = lax.axis_index("node")
    place, side = device % PLANE, device // PLANE % 2
    for v, ref in enumerate(chunk_refs):
        row = pl.ds(pl.multiple_of((place ^ v) * wide, wide), wide)
        for half, out_ref in enumerate(out_refs):
            at = pl.ds(pl.multiple_of((side ^ half) * wide, wide), wide)
            out_ref[row, :] = ref[at, :]


def shards(
    features, upstream, weight_one, weight_two, neighbours, edge_weight, fetch_block, fetch_count
):
    count = lax.axis_size("node")
    far = count * SLOT
    chain = FAR_COL + far
    wide = D // PLANE
    onward = [(i, i + 1) for i in range(1, count - 1, 2)]
    onward = onward + [(target, source) for source, target in onward]

    def swap(value, flip):
        return lax.ppermute(value, "node", [(i, i ^ flip) for i in range(count)])

    matrix, own, send, near, onto = call(
        functools.partial(prepare_kernel, count),
        (
            struct((ROWS, chain + far), BF16),
            struct((ROWS, D), F32),
            struct((count, 2 * SLOT, D), BF16),
            struct((2 * HALO, D), BF16),
            struct((2 * HALO, D), BF16),
        ),
        (
            pltpu.VMEM((K, ROWS), jnp.int32),
            pltpu.VMEM((K, ROWS), jnp.int32),
            pltpu.VMEM((CAP, count * count), jnp.int32),
            pltpu.VMEM((1, count * count), jnp.int32),
            pltpu.VMEM((ROWS, D), BF16),
            pltpu.VMEM((ROWS, D), BF16),
            pltpu.SemaphoreType.DMA((6,)),
            pltpu.VMEM((8, count * count), F32),
            pltpu.VMEM((chain, ROWS), F32),
        ),
        in_specs=[pl.BlockSpec(memory_space=pltpu.HBM)] * 6,
    )(
        *(
            pltpu.with_memory_space_constraint(value, pltpu.HBM)
            for value in (
                neighbours.T, edge_weight.T, fetch_block.T, fetch_count.reshape(1, -1),
                features, upstream,
            )
        )
    )
    near = swap(near, 1)
    onto = lax.ppermute(onto, "node", onward)
    received = lax.all_to_all(send, "node", split_axis=0, concat_axis=0, tiled=True)

    *parts, d_pre = call(
        functools.partial(layer_kernel, count),
        (
            struct((2 * D // PLANE, D), F32),
            *[struct((2 * D // PLANE, D), BF16)] * (PLANE - 1),
            struct((ROWS, D), BF16),
        ),
        (
            pltpu.VMEM((ROWS, D), BF16),
            pltpu.VMEM((ROWS, D), F32),
            pltpu.VMEM((ROWS, D), BF16),
            pltpu.VMEM((ROWS, D), BF16),
        ),
    )(matrix, features, own, received, near, onto, weight_one, weight_two)
    parts = [parts[0]] + [swap(parts[v], v) for v in range(1, PLANE)]

    bits = hop_bits(count)
    carried = (
        struct((count, SLOT, D), BF16),
        struct((HALO, D), BF16),
        struct((HALO, D), BF16),
    )

    def message(bit):
        return struct((hop_rows(count, bit), D), BF16)

    def next_hop(at, got, held):
        *held, out = call(
            functools.partial(hop_kernel, count, bits[at - 1], bits[at]),
            (*carried, message(bits[at])),
        )(got, *held)
        return out, held

    own, *held, out = call(
        functools.partial(back_kernel, count, bits[0]),
        (struct((ROWS, D), F32), *carried, message(bits[0])),
    )(matrix, d_pre, weight_one)
    parts, got = lax.optimization_barrier((parts, swap(out, 1 << bits[0])))

    keep, give = call(plane_sum_kernel, (struct((wide, D), F32), struct((wide, D), BF16)))(*parts)
    out, held = next_hop(1, got, held)
    give, out = lax.optimization_barrier((give, out))
    other, got = lax.optimization_barrier((swap(give, PLANE), swap(out, 1 << bits[1])))

    pair = functools.partial(pair_sum_kernel, 1.0)
    total = call(pair, struct((wide, D), BF16))(keep, other)
    out, held = next_hop(2, got, held)
    for bit in bits[3:-1]:
        total = call(pair, struct((wide, D), BF16))(total, swap(total, 1 << bit))
    total, out = lax.optimization_barrier((total, out))
    other, got = lax.optimization_barrier((swap(total, 1 << bits[-1]), swap(out, 1 << bits[2])))

    total = call(
        functools.partial(pair_sum_kernel, 1.0 / math.sqrt(ROWS * count)),
        struct((wide, D), BF16),
    )(total, other)
    out, held = next_hop(3, got, held)
    total, out = lax.optimization_barrier((total, out))
    other, got = lax.optimization_barrier((swap(total, PLANE), swap(out, 1 << bits[3])))

    chunk = jnp.concatenate([total, other], axis=0)
    chunks = [chunk] + [swap(chunk, v) for v in range(1, PLANE)]
    for at in range(4, len(bits)):
        out, held = next_hop(at, got, held)
        got = swap(out, 1 << bits[at])
    d_features = call(
        functools.partial(features_kernel, count, bits[-1]),
        struct((ROWS, D), BF16),
        (
            pltpu.VMEM((ROWS, D), F32),
            pltpu.VMEM((count, SLOT, D), BF16),
            pltpu.VMEM((count, SLOT, D), BF16),
        ),
    )(matrix, own, got, *held)
    grad_two, grad_one = call(gather_kernel, (struct((D, D), BF16), struct((D, D), BF16)))(*chunks)
    return d_features, grad_one, grad_two


def solution(mesh):
    placed = (
        P(("rep", "node"), None),
        P(("rep", "node"), None),
        P(),
        P(),
        P(("rep", "node"), None),
        P(("rep", "node"), None),
        P("rep", None),
        P("rep"),
    )
    return jax.shard_map(
        shards,
        mesh=mesh,
        in_specs=placed,
        out_specs=(P(("rep", "node"), None), P("rep", None), P("rep", None)),
        check_vma=False,
    )
```

```python
import functools
import math

import jax
import jax.numpy as jnp
from jax import lax
from jax.experimental import pallas as pl
from jax.experimental.pallas import tpu as pltpu
from jax.sharding import PartitionSpec as P

D = 512
K = 32
ROWS = 128
HALO = 32
BLK = 8
CAP = 2
SELF_WEIGHT = 8.0
SLOT = CAP * BLK
HALO_COL = ROWS
FAR_COL = 2 * ROWS
PLANE = 4

F32 = jnp.float32
BF16 = jnp.bfloat16
VMEM_LIMIT = 48 * 1024 * 1024


def nn(left, right):
    return jnp.dot(left, right, preferred_element_type=F32)


def nt(left, right):
    return lax.dot_general(left, right, (((1,), (1,)), ((), ())), preferred_element_type=F32)


def tn(left, right):
    return lax.dot_general(left, right, (((0,), (0,)), ((), ())), preferred_element_type=F32)


def iota(shape, dim):
    return lax.broadcasted_iota(jnp.int32, shape, dim)


def call(kernel, out_shape, scratch=(), **specs):
    return pl.pallas_call(
        kernel,
        out_shape=out_shape,
        **specs,
        scratch_shapes=list(scratch),
        compiler_params=pltpu.CompilerParams(vmem_limit_bytes=VMEM_LIMIT),
    )


def struct(shape, dtype):
    return jax.ShapeDtypeStruct(shape, dtype)


def prepare_kernel(
    count, nbr_hbm, wgt_hbm, tab_hbm, cnt_hbm, feat_hbm, up_hbm,
    mat_ref, own_ref, send_ref, near_ref, next_ref,
    nbr_ref, wgt_ref, tab_ref, cnt_ref, feat_ref, up_ref, sems, rows_scr, at_scr,
):
    inputs = (
        (tab_hbm, tab_ref), (cnt_hbm, cnt_ref), (nbr_hbm, nbr_ref),
        (wgt_hbm, wgt_ref), (up_hbm, up_ref), (feat_hbm, feat_ref),
    )
    copies = [
        pltpu.make_async_copy(src, dst, sems.at[i]) for i, (src, dst) in enumerate(inputs)
    ]
    for copy in copies:
        copy.start()
    copies[0].wait()
    copies[1].wait()
    device = lax.axis_index("node")
    first = device * ROWS
    far = count * SLOT
    pairs = count * count
    rows_scr[...] = jnp.zeros_like(rows_scr)
    rows_scr[0:CAP, :] = tab_ref[...].astype(F32)
    rows_scr[CAP : CAP + 1, :] = cnt_ref[...].astype(F32)
    step = min(pairs, 256)
    listed = jnp.zeros((far, 8), F32)
    asked = jnp.zeros((far, 8), F32)
    peer_wide = iota((far, step), 0) // SLOT
    for at in range(0, pairs, step):
        pair = iota((far, step), 1) + at
        rows = rows_scr[:, at : at + step].astype(BF16)
        mine = jnp.where(pair == device * count + peer_wide, 1.0, 0.0).astype(BF16)
        theirs = jnp.where(pair == peer_wide * count + device, 1.0, 0.0).astype(BF16)
        listed = listed + nt(mine, rows)
        asked = asked + nt(theirs, rows)
    listed = listed.astype(jnp.int32)
    asked = asked.astype(jnp.int32)
    col = iota((far, 1), 0)
    slot = col // BLK % CAP
    inner = col % BLK
    block = jnp.where(slot == 0, listed[:, 0:1], listed[:, 1:2])
    node = col // SLOT * ROWS + block * BLK + inner
    in_band = (node >= first - HALO) & (node < first + ROWS + HALO)
    far_node = jnp.where((slot < listed[:, 2:3]) & jnp.logical_not(in_band), node, -1)
    asked_row = jnp.where(slot == 0, asked[:, 0:1], asked[:, 1:2]) * BLK + inner

    copies[2].wait()
    copies[3].wait()
    weight = wgt_ref[...].astype(F32)
    neighbour = nbr_ref[...]

    def counted(nodes, total):
        for k in range(K):
            total = total + jnp.where(neighbour[k : k + 1, :] == nodes, weight[k : k + 1, :], 0.0)
        return total

    square = (ROWS, ROWS)
    row = iota(square, 0)
    at_scr[0:ROWS, :] = counted(first + row, jnp.where(row == iota(square, 1), SELF_WEIGHT, 0.0))
    rim = iota((2 * HALO, ROWS), 0)
    rim_node = first + jnp.where(rim < HALO, rim - HALO, rim - HALO + ROWS)
    at_scr[HALO_COL : HALO_COL + 2 * HALO, :] = counted(rim_node, jnp.zeros((2 * HALO, ROWS), F32))
    at_scr[HALO_COL + 2 * HALO : FAR_COL, :] = jnp.zeros((FAR_COL - HALO_COL - 2 * HALO, ROWS), F32)
    for at in range(0, far, ROWS):
        nodes = jnp.broadcast_to(far_node[at : at + ROWS], square)
        at_scr[FAR_COL + at : FAR_COL + at + ROWS, :] = counted(nodes, jnp.zeros(square, F32))

    adj_mat = at_scr[...]
    matrix = adj_mat.T
    adj_mat = adj_mat.astype(BF16)
    total = jnp.sum(matrix, axis=1, keepdims=True)
    mat_ref[:, 0 : FAR_COL + far] = matrix.astype(BF16)
    pick = jnp.where(asked_row == iota((far, ROWS), 1), 1.0, 0.0)
    mat_ref[:, FAR_COL + far :] = pick.T.astype(BF16)

    copies[4].wait()
    scaled = (up_ref[...].astype(F32) / total).astype(BF16)
    copies[5].wait()
    features = feat_ref[...]
    own_ref[...] = nn(adj_mat[0:ROWS], scaled)
    rims = nn(adj_mat[HALO_COL : HALO_COL + 2 * HALO], scaled).astype(BF16)
    even = device % 2 == 0
    low, high = features[0:HALO], features[ROWS - HALO : ROWS]
    near_ref[0:HALO, :] = jnp.where(even, high, low)
    near_ref[HALO:, :] = jnp.where(even, rims[HALO:], rims[0:HALO])
    next_ref[0:HALO, :] = jnp.where(even, low, high)
    next_ref[HALO:, :] = jnp.where(even, rims[0:HALO], rims[HALO:])
    rows_out = nn(pick.astype(BF16), features).astype(BF16)
    send_ref[:, 0:SLOT, :] = rows_out.reshape(count, SLOT, D)
    terms = nn(adj_mat[FAR_COL:], scaled).astype(BF16)
    send_ref[:, SLOT : 2 * SLOT, :] = terms.reshape(count, SLOT, D)


def row_total(mat_ref, far):
    return jnp.sum(mat_ref[:, 0 : FAR_COL + far].astype(F32), axis=1, keepdims=True)


def layer_kernel(
    count, mat_ref, feat_ref, own_ref, recv_ref, near_ref, next_ref, w_one_ref, w_two_ref,
    *refs,
):
    part_refs = refs[:PLANE]
    d_pre_ref, rim_scr, u_scr, hidden_scr, agg_scr = refs[PLANE:]
    device = lax.axis_index("node")
    place, side = device % PLANE, device // PLANE % 2
    even = device % 2 == 0
    left = jnp.where(even, next_ref[...], near_ref[...])
    right = jnp.where(even, near_ref[...], next_ref[...])
    far = count * SLOT
    total = row_total(mat_ref, far)
    rim_scr[0:HALO, :] = left[0:HALO]
    rim_scr[HALO : 2 * HALO, :] = right[0:HALO]
    rim_scr[2 * HALO :, :] = jnp.zeros((ROWS - 2 * HALO, D), BF16)
    sums = nn(mat_ref[:, 0:ROWS], feat_ref[...])
    sums = sums + nn(mat_ref[:, HALO_COL:FAR_COL], rim_scr[...])
    sums = sums + nn(
        mat_ref[:, FAR_COL : FAR_COL + far], recv_ref[:, 0:SLOT, :].reshape(far, D)
    )
    agg = (sums / total).astype(BF16)
    agg_scr[...] = agg
    u_scr[...] = own_ref[...] + nn(
        mat_ref[:, FAR_COL + far :], recv_ref[:, SLOT : 2 * SLOT, :].reshape(far, D)
    )
    u_scr[0:HALO, :] += left[HALO:].astype(F32)
    u_scr[ROWS - HALO : ROWS, :] += right[HALO:].astype(F32)
    u = u_scr[...].astype(BF16)
    back = nt(u, w_two_ref[...])
    pre = nn(agg, w_one_ref[...])
    square = pre * pre
    bend = jnp.tanh(0.7978845608 * pre * (1.0 + 0.044715 * square))
    hidden_scr[...] = (0.5 * pre * (1.0 + bend)).astype(BF16)
    slope = 0.5 * (1.0 + bend) + 0.5 * pre * (1.0 - bend * bend) * (
        0.7978845608 * (1.0 + 3.0 * 0.044715 * square)
    )
    d_pre = (back * slope).astype(BF16)
    d_pre_ref[...] = d_pre
    wide = D // PLANE
    for v in range(PLANE):
        cols = pl.ds(pl.multiple_of((place ^ v) * wide, wide), wide)
        for half, (first, second) in enumerate(((hidden_scr, u), (agg_scr, d_pre))):
            rows = pl.ds(pl.multiple_of((side ^ half) * wide, wide), wide)
            part_refs[v][rows, :] = tn(first[:, cols], second).astype(part_refs[v].dtype)


def hop_bits(count):
    return list(range(count.bit_length() - 2, 2, -1)) + [0, 1, 2]


def hop_rows(count, bit):
    return count // 2 * SLOT + HALO * (2 if bit == 0 else 1)


def moves(device, bit):
    low = device % (1 << bit)
    ones = (1 << bit) - 1
    return (low == 0, low == ones) if bit > 2 else (low == ones, low == 0)


def pack_hop(count, bit, held_ref, left, right, out_ref):
    device = lax.axis_index("node")
    chosen = [r for r in range(count) if r >> bit & 1]
    for at, r in enumerate(chosen):
        out_ref[at * SLOT : (at + 1) * SLOT, :] = held_ref[r]
    size = len(chosen) * SLOT
    if bit == 0:
        out_ref[size : size + HALO, :] = left
        out_ref[size + HALO :, :] = right
    else:
        out_ref[size:, :] = jnp.where(moves(device, bit)[1], right, left)


def unpack_hop(count, bit, got_ref, held_ref, left, right):
    device = lax.axis_index("node")
    chosen = [r for r in range(count) if r >> bit & 1]
    for at, r in enumerate(chosen):
        held_ref[r] = got_ref[at * SLOT : (at + 1) * SLOT, :]
    size = len(chosen) * SLOT
    if bit == 0:
        return got_ref[size : size + HALO, :], got_ref[size + HALO :, :]
    got = got_ref[size:, :]
    left_moves, right_moves = moves(device, bit)
    return jnp.where(left_moves, got, left), jnp.where(right_moves, got, right)


def back_kernel(
    count, bit, mat_ref, d_pre_ref, w_one_ref, own_ref, held_ref, left_ref, right_ref, out_ref
):
    device = lax.axis_index("node")
    far = count * SLOT
    q = (nt(d_pre_ref[...], w_one_ref[...]) / row_total(mat_ref, far)).astype(BF16)
    rims = tn(mat_ref[:, HALO_COL:FAR_COL], q).astype(BF16)
    left_ref[...] = rims[0:HALO]
    right_ref[...] = rims[HALO : 2 * HALO]
    terms = tn(mat_ref[:, FAR_COL : FAR_COL + far], q).astype(BF16).reshape(count, SLOT, D)
    for peer in range(count):
        held_ref[device ^ peer] = terms[peer]
    pack_hop(count, bit, held_ref, rims[0:HALO], rims[HALO : 2 * HALO], out_ref)
    own_ref[...] = tn(mat_ref[:, 0:ROWS], q)


def hop_kernel(
    count, last, bit, got_ref, was_ref, was_left_ref, was_right_ref,
    held_ref, left_ref, right_ref, out_ref,
):
    held_ref[...] = was_ref[...]
    left, right = unpack_hop(
        count, last, got_ref, held_ref, was_left_ref[...], was_right_ref[...]
    )
    left_ref[...] = left
    right_ref[...] = right
    pack_hop(count, bit, held_ref, left, right, out_ref)


def features_kernel(
    count, last, mat_ref, own_ref, got_ref, was_ref, was_left_ref, was_right_ref,
    out_ref, sum_scr, held_scr, block_scr,
):
    device = lax.axis_index("node")
    far = count * SLOT
    held_scr[...] = was_ref[...]
    left, right = unpack_hop(
        count, last, got_ref, held_scr, was_left_ref[...], was_right_ref[...]
    )
    for r in range(count):
        block_scr[device ^ r] = held_scr[r]
    sum_scr[...] = own_ref[...] + nn(mat_ref[:, FAR_COL + far :], block_scr[...].reshape(far, D))
    sum_scr[0:HALO, :] += right.astype(F32)
    sum_scr[ROWS - HALO : ROWS, :] += left.astype(F32)
    out_ref[...] = sum_scr[...].astype(BF16)


def sum_refs(refs, rows=slice(None)):
    total = refs[0][rows, :].astype(F32)
    for ref in refs[1:]:
        total = total + ref[rows, :].astype(F32)
    return total


def plane_sum_kernel(*refs):
    part_refs, (keep_ref, give_ref) = refs[:PLANE], refs[PLANE:]
    wide = D // PLANE
    keep_ref[...] = sum_refs(part_refs, slice(0, wide))
    give_ref[...] = sum_refs(part_refs, slice(wide, 2 * wide)).astype(BF16)


def pair_sum_kernel(scale, one_ref, two_ref, out_ref):
    total = one_ref[...].astype(F32) + two_ref[...].astype(F32)
    out_ref[...] = (total * scale).astype(BF16)


def gather_kernel(*refs):
    chunk_refs, out_refs = refs[:PLANE], refs[PLANE:]
    wide = D // PLANE
    device = lax.axis_index("node")
    place, side = device % PLANE, device // PLANE % 2
    for v, ref in enumerate(chunk_refs):
        row = pl.ds(pl.multiple_of((place ^ v) * wide, wide), wide)
        for half, out_ref in enumerate(out_refs):
            at = pl.ds(pl.multiple_of((side ^ half) * wide, wide), wide)
            out_ref[row, :] = ref[at, :]


def shards(
    features, upstream, weight_one, weight_two, neighbours, edge_weight, fetch_block, fetch_count
):
    count = lax.axis_size("node")
    far = count * SLOT
    chain = FAR_COL + far
    wide = D // PLANE
    onward = [(i, i + 1) for i in range(1, count - 1, 2)]
    onward = onward + [(target, source) for source, target in onward]

    def swap(value, flip):
        return lax.ppermute(value, "node", [(i, i ^ flip) for i in range(count)])

    matrix, own, send, near, onto = call(
        functools.partial(prepare_kernel, count),
        (
            struct((ROWS, chain + far), BF16),
            struct((ROWS, D), F32),
            struct((count, 2 * SLOT, D), BF16),
            struct((2 * HALO, D), BF16),
            struct((2 * HALO, D), BF16),
        ),
        (
            pltpu.VMEM((K, ROWS), jnp.int32),
            pltpu.VMEM((K, ROWS), jnp.int32),
            pltpu.VMEM((CAP, count * count), jnp.int32),
            pltpu.VMEM((1, count * count), jnp.int32),
            pltpu.VMEM((ROWS, D), BF16),
            pltpu.VMEM((ROWS, D), BF16),
            pltpu.SemaphoreType.DMA((6,)),
            pltpu.VMEM((8, count * count), F32),
            pltpu.VMEM((chain, ROWS), F32),
        ),
        in_specs=[pl.BlockSpec(memory_space=pltpu.HBM)] * 6,
    )(
        *(
            pltpu.with_memory_space_constraint(value, pltpu.HBM)
            for value in (
                neighbours.T, edge_weight.T, fetch_block.T, fetch_count.reshape(1, -1),
                features, upstream,
            )
        )
    )
    near = swap(near, 1)
    onto = lax.ppermute(onto, "node", onward)
    received = lax.all_to_all(send, "node", split_axis=0, concat_axis=0, tiled=True)

    *parts, d_pre = call(
        functools.partial(layer_kernel, count),
        (
            struct((2 * D // PLANE, D), F32),
            *[struct((2 * D // PLANE, D), BF16)] * (PLANE - 1),
            struct((ROWS, D), BF16),
        ),
        (
            pltpu.VMEM((ROWS, D), BF16),
            pltpu.VMEM((ROWS, D), F32),
            pltpu.VMEM((ROWS, D), BF16),
            pltpu.VMEM((ROWS, D), BF16),
        ),
    )(matrix, features, own, received, near, onto, weight_one, weight_two)
    parts = [parts[0]] + [swap(parts[v], v) for v in range(1, PLANE)]

    bits = hop_bits(count)
    carried = (
        struct((count, SLOT, D), BF16),
        struct((HALO, D), BF16),
        struct((HALO, D), BF16),
    )

    def message(bit):
        return struct((hop_rows(count, bit), D), BF16)

    def next_hop(at, got, held):
        *held, out = call(
            functools.partial(hop_kernel, count, bits[at - 1], bits[at]),
            (*carried, message(bits[at])),
        )(got, *held)
        return out, held

    own, *held, out = call(
        functools.partial(back_kernel, count, bits[0]),
        (struct((ROWS, D), F32), *carried, message(bits[0])),
    )(matrix, d_pre, weight_one)
    got = swap(out, 1 << bits[0])
    for at in range(1, len(bits) - 3):
        out, held = next_hop(at, got, held)
        got = swap(out, 1 << bits[at])
    parts, got = lax.optimization_barrier((parts, got))

    keep, give = call(plane_sum_kernel, (struct((wide, D), F32), struct((wide, D), BF16)))(*parts)
    out, held = next_hop(len(bits) - 3, got, held)
    other, got = lax.optimization_barrier((swap(give, PLANE), swap(out, 1)))

    pair = functools.partial(pair_sum_kernel, 1.0)
    total = call(pair, struct((wide, D), BF16))(keep, other)
    out, held = next_hop(len(bits) - 2, got, held)
    for bit in range(3, len(bits) - 1):
        total = call(pair, struct((wide, D), BF16))(total, swap(total, 1 << bit))
    other, got = lax.optimization_barrier((swap(total, count // 2), swap(out, 2)))

    total = call(
        functools.partial(pair_sum_kernel, 1.0 / math.sqrt(ROWS * count)),
        struct((wide, D), BF16),
    )(total, other)
    other = swap(total, PLANE)

    chunk = jnp.concatenate([total, other], axis=0)
    chunks = [chunk] + [swap(chunk, v) for v in range(1, PLANE)]
    out, held = next_hop(len(bits) - 1, got, held)
    got = swap(out, PLANE)
    d_features = call(
        functools.partial(features_kernel, count, bits[-1]),
        struct((ROWS, D), BF16),
        (
            pltpu.VMEM((ROWS, D), F32),
            pltpu.VMEM((count, SLOT, D), BF16),
            pltpu.VMEM((count, SLOT, D), BF16),
        ),
    )(matrix, own, got, *held)
    grad_two, grad_one = call(gather_kernel, (struct((D, D), BF16), struct((D, D), BF16)))(*chunks)
    return d_features, grad_one, grad_two


def solution(mesh):
    placed = (
        P(("rep", "node"), None),
        P(("rep", "node"), None),
        P(),
        P(),
        P(("rep", "node"), None),
        P(("rep", "node"), None),
        P("rep", None),
        P("rep"),
    )
    return jax.shard_map(
        shards,
        mesh=mesh,
        in_specs=placed,
        out_specs=(P(("rep", "node"), None), P("rep", None), P("rep", None)),
        check_vma=False,
    )
```

```python
import functools
import math

import jax
import jax.numpy as jnp
from jax import lax
from jax.experimental import pallas as pl
from jax.experimental.pallas import tpu as pltpu
from jax.sharding import PartitionSpec as P

D = 512
K = 32
ROWS = 128
HALO = 32
BLK = 8
CAP = 2
SELF_WEIGHT = 8.0
SLOT = CAP * BLK
HALO_COL = ROWS
FAR_COL = 2 * ROWS
PLANE = 4
WIDE = D // PLANE

F32 = jnp.float32
BF16 = jnp.bfloat16
VMEM_LIMIT = 48 * 1024 * 1024


def nn(left, right):
    return jnp.dot(left, right, preferred_element_type=F32)


def nt(left, right):
    return lax.dot_general(left, right, (((1,), (1,)), ((), ())), preferred_element_type=F32)


def tn(left, right):
    return lax.dot_general(left, right, (((0,), (0,)), ((), ())), preferred_element_type=F32)


def iota(shape, dim):
    return lax.broadcasted_iota(jnp.int32, shape, dim)


def call(kernel, out_shape, scratch=(), **specs):
    return pl.pallas_call(
        kernel,
        out_shape=out_shape,
        **specs,
        scratch_shapes=list(scratch),
        compiler_params=pltpu.CompilerParams(vmem_limit_bytes=VMEM_LIMIT),
    )


def struct(shape, dtype):
    return jax.ShapeDtypeStruct(shape, dtype)


def prepare_kernel(
    count, nbr_hbm, wgt_hbm, tab_hbm, cnt_hbm, feat_hbm, up_hbm,
    mat_ref, pick_ref, total_ref, own_ref, send_hbm, near_ref, next_ref,
    nbr_ref, wgt_ref, tab_ref, cnt_ref, feat_ref, up_ref, sems, rows_scr, at_scr,
    rows_out, terms_out, out_sems,
):
    inputs = (
        (tab_hbm, tab_ref), (cnt_hbm, cnt_ref), (feat_hbm, feat_ref),
        (nbr_hbm, nbr_ref), (wgt_hbm, wgt_ref), (up_hbm, up_ref),
    )
    copies = [
        pltpu.make_async_copy(src, dst, sems.at[i]) for i, (src, dst) in enumerate(inputs)
    ]
    for copy in copies:
        copy.start()
    copies[0].wait()
    copies[1].wait()
    device = lax.axis_index("node")
    first = device * ROWS
    far = count * SLOT
    pairs = count * count
    rows_scr[...] = jnp.zeros_like(rows_scr)
    rows_scr[0:CAP, :] = tab_ref[...].astype(F32)
    rows_scr[CAP : CAP + 1, :] = cnt_ref[...].astype(F32)
    step = min(pairs, 256)
    listed = jnp.zeros((far, 8), F32)
    asked = jnp.zeros((far, 8), F32)
    asked_wide = jnp.zeros((8, far), F32)
    peer_wide = iota((far, step), 0) // SLOT
    for at in range(0, pairs, step):
        pair = iota((far, step), 1) + at
        rows = rows_scr[:, at : at + step].astype(BF16)
        mine = jnp.where(pair == device * count + peer_wide, 1.0, 0.0).astype(BF16)
        theirs = jnp.where(pair == peer_wide * count + device, 1.0, 0.0).astype(BF16)
        listed = listed + nt(mine, rows)
        asked = asked + nt(theirs, rows)
        asked_wide = asked_wide + nt(rows, theirs)
    listed = listed.astype(jnp.int32)
    asked = asked.astype(jnp.int32)
    col = iota((far, 1), 0)
    slot = col // BLK % CAP
    inner = col % BLK
    block = jnp.where(slot == 0, listed[:, 0:1], listed[:, 1:2])
    node = col // SLOT * ROWS + block * BLK + inner
    in_band = (node >= first - HALO) & (node < first + ROWS + HALO)
    far_node = jnp.where((slot < listed[:, 2:3]) & jnp.logical_not(in_band), node, -1)
    asked_row = jnp.where(slot == 0, asked[:, 0:1], asked[:, 1:2]) * BLK + inner
    pick = jnp.where(asked_row == iota((far, ROWS), 1), 1.0, 0.0).astype(BF16)
    wide_col = iota((1, far), 1)
    asked_wide = asked_wide.astype(jnp.int32)
    wide_row = jnp.where(wide_col // BLK % CAP == 0, asked_wide[0:1], asked_wide[1:2]) * BLK
    wide_row = wide_row + wide_col % BLK
    pick_ref[...] = jnp.where(wide_row == iota((ROWS, far), 0), 1.0, 0.0).astype(BF16)
    copies[2].wait()
    features = feat_ref[...]
    rows_out[...] = nn(pick, features).astype(BF16).reshape(count, SLOT, D)
    rows_copy = pltpu.make_async_copy(rows_out, send_hbm.at[:, 0:SLOT, :], out_sems.at[0])
    rows_copy.start()

    copies[3].wait()
    copies[4].wait()
    weight = wgt_ref[...].astype(F32)
    neighbour = nbr_ref[...]

    def counted(nodes, total):
        for k in range(K):
            total = total + jnp.where(neighbour[k : k + 1, :] == nodes, weight[k : k + 1, :], 0.0)
        return total

    square = (ROWS, ROWS)
    row = iota(square, 0)
    at_scr[0:ROWS, :] = counted(first + row, jnp.where(row == iota(square, 1), SELF_WEIGHT, 0.0))
    rim = iota((2 * HALO, ROWS), 0)
    rim_node = first + jnp.where(rim < HALO, rim - HALO, rim - HALO + ROWS)
    at_scr[HALO_COL : HALO_COL + 2 * HALO, :] = counted(rim_node, jnp.zeros((2 * HALO, ROWS), F32))
    at_scr[HALO_COL + 2 * HALO : FAR_COL, :] = jnp.zeros((FAR_COL - HALO_COL - 2 * HALO, ROWS), F32)
    for at in range(0, far, ROWS):
        nodes = jnp.broadcast_to(far_node[at : at + ROWS], square)
        at_scr[FAR_COL + at : FAR_COL + at + ROWS, :] = counted(nodes, jnp.zeros(square, F32))

    adj_mat = at_scr[...]
    total = jnp.broadcast_to(jnp.sum(adj_mat, axis=0, keepdims=True), square).T
    total_ref[...] = total
    adj_mat = adj_mat.astype(BF16)
    mat_ref[...] = adj_mat
    copies[5].wait()
    scaled = (up_ref[...].astype(F32) / total[:, 0:1]).astype(BF16)
    terms_out[...] = nn(adj_mat[FAR_COL:], scaled).astype(BF16).reshape(count, SLOT, D)
    terms_copy = pltpu.make_async_copy(
        terms_out, send_hbm.at[:, SLOT : 2 * SLOT, :], out_sems.at[1]
    )
    terms_copy.start()
    own_ref[...] = nn(adj_mat[0:ROWS], scaled)
    rims = nn(adj_mat[HALO_COL : HALO_COL + 2 * HALO], scaled).astype(BF16)
    even = device % 2 == 0
    low, high = features[0:HALO], features[ROWS - HALO : ROWS]
    near_ref[0:HALO, :] = jnp.where(even, high, low)
    near_ref[HALO:, :] = jnp.where(even, rims[HALO:], rims[0:HALO])
    next_ref[0:HALO, :] = jnp.where(even, low, high)
    next_ref[HALO:, :] = jnp.where(even, rims[0:HALO], rims[HALO:])
    rows_copy.wait()
    terms_copy.wait()


def layer_kernel(
    count, mat_ref, pick_ref, total_ref, feat_ref, own_ref, recv_ref, near_ref, next_ref,
    w_one_ref, w_two_ref,
    *refs,
):
    part_refs = refs[:PLANE], refs[PLANE : 2 * PLANE]
    d_pre_ref, rim_scr, u_scr, first_scr, second_scr = refs[2 * PLANE :]
    device = lax.axis_index("node")
    place, side = device % PLANE, device // PLANE % 2
    even = device % 2 == 0
    left = jnp.where(even, next_ref[...], near_ref[...])
    right = jnp.where(even, near_ref[...], next_ref[...])
    far = count * SLOT
    rim_scr[0:HALO, :] = left[0:HALO]
    rim_scr[HALO : 2 * HALO, :] = right[0:HALO]
    rim_scr[2 * HALO :, :] = jnp.zeros((ROWS - 2 * HALO, D), BF16)
    sums = tn(mat_ref[0:ROWS, :], feat_ref[...])
    sums = sums + tn(mat_ref[HALO_COL:FAR_COL, :], rim_scr[...])
    sums = sums + tn(mat_ref[FAR_COL:, :], recv_ref[:, 0:SLOT, :].reshape(far, D))
    agg = (sums / total_ref[:, 0:1]).astype(BF16)
    first_scr[1] = agg
    u_scr[...] = own_ref[...] + nn(
        pick_ref[...], recv_ref[:, SLOT : 2 * SLOT, :].reshape(far, D)
    )
    u_scr[0:HALO, :] += left[HALO:].astype(F32)
    u_scr[ROWS - HALO : ROWS, :] += right[HALO:].astype(F32)
    u = u_scr[...].astype(BF16)
    second_scr[0] = u
    back = nt(u, w_two_ref[...])
    pre = nn(agg, w_one_ref[...])
    square = pre * pre
    bend = jnp.tanh(0.7978845608 * pre * (1.0 + 0.044715 * square))
    first_scr[0] = (0.5 * pre * (1.0 + bend)).astype(BF16)
    slope = 0.5 * (1.0 + bend) + 0.5 * pre * (1.0 - bend * bend) * (
        0.7978845608 * (1.0 + 3.0 * 0.044715 * square)
    )
    d_pre = (back * slope).astype(BF16)
    d_pre_ref[...] = d_pre
    second_scr[1] = d_pre
    for half, half_refs in enumerate(part_refs):
        for v, ref in enumerate(half_refs):
            cols = pl.ds(pl.multiple_of((place ^ v) * WIDE, WIDE), WIDE)
            part = tn(first_scr[side ^ half, :, cols], second_scr[side ^ half])
            ref[...] = part.astype(ref.dtype)


def hop_bits(count):
    return list(range(count.bit_length() - 2, 2, -1)) + [0, 1, 2]


def hop_rows(count, bit):
    return count // 2 * SLOT + HALO * (2 if bit == 0 else 1)


def moves(device, bit):
    low = device % (1 << bit)
    ones = (1 << bit) - 1
    return (low == 0, low == ones) if bit > 2 else (low == ones, low == 0)


def pack_hop(count, bit, held_ref, left, right, out_ref):
    device = lax.axis_index("node")
    chosen = [r for r in range(count) if r >> bit & 1]
    for at, r in enumerate(chosen):
        out_ref[at * SLOT : (at + 1) * SLOT, :] = held_ref[r]
    size = len(chosen) * SLOT
    if bit == 0:
        out_ref[size : size + HALO, :] = left
        out_ref[size + HALO :, :] = right
    else:
        out_ref[size:, :] = jnp.where(moves(device, bit)[1], right, left)


def unpack_hop(count, bit, got_ref, held_ref, left, right):
    device = lax.axis_index("node")
    chosen = [r for r in range(count) if r >> bit & 1]
    for at, r in enumerate(chosen):
        held_ref[r] = got_ref[at * SLOT : (at + 1) * SLOT, :]
    size = len(chosen) * SLOT
    if bit == 0:
        return got_ref[size : size + HALO, :], got_ref[size + HALO :, :]
    got = got_ref[size:, :]
    left_moves, right_moves = moves(device, bit)
    return jnp.where(left_moves, got, left), jnp.where(right_moves, got, right)


def back_kernel(
    count, bit, mat_ref, total_ref, d_pre_ref, w_one_ref,
    own_ref, held_ref, left_ref, right_ref, out_ref,
):
    device = lax.axis_index("node")
    q = (nt(d_pre_ref[...], w_one_ref[...]) / total_ref[:, 0:1]).astype(BF16)
    rims = nn(mat_ref[HALO_COL : HALO_COL + 2 * HALO, :], q).astype(BF16)
    left_ref[...] = rims[0:HALO]
    right_ref[...] = rims[HALO : 2 * HALO]
    terms = nn(mat_ref[FAR_COL:, :], q).astype(BF16).reshape(count, SLOT, D)
    for peer in range(count):
        held_ref[device ^ peer] = terms[peer]
    pack_hop(count, bit, held_ref, rims[0:HALO], rims[HALO : 2 * HALO], out_ref)
    own_ref[...] = nn(mat_ref[0:ROWS, :], q)


def hop_kernel(
    count, last, bit, got_ref, was_ref, was_left_ref, was_right_ref,
    held_ref, left_ref, right_ref, out_ref,
):
    held_ref[...] = was_ref[...]
    left, right = unpack_hop(
        count, last, got_ref, held_ref, was_left_ref[...], was_right_ref[...]
    )
    left_ref[...] = left
    right_ref[...] = right
    pack_hop(count, bit, held_ref, left, right, out_ref)


def features_kernel(
    count, last, pick_ref, own_ref, got_ref, was_ref, was_left_ref, was_right_ref,
    out_ref, sum_scr, held_scr, block_scr,
):
    device = lax.axis_index("node")
    far = count * SLOT
    held_scr[...] = was_ref[...]
    left, right = unpack_hop(
        count, last, got_ref, held_scr, was_left_ref[...], was_right_ref[...]
    )
    for r in range(count):
        block_scr[device ^ r] = held_scr[r]
    sum_scr[...] = own_ref[...] + nn(pick_ref[...], block_scr[...].reshape(far, D))
    sum_scr[0:HALO, :] += right.astype(F32)
    sum_scr[ROWS - HALO : ROWS, :] += left.astype(F32)
    out_ref[...] = sum_scr[...].astype(BF16)


def sum_kernel(*refs):
    total = refs[0][...].astype(F32)
    for ref in refs[1:-1]:
        total = total + ref[...].astype(F32)
    refs[-1][...] = total.astype(BF16)


def pair_sum_kernel(scale, one_ref, two_ref, out_ref):
    total = one_ref[...].astype(F32) + two_ref[...].astype(F32)
    out_ref[...] = (total * scale).astype(BF16)


def gather_kernel(*refs):
    chunk_refs, out_refs, sems = refs[: 2 * PLANE], refs[2 * PLANE : 2 * PLANE + 2], refs[-1]
    device = lax.axis_index("node")
    place, side = device % PLANE, device // PLANE % 2
    for low in range(2):

        @pl.when(side == low)
        def _():
            copies = []
            for at, ref in enumerate(chunk_refs):
                row = pl.multiple_of((place ^ (at % PLANE)) * WIDE, WIDE)
                out_ref = out_refs[low ^ (at // PLANE)]
                copies.append(
                    pltpu.make_async_copy(ref, out_ref.at[pl.ds(row, WIDE), :], sems.at[at])
                )
                copies[-1].start()
            for copy in copies:
                copy.wait()


def shards(
    features, upstream, weight_one, weight_two, neighbours, edge_weight, fetch_block, fetch_count
):
    count = lax.axis_size("node")
    far = count * SLOT
    chain = FAR_COL + far
    onward = [(i, i + 1) for i in range(1, count - 1, 2)]
    onward = onward + [(target, source) for source, target in onward]

    def swap(value, flip):
        return lax.ppermute(value, "node", [(i, i ^ flip) for i in range(count)])

    vmem, hbm = (pl.BlockSpec(memory_space=space) for space in (pltpu.VMEM, pltpu.HBM))
    matrix, pick, total, own, send, near, onto = call(
        functools.partial(prepare_kernel, count),
        (
            struct((chain, ROWS), BF16),
            struct((ROWS, far), BF16),
            struct((ROWS, ROWS), F32),
            struct((ROWS, D), F32),
            struct((count, 2 * SLOT, D), BF16),
            struct((2 * HALO, D), BF16),
            struct((2 * HALO, D), BF16),
        ),
        (
            pltpu.VMEM((K, ROWS), jnp.int32),
            pltpu.VMEM((K, ROWS), jnp.int32),
            pltpu.VMEM((CAP, count * count), jnp.int32),
            pltpu.VMEM((1, count * count), jnp.int32),
            pltpu.VMEM((ROWS, D), BF16),
            pltpu.VMEM((ROWS, D), BF16),
            pltpu.SemaphoreType.DMA((6,)),
            pltpu.VMEM((8, count * count), F32),
            pltpu.VMEM((chain, ROWS), F32),
            pltpu.VMEM((count, SLOT, D), BF16),
            pltpu.VMEM((count, SLOT, D), BF16),
            pltpu.SemaphoreType.DMA((2,)),
        ),
        in_specs=[hbm] * 6,
        out_specs=(vmem, vmem, vmem, vmem, hbm, vmem, vmem),
    )(
        *(
            pltpu.with_memory_space_constraint(value, pltpu.HBM)
            for value in (
                neighbours.T, edge_weight.T, fetch_block.T, fetch_count.reshape(1, -1),
                features, upstream,
            )
        )
    )
    near = swap(near, 1)
    onto = lax.ppermute(onto, "node", onward)
    received = lax.all_to_all(send, "node", split_axis=0, concat_axis=0, tiled=True)

    piece, sent = struct((WIDE, D), F32), struct((WIDE, D), BF16)
    *parts, d_pre = call(
        functools.partial(layer_kernel, count),
        (*([piece] + [sent] * (PLANE - 1)) * 2, struct((ROWS, D), BF16)),
        (
            pltpu.VMEM((ROWS, D), BF16),
            pltpu.VMEM((ROWS, D), F32),
            pltpu.VMEM((2, ROWS, D), BF16),
            pltpu.VMEM((2, ROWS, D), BF16),
        ),
    )(matrix, pick, total, features, own, received, near, onto, weight_one, weight_two)
    kept, given = parts[:PLANE], parts[PLANE:]
    given = [given[0]] + [swap(given[v], v) for v in range(1, PLANE)]
    kept = [kept[0]] + [swap(kept[v], v) for v in range(1, PLANE)]

    bits = hop_bits(count)
    carried = (
        struct((count, SLOT, D), BF16),
        struct((HALO, D), BF16),
        struct((HALO, D), BF16),
    )

    def message(bit):
        return struct((hop_rows(count, bit), D), BF16)

    def next_hop(at, got, held):
        *held, out = call(
            functools.partial(hop_kernel, count, bits[at - 1], bits[at]),
            (*carried, message(bits[at])),
        )(got, *held)
        return out, held

    own, *held, out = call(
        functools.partial(back_kernel, count, bits[0]),
        (struct((ROWS, D), F32), *carried, message(bits[0])),
    )(matrix, total, d_pre, weight_one)
    got = swap(out, 1 << bits[0])
    for at in range(1, len(bits)):
        out, held = next_hop(at, got, held)
        got = swap(out, 1 << bits[at])
    total = call(sum_kernel, sent)(*kept, swap(call(sum_kernel, sent)(*given), PLANE))
    for bit in range(3, len(bits) - 1):
        total = call(functools.partial(pair_sum_kernel, 1.0), sent)(
            total, swap(total, 1 << bit)
        )
    other = swap(total, count // 2)
    total = call(
        functools.partial(pair_sum_kernel, 1.0 / math.sqrt(ROWS * count)), sent
    )(total, other)
    far_total = swap(total, PLANE)
    chunks = [total] + [swap(total, v) for v in range(1, PLANE)]
    chunks = chunks + [far_total] + [swap(far_total, v) for v in range(1, PLANE)]
    d_features = call(
        functools.partial(features_kernel, count, bits[-1]),
        struct((ROWS, D), BF16),
        (
            pltpu.VMEM((ROWS, D), F32),
            pltpu.VMEM((count, SLOT, D), BF16),
            pltpu.VMEM((count, SLOT, D), BF16),
        ),
    )(pick, own, got, *held)
    anywhere = pl.BlockSpec(memory_space=pl.ANY)
    grad_two, grad_one = call(
        gather_kernel,
        (struct((D, D), BF16), struct((D, D), BF16)),
        (pltpu.SemaphoreType.DMA((2 * PLANE,)),),
        in_specs=[anywhere] * (2 * PLANE),
        out_specs=(anywhere, anywhere),
    )(*chunks)
    return d_features, grad_one, grad_two


def solution(mesh):
    placed = (
        P(("rep", "node"), None),
        P(("rep", "node"), None),
        P(),
        P(),
        P(("rep", "node"), None),
        P(("rep", "node"), None),
        P("rep", None),
        P("rep"),
    )
    return jax.shard_map(
        shards,
        mesh=mesh,
        in_specs=placed,
        out_specs=(P(("rep", "node"), None), P("rep", None), P("rep", None)),
        check_vma=False,
    )
```

```python
import functools
import math

import jax
import jax.numpy as jnp
from jax import lax
from jax.experimental import pallas as pl
from jax.experimental.pallas import tpu as pltpu
from jax.sharding import PartitionSpec as P

D = 512
K = 32
ROWS = 128
HALO = 32
BLK = 8
CAP = 2
SELF_WEIGHT = 8.0
SLOT = CAP * BLK
HALO_COL = ROWS
FAR_COL = 2 * ROWS
PLANE = 4
WIDE = D // PLANE

F32 = jnp.float32
BF16 = jnp.bfloat16
VMEM_LIMIT = 48 * 1024 * 1024


def nn(left, right):
    return jnp.dot(left, right, preferred_element_type=F32)


def nt(left, right):
    return lax.dot_general(left, right, (((1,), (1,)), ((), ())), preferred_element_type=F32)


def tn(left, right):
    return lax.dot_general(left, right, (((0,), (0,)), ((), ())), preferred_element_type=F32)


def iota(shape, dim):
    return lax.broadcasted_iota(jnp.int32, shape, dim)


def call(kernel, out_shape, scratch=(), work=0, **specs):
    if work:
        specs["cost_estimate"] = pl.CostEstimate(
            flops=work, transcendentals=0, bytes_accessed=work // 64
        )
    return pl.pallas_call(
        kernel,
        out_shape=out_shape,
        **specs,
        scratch_shapes=list(scratch),
        compiler_params=pltpu.CompilerParams(vmem_limit_bytes=VMEM_LIMIT),
    )


def struct(shape, dtype):
    return jax.ShapeDtypeStruct(shape, dtype)


def prepare_kernel(
    count, nbr_hbm, wgt_hbm, tab_hbm, cnt_hbm, feat_hbm, up_hbm,
    mat_ref, pick_ref, total_ref, own_ref, send_hbm, near_ref, next_ref,
    nbr_ref, wgt_ref, tab_ref, cnt_ref, feat_ref, up_ref, sems, rows_scr, at_scr,
    rows_out, terms_out, out_sems,
):
    inputs = (
        (tab_hbm, tab_ref), (cnt_hbm, cnt_ref), (feat_hbm, feat_ref),
        (nbr_hbm, nbr_ref), (wgt_hbm, wgt_ref), (up_hbm, up_ref),
    )
    copies = [
        pltpu.make_async_copy(src, dst, sems.at[i]) for i, (src, dst) in enumerate(inputs)
    ]
    for copy in copies:
        copy.start()
    copies[0].wait()
    copies[1].wait()
    device = lax.axis_index("node")
    first = device * ROWS
    far = count * SLOT
    pairs = count * count
    rows_scr[...] = jnp.zeros_like(rows_scr)
    rows_scr[0:CAP, :] = tab_ref[...].astype(F32)
    rows_scr[CAP : CAP + 1, :] = cnt_ref[...].astype(F32)
    step = min(pairs, 256)
    listed = jnp.zeros((far, 8), F32)
    asked = jnp.zeros((far, 8), F32)
    asked_wide = jnp.zeros((8, far), F32)
    peer_wide = iota((far, step), 0) // SLOT
    for at in range(0, pairs, step):
        pair = iota((far, step), 1) + at
        rows = rows_scr[:, at : at + step].astype(BF16)
        mine = jnp.where(pair == device * count + peer_wide, 1.0, 0.0).astype(BF16)
        theirs = jnp.where(pair == peer_wide * count + device, 1.0, 0.0).astype(BF16)
        listed = listed + nt(mine, rows)
        asked = asked + nt(theirs, rows)
        asked_wide = asked_wide + nt(rows, theirs)
    listed = listed.astype(jnp.int32)
    asked = asked.astype(jnp.int32)
    col = iota((far, 1), 0)
    slot = col // BLK % CAP
    inner = col % BLK
    block = jnp.where(slot == 0, listed[:, 0:1], listed[:, 1:2])
    node = col // SLOT * ROWS + block * BLK + inner
    in_band = (node >= first - HALO) & (node < first + ROWS + HALO)
    far_node = jnp.where((slot < listed[:, 2:3]) & jnp.logical_not(in_band), node, -1)
    asked_row = jnp.where(slot == 0, asked[:, 0:1], asked[:, 1:2]) * BLK + inner
    pick = jnp.where(asked_row == iota((far, ROWS), 1), 1.0, 0.0).astype(BF16)
    wide_col = iota((1, far), 1)
    asked_wide = asked_wide.astype(jnp.int32)
    wide_row = jnp.where(wide_col // BLK % CAP == 0, asked_wide[0:1], asked_wide[1:2]) * BLK
    wide_row = wide_row + wide_col % BLK
    pick_ref[...] = jnp.where(wide_row == iota((ROWS, far), 0), 1.0, 0.0).astype(BF16)
    copies[2].wait()
    features = feat_ref[...]
    rows_out[...] = nn(pick, features).astype(BF16).reshape(count, SLOT, D)
    rows_copy = pltpu.make_async_copy(rows_out, send_hbm.at[:, 0:SLOT, :], out_sems.at[0])
    rows_copy.start()

    copies[3].wait()
    copies[4].wait()
    weight = wgt_ref[...].astype(F32)
    neighbour = nbr_ref[...]

    def counted(nodes, total):
        for k in range(K):
            total = total + jnp.where(neighbour[k : k + 1, :] == nodes, weight[k : k + 1, :], 0.0)
        return total

    square = (ROWS, ROWS)
    row = iota(square, 0)
    at_scr[0:ROWS, :] = counted(first + row, jnp.where(row == iota(square, 1), SELF_WEIGHT, 0.0))
    rim = iota((2 * HALO, ROWS), 0)
    rim_node = first + jnp.where(rim < HALO, rim - HALO, rim - HALO + ROWS)
    at_scr[HALO_COL : HALO_COL + 2 * HALO, :] = counted(rim_node, jnp.zeros((2 * HALO, ROWS), F32))
    at_scr[HALO_COL + 2 * HALO : FAR_COL, :] = jnp.zeros((FAR_COL - HALO_COL - 2 * HALO, ROWS), F32)
    for at in range(0, far, ROWS):
        nodes = jnp.broadcast_to(far_node[at : at + ROWS], square)
        at_scr[FAR_COL + at : FAR_COL + at + ROWS, :] = counted(nodes, jnp.zeros(square, F32))

    adj_mat = at_scr[...]
    total = jnp.broadcast_to(jnp.sum(adj_mat, axis=0, keepdims=True), square).T
    total_ref[...] = total
    adj_mat = adj_mat.astype(BF16)
    mat_ref[...] = adj_mat
    copies[5].wait()
    scaled = (up_ref[...].astype(F32) / total[:, 0:1]).astype(BF16)
    terms_out[...] = nn(adj_mat[FAR_COL:], scaled).astype(BF16).reshape(count, SLOT, D)
    terms_copy = pltpu.make_async_copy(
        terms_out, send_hbm.at[:, SLOT : 2 * SLOT, :], out_sems.at[1]
    )
    terms_copy.start()
    own_ref[...] = nn(adj_mat[0:ROWS], scaled)
    rims = nn(adj_mat[HALO_COL : HALO_COL + 2 * HALO], scaled).astype(BF16)
    even = device % 2 == 0
    low, high = features[0:HALO], features[ROWS - HALO : ROWS]
    near_ref[0:HALO, :] = jnp.where(even, high, low)
    near_ref[HALO:, :] = jnp.where(even, rims[HALO:], rims[0:HALO])
    next_ref[0:HALO, :] = jnp.where(even, low, high)
    next_ref[HALO:, :] = jnp.where(even, rims[0:HALO], rims[HALO:])
    rows_copy.wait()
    terms_copy.wait()


def layer_kernel(
    count, mat_ref, pick_ref, total_ref, feat_ref, own_ref, recv_ref, near_ref, next_ref,
    w_one_ref, w_two_ref,
    *refs,
):
    part_refs = refs[:PLANE], refs[PLANE : 2 * PLANE]
    d_pre_ref, rim_scr, u_scr, first_scr, second_scr = refs[2 * PLANE :]
    device = lax.axis_index("node")
    place, side = device % PLANE, device // PLANE % 2
    even = device % 2 == 0
    left = jnp.where(even, next_ref[...], near_ref[...])
    right = jnp.where(even, near_ref[...], next_ref[...])
    far = count * SLOT
    rim_scr[0:HALO, :] = left[0:HALO]
    rim_scr[HALO : 2 * HALO, :] = right[0:HALO]
    rim_scr[2 * HALO :, :] = jnp.zeros((ROWS - 2 * HALO, D), BF16)
    sums = tn(mat_ref[0:ROWS, :], feat_ref[...])
    sums = sums + tn(mat_ref[HALO_COL:FAR_COL, :], rim_scr[...])
    sums = sums + tn(mat_ref[FAR_COL:, :], recv_ref[:, 0:SLOT, :].reshape(far, D))
    agg = (sums / total_ref[:, 0:1]).astype(BF16)
    first_scr[1] = agg
    u_scr[...] = own_ref[...] + nn(
        pick_ref[...], recv_ref[:, SLOT : 2 * SLOT, :].reshape(far, D)
    )
    u_scr[0:HALO, :] += left[HALO:].astype(F32)
    u_scr[ROWS - HALO : ROWS, :] += right[HALO:].astype(F32)
    u = u_scr[...].astype(BF16)
    second_scr[0] = u
    back = nt(u, w_two_ref[...])
    pre = nn(agg, w_one_ref[...])
    square = pre * pre
    bend = jnp.tanh(0.7978845608 * pre * (1.0 + 0.044715 * square))
    first_scr[0] = (0.5 * pre * (1.0 + bend)).astype(BF16)
    slope = 0.5 * (1.0 + bend) + 0.5 * pre * (1.0 - bend * bend) * (
        0.7978845608 * (1.0 + 3.0 * 0.044715 * square)
    )
    d_pre = (back * slope).astype(BF16)
    d_pre_ref[...] = d_pre
    second_scr[1] = d_pre
    for half, half_refs in enumerate(part_refs):
        for v, ref in enumerate(half_refs):
            cols = pl.ds(pl.multiple_of((place ^ v) * WIDE, WIDE), WIDE)
            part = tn(first_scr[side ^ half, :, cols], second_scr[side ^ half])
            ref[...] = part.astype(ref.dtype)


def hop_bits(count):
    return list(range(count.bit_length() - 2, 2, -1)) + [0, 1, 2]


def hop_rows(count, bit):
    return count // 2 * SLOT + HALO * (2 if bit == 0 else 1)


def moves(device, bit):
    low = device % (1 << bit)
    ones = (1 << bit) - 1
    return (low == 0, low == ones) if bit > 2 else (low == ones, low == 0)


def pack_hop(count, bit, held_ref, left, right, out_ref):
    device = lax.axis_index("node")
    chosen = [r for r in range(count) if r >> bit & 1]
    for at, r in enumerate(chosen):
        out_ref[at * SLOT : (at + 1) * SLOT, :] = held_ref[r]
    size = len(chosen) * SLOT
    if bit == 0:
        out_ref[size : size + HALO, :] = left
        out_ref[size + HALO :, :] = right
    else:
        out_ref[size:, :] = jnp.where(moves(device, bit)[1], right, left)


def unpack_hop(count, bit, got_ref, held_ref, left, right):
    device = lax.axis_index("node")
    chosen = [r for r in range(count) if r >> bit & 1]
    for at, r in enumerate(chosen):
        held_ref[r] = got_ref[at * SLOT : (at + 1) * SLOT, :]
    size = len(chosen) * SLOT
    if bit == 0:
        return got_ref[size : size + HALO, :], got_ref[size + HALO :, :]
    got = got_ref[size:, :]
    left_moves, right_moves = moves(device, bit)
    return jnp.where(left_moves, got, left), jnp.where(right_moves, got, right)


def back_kernel(
    count, bit, mat_ref, total_ref, d_pre_ref, w_one_ref,
    own_ref, held_ref, left_ref, right_ref, out_ref,
):
    device = lax.axis_index("node")
    q = (nt(d_pre_ref[...], w_one_ref[...]) / total_ref[:, 0:1]).astype(BF16)
    rims = nn(mat_ref[HALO_COL : HALO_COL + 2 * HALO, :], q).astype(BF16)
    left_ref[...] = rims[0:HALO]
    right_ref[...] = rims[HALO : 2 * HALO]
    terms = nn(mat_ref[FAR_COL:, :], q).astype(BF16).reshape(count, SLOT, D)
    for peer in range(count):
        held_ref[device ^ peer] = terms[peer]
    pack_hop(count, bit, held_ref, rims[0:HALO], rims[HALO : 2 * HALO], out_ref)
    own_ref[...] = nn(mat_ref[0:ROWS, :], q)


def hop_kernel(
    count, last, bit, got_ref, was_ref, was_left_ref, was_right_ref,
    held_ref, left_ref, right_ref, out_ref,
):
    held_ref[...] = was_ref[...]
    left, right = unpack_hop(
        count, last, got_ref, held_ref, was_left_ref[...], was_right_ref[...]
    )
    left_ref[...] = left
    right_ref[...] = right
    pack_hop(count, bit, held_ref, left, right, out_ref)


def features_kernel(
    count, last, pick_ref, own_ref, got_ref, was_ref, was_left_ref, was_right_ref,
    out_ref, sum_scr, held_scr, block_scr,
):
    device = lax.axis_index("node")
    far = count * SLOT
    held_scr[...] = was_ref[...]
    left, right = unpack_hop(
        count, last, got_ref, held_scr, was_left_ref[...], was_right_ref[...]
    )
    for r in range(count):
        block_scr[device ^ r] = held_scr[r]
    sum_scr[...] = own_ref[...] + nn(pick_ref[...], block_scr[...].reshape(far, D))
    sum_scr[0:HALO, :] += right.astype(F32)
    sum_scr[ROWS - HALO : ROWS, :] += left.astype(F32)
    out_ref[...] = sum_scr[...].astype(BF16)


def sum_kernel(*refs):
    total = refs[0][...].astype(F32)
    for ref in refs[1:-1]:
        total = total + ref[...].astype(F32)
    refs[-1][...] = total.astype(BF16)


def pair_sum_kernel(scale, one_ref, two_ref, out_ref):
    total = one_ref[...].astype(F32) + two_ref[...].astype(F32)
    out_ref[...] = (total * scale).astype(BF16)


def gather_kernel(*refs):
    chunk_refs, out_refs, sems = refs[: 2 * PLANE], refs[2 * PLANE : 2 * PLANE + 2], refs[-1]
    device = lax.axis_index("node")
    place, side = device % PLANE, device // PLANE % 2
    for low in range(2):

        @pl.when(side == low)
        def _():
            copies = []
            for at, ref in enumerate(chunk_refs):
                row = pl.multiple_of((place ^ (at % PLANE)) * WIDE, WIDE)
                out_ref = out_refs[low ^ (at // PLANE)]
                copies.append(
                    pltpu.make_async_copy(ref, out_ref.at[pl.ds(row, WIDE), :], sems.at[at])
                )
                copies[-1].start()
            for copy in copies:
                copy.wait()


def shards(
    features, upstream, weight_one, weight_two, neighbours, edge_weight, fetch_block, fetch_count
):
    count = lax.axis_size("node")
    far = count * SLOT
    chain = FAR_COL + far
    onward = [(i, i + 1) for i in range(1, count - 1, 2)]
    onward = onward + [(target, source) for source, target in onward]

    def swap(value, flip):
        return lax.ppermute(value, "node", [(i, i ^ flip) for i in range(count)])

    vmem, hbm = (pl.BlockSpec(memory_space=space) for space in (pltpu.VMEM, pltpu.HBM))
    matrix, pick, total, own, send, near, onto = call(
        functools.partial(prepare_kernel, count),
        (
            struct((chain, ROWS), BF16),
            struct((ROWS, far), BF16),
            struct((ROWS, ROWS), F32),
            struct((ROWS, D), F32),
            struct((count, 2 * SLOT, D), BF16),
            struct((2 * HALO, D), BF16),
            struct((2 * HALO, D), BF16),
        ),
        (
            pltpu.VMEM((K, ROWS), jnp.int32),
            pltpu.VMEM((K, ROWS), jnp.int32),
            pltpu.VMEM((CAP, count * count), jnp.int32),
            pltpu.VMEM((1, count * count), jnp.int32),
            pltpu.VMEM((ROWS, D), BF16),
            pltpu.VMEM((ROWS, D), BF16),
            pltpu.SemaphoreType.DMA((6,)),
            pltpu.VMEM((8, count * count), F32),
            pltpu.VMEM((chain, ROWS), F32),
            pltpu.VMEM((count, SLOT, D), BF16),
            pltpu.VMEM((count, SLOT, D), BF16),
            pltpu.SemaphoreType.DMA((2,)),
        ),
        in_specs=[hbm] * 6,
        out_specs=(vmem, vmem, vmem, vmem, hbm, vmem, vmem),
    )(
        *(
            pltpu.with_memory_space_constraint(value, pltpu.HBM)
            for value in (
                neighbours.T, edge_weight.T, fetch_block.T, fetch_count.reshape(1, -1),
                features, upstream,
            )
        )
    )
    near = swap(near, 1)
    onto = lax.ppermute(onto, "node", onward)
    received = lax.all_to_all(send, "node", split_axis=0, concat_axis=0, tiled=True)

    piece, sent = struct((WIDE, D), F32), struct((WIDE, D), BF16)
    *parts, d_pre = call(
        functools.partial(layer_kernel, count),
        (*([piece] + [sent] * (PLANE - 1)) * 2, struct((ROWS, D), BF16)),
        (
            pltpu.VMEM((ROWS, D), BF16),
            pltpu.VMEM((ROWS, D), F32),
            pltpu.VMEM((2, ROWS, D), BF16),
            pltpu.VMEM((2, ROWS, D), BF16),
        ),
    )(matrix, pick, total, features, own, received, near, onto, weight_one, weight_two)
    kept, given = parts[:PLANE], parts[PLANE:]
    given = [given[0]] + [swap(given[v], v) for v in range(1, PLANE)]
    kept = [kept[0]] + [swap(kept[v], v) for v in range(1, PLANE)]

    bits = hop_bits(count)
    carried = (
        struct((count, SLOT, D), BF16),
        struct((HALO, D), BF16),
        struct((HALO, D), BF16),
    )

    def message(bit):
        return struct((hop_rows(count, bit), D), BF16)

    def next_hop(at, got, held):
        *held, out = call(
            functools.partial(hop_kernel, count, bits[at - 1], bits[at]),
            (*carried, message(bits[at])),
        )(got, *held)
        return out, held

    own, *held, out = call(
        functools.partial(back_kernel, count, bits[0]),
        (struct((ROWS, D), F32), *carried, message(bits[0])),
    )(matrix, total, d_pre, weight_one)
    got = swap(out, 1 << bits[0])
    for at in range(1, len(bits)):
        out, held = next_hop(at, got, held)
        got = swap(out, 1 << bits[at])
    total = call(sum_kernel, sent)(*kept, swap(call(sum_kernel, sent, work=1073741824)(*given), PLANE))
    for bit in range(3, len(bits) - 1):
        total = call(functools.partial(pair_sum_kernel, 1.0), sent)(
            total, swap(total, 1 << bit)
        )
    other = swap(total, count // 2)
    total = call(
        functools.partial(pair_sum_kernel, 1.0 / math.sqrt(ROWS * count)), sent
    )(total, other)
    far_total = swap(total, PLANE)
    chunks = [total] + [swap(total, v) for v in range(1, PLANE)]
    chunks = chunks + [far_total] + [swap(far_total, v) for v in range(1, PLANE)]
    d_features = call(
        functools.partial(features_kernel, count, bits[-1]),
        struct((ROWS, D), BF16),
        (
            pltpu.VMEM((ROWS, D), F32),
            pltpu.VMEM((count, SLOT, D), BF16),
            pltpu.VMEM((count, SLOT, D), BF16),
        ),
    )(pick, own, got, *held)
    anywhere = pl.BlockSpec(memory_space=pl.ANY)
    grad_two, grad_one = call(
        gather_kernel,
        (struct((D, D), BF16), struct((D, D), BF16)),
        (pltpu.SemaphoreType.DMA((2 * PLANE,)),),
        in_specs=[anywhere] * (2 * PLANE),
        out_specs=(anywhere, anywhere),
    )(*chunks)
    return d_features, grad_one, grad_two


def solution(mesh):
    placed = (
        P(("rep", "node"), None),
        P(("rep", "node"), None),
        P(),
        P(),
        P(("rep", "node"), None),
        P(("rep", "node"), None),
        P("rep", None),
        P("rep"),
    )
    return jax.shard_map(
        shards,
        mesh=mesh,
        in_specs=placed,
        out_specs=(P(("rep", "node"), None), P("rep", None), P("rep", None)),
        check_vma=False,
    )
```

```python
import functools
import math

import jax
import jax.numpy as jnp
from jax import lax
from jax.experimental import pallas as pl
from jax.experimental.pallas import tpu as pltpu
from jax.sharding import PartitionSpec as P

D = 512
K = 32
ROWS = 128
HALO = 32
BLK = 8
CAP = 2
SELF_WEIGHT = 8.0
SLOT = CAP * BLK
HALO_COL = ROWS
FAR_COL = 2 * ROWS
PLANE = 4
WIDE = D // PLANE

F32 = jnp.float32
BF16 = jnp.bfloat16
VMEM_LIMIT = 48 * 1024 * 1024


def nn(left, right):
    return jnp.dot(left, right, preferred_element_type=F32)


def nt(left, right):
    return lax.dot_general(left, right, (((1,), (1,)), ((), ())), preferred_element_type=F32)


def tn(left, right):
    return lax.dot_general(left, right, (((0,), (0,)), ((), ())), preferred_element_type=F32)


def iota(shape, dim):
    return lax.broadcasted_iota(jnp.int32, shape, dim)


def call(kernel, out_shape, scratch=(), work=0, **specs):
    if work:
        specs["cost_estimate"] = pl.CostEstimate(
            flops=work, transcendentals=0, bytes_accessed=work // 64
        )
    return pl.pallas_call(
        kernel,
        out_shape=out_shape,
        **specs,
        scratch_shapes=list(scratch),
        compiler_params=pltpu.CompilerParams(vmem_limit_bytes=VMEM_LIMIT),
    )


def struct(shape, dtype):
    return jax.ShapeDtypeStruct(shape, dtype)


def prepare_kernel(
    count, nbr_hbm, wgt_hbm, tab_hbm, cnt_hbm, feat_hbm, up_hbm,
    mat_ref, pick_ref, total_ref, own_ref, send_hbm, near_ref, next_ref,
    nbr_ref, wgt_ref, tab_ref, cnt_ref, feat_ref, up_ref, sems, rows_scr, at_scr,
    rows_out, terms_out, out_sems,
):
    inputs = (
        (tab_hbm, tab_ref), (cnt_hbm, cnt_ref), (feat_hbm, feat_ref),
        (nbr_hbm, nbr_ref), (wgt_hbm, wgt_ref), (up_hbm, up_ref),
    )
    copies = [
        pltpu.make_async_copy(src, dst, sems.at[i]) for i, (src, dst) in enumerate(inputs)
    ]
    for copy in copies:
        copy.start()
    copies[0].wait()
    copies[1].wait()
    device = lax.axis_index("node")
    first = device * ROWS
    far = count * SLOT
    pairs = count * count
    rows_scr[...] = jnp.zeros_like(rows_scr)
    rows_scr[0:CAP, :] = tab_ref[...].astype(F32)
    rows_scr[CAP : CAP + 1, :] = cnt_ref[...].astype(F32)
    step = min(pairs, 256)
    listed = jnp.zeros((far, 8), F32)
    asked = jnp.zeros((far, 8), F32)
    asked_wide = jnp.zeros((8, far), F32)
    peer_wide = iota((far, step), 0) // SLOT
    for at in range(0, pairs, step):
        pair = iota((far, step), 1) + at
        rows = rows_scr[:, at : at + step].astype(BF16)
        mine = jnp.where(pair == device * count + peer_wide, 1.0, 0.0).astype(BF16)
        theirs = jnp.where(pair == peer_wide * count + device, 1.0, 0.0).astype(BF16)
        listed = listed + nt(mine, rows)
        asked = asked + nt(theirs, rows)
        asked_wide = asked_wide + nt(rows, theirs)
    listed = listed.astype(jnp.int32)
    asked = asked.astype(jnp.int32)
    col = iota((far, 1), 0)
    slot = col // BLK % CAP
    inner = col % BLK
    block = jnp.where(slot == 0, listed[:, 0:1], listed[:, 1:2])
    node = col // SLOT * ROWS + block * BLK + inner
    in_band = (node >= first - HALO) & (node < first + ROWS + HALO)
    far_node = jnp.where((slot < listed[:, 2:3]) & jnp.logical_not(in_band), node, -1)
    asked_row = jnp.where(slot == 0, asked[:, 0:1], asked[:, 1:2]) * BLK + inner
    pick = jnp.where(asked_row == iota((far, ROWS), 1), 1.0, 0.0).astype(BF16)
    wide_col = iota((1, far), 1)
    asked_wide = asked_wide.astype(jnp.int32)
    wide_row = jnp.where(wide_col // BLK % CAP == 0, asked_wide[0:1], asked_wide[1:2]) * BLK
    wide_row = wide_row + wide_col % BLK
    pick_ref[...] = jnp.where(wide_row == iota((ROWS, far), 0), 1.0, 0.0).astype(BF16)
    copies[2].wait()
    features = feat_ref[...]
    rows_out[...] = nn(pick, features).astype(BF16).reshape(count, SLOT, D)
    rows_copy = pltpu.make_async_copy(rows_out, send_hbm.at[:, 0:SLOT, :], out_sems.at[0])
    rows_copy.start()

    copies[3].wait()
    copies[4].wait()
    weight = wgt_ref[...].astype(F32)
    neighbour = nbr_ref[...]

    def counted(nodes, total):
        for k in range(K):
            total = total + jnp.where(neighbour[k : k + 1, :] == nodes, weight[k : k + 1, :], 0.0)
        return total

    square = (ROWS, ROWS)
    row = iota(square, 0)
    at_scr[0:ROWS, :] = counted(first + row, jnp.where(row == iota(square, 1), SELF_WEIGHT, 0.0))
    rim = iota((2 * HALO, ROWS), 0)
    rim_node = first + jnp.where(rim < HALO, rim - HALO, rim - HALO + ROWS)
    at_scr[HALO_COL : HALO_COL + 2 * HALO, :] = counted(rim_node, jnp.zeros((2 * HALO, ROWS), F32))
    at_scr[HALO_COL + 2 * HALO : FAR_COL, :] = jnp.zeros((FAR_COL - HALO_COL - 2 * HALO, ROWS), F32)
    for at in range(0, far, ROWS):
        nodes = jnp.broadcast_to(far_node[at : at + ROWS], square)
        at_scr[FAR_COL + at : FAR_COL + at + ROWS, :] = counted(nodes, jnp.zeros(square, F32))

    adj_mat = at_scr[...]
    total = jnp.broadcast_to(jnp.sum(adj_mat, axis=0, keepdims=True), square).T
    total_ref[...] = total
    adj_mat = adj_mat.astype(BF16)
    mat_ref[...] = adj_mat
    copies[5].wait()
    scaled = (up_ref[...].astype(F32) / total[:, 0:1]).astype(BF16)
    terms_out[...] = nn(adj_mat[FAR_COL:], scaled).astype(BF16).reshape(count, SLOT, D)
    terms_copy = pltpu.make_async_copy(
        terms_out, send_hbm.at[:, SLOT : 2 * SLOT, :], out_sems.at[1]
    )
    terms_copy.start()
    own_ref[...] = nn(adj_mat[0:ROWS], scaled)
    rims = nn(adj_mat[HALO_COL : HALO_COL + 2 * HALO], scaled).astype(BF16)
    even = device % 2 == 0
    low, high = features[0:HALO], features[ROWS - HALO : ROWS]
    near_ref[0:HALO, :] = jnp.where(even, high, low)
    near_ref[HALO:, :] = jnp.where(even, rims[HALO:], rims[0:HALO])
    next_ref[0:HALO, :] = jnp.where(even, low, high)
    next_ref[HALO:, :] = jnp.where(even, rims[0:HALO], rims[HALO:])
    rows_copy.wait()
    terms_copy.wait()


def layer_kernel(
    count, mat_ref, pick_ref, total_ref, feat_ref, own_ref, recv_ref, near_ref, next_ref,
    w_one_ref, w_two_ref,
    *refs,
):
    part_refs = refs[:PLANE], refs[PLANE : 2 * PLANE]
    d_pre_ref, rim_scr, u_scr, first_scr, second_scr = refs[2 * PLANE :]
    device = lax.axis_index("node")
    place, side = device % PLANE, device // PLANE % 2
    even = device % 2 == 0
    left = jnp.where(even, next_ref[...], near_ref[...])
    right = jnp.where(even, near_ref[...], next_ref[...])
    far = count * SLOT
    rim_scr[0:HALO, :] = left[0:HALO]
    rim_scr[HALO : 2 * HALO, :] = right[0:HALO]
    rim_scr[2 * HALO :, :] = jnp.zeros((ROWS - 2 * HALO, D), BF16)
    sums = tn(mat_ref[0:ROWS, :], feat_ref[...])
    sums = sums + tn(mat_ref[HALO_COL:FAR_COL, :], rim_scr[...])
    sums = sums + tn(mat_ref[FAR_COL:, :], recv_ref[:, 0:SLOT, :].reshape(far, D))
    agg = (sums / total_ref[:, 0:1]).astype(BF16)
    first_scr[1] = agg
    u_scr[...] = own_ref[...] + nn(
        pick_ref[...], recv_ref[:, SLOT : 2 * SLOT, :].reshape(far, D)
    )
    u_scr[0:HALO, :] += left[HALO:].astype(F32)
    u_scr[ROWS - HALO : ROWS, :] += right[HALO:].astype(F32)
    u = u_scr[...].astype(BF16)
    second_scr[0] = u
    back = nt(u, w_two_ref[...])
    pre = nn(agg, w_one_ref[...])
    square = pre * pre
    bend = jnp.tanh(0.7978845608 * pre * (1.0 + 0.044715 * square))
    first_scr[0] = (0.5 * pre * (1.0 + bend)).astype(BF16)
    slope = 0.5 * (1.0 + bend) + 0.5 * pre * (1.0 - bend * bend) * (
        0.7978845608 * (1.0 + 3.0 * 0.044715 * square)
    )
    d_pre = (back * slope).astype(BF16)
    d_pre_ref[...] = d_pre
    second_scr[1] = d_pre
    for half, half_refs in enumerate(part_refs):
        for v, ref in enumerate(half_refs):
            cols = pl.ds(pl.multiple_of((place ^ v) * WIDE, WIDE), WIDE)
            part = tn(first_scr[side ^ half, :, cols], second_scr[side ^ half])
            ref[...] = part.astype(ref.dtype)


def hop_bits(count):
    return list(range(count.bit_length() - 2, 2, -1)) + [0, 1, 2]


def hop_rows(count, bit):
    return count // 2 * SLOT + HALO * (2 if bit == 0 else 1)


def moves(device, bit):
    low = device % (1 << bit)
    ones = (1 << bit) - 1
    return (low == 0, low == ones) if bit > 2 else (low == ones, low == 0)


def pack_hop(count, bit, held_ref, left, right, out_ref):
    device = lax.axis_index("node")
    chosen = [r for r in range(count) if r >> bit & 1]
    for at, r in enumerate(chosen):
        out_ref[at * SLOT : (at + 1) * SLOT, :] = held_ref[r]
    size = len(chosen) * SLOT
    if bit == 0:
        out_ref[size : size + HALO, :] = left
        out_ref[size + HALO :, :] = right
    else:
        out_ref[size:, :] = jnp.where(moves(device, bit)[1], right, left)


def unpack_hop(count, bit, got_ref, held_ref, left, right):
    device = lax.axis_index("node")
    chosen = [r for r in range(count) if r >> bit & 1]
    for at, r in enumerate(chosen):
        held_ref[r] = got_ref[at * SLOT : (at + 1) * SLOT, :]
    size = len(chosen) * SLOT
    if bit == 0:
        return got_ref[size : size + HALO, :], got_ref[size + HALO :, :]
    got = got_ref[size:, :]
    left_moves, right_moves = moves(device, bit)
    return jnp.where(left_moves, got, left), jnp.where(right_moves, got, right)


def back_kernel(
    count, bit, mat_ref, total_ref, d_pre_ref, w_one_ref,
    own_ref, held_ref, left_ref, right_ref, out_ref,
):
    device = lax.axis_index("node")
    q = (nt(d_pre_ref[...], w_one_ref[...]) / total_ref[:, 0:1]).astype(BF16)
    rims = nn(mat_ref[HALO_COL : HALO_COL + 2 * HALO, :], q).astype(BF16)
    left_ref[...] = rims[0:HALO]
    right_ref[...] = rims[HALO : 2 * HALO]
    terms = nn(mat_ref[FAR_COL:, :], q).astype(BF16).reshape(count, SLOT, D)
    for peer in range(count):
        held_ref[device ^ peer] = terms[peer]
    pack_hop(count, bit, held_ref, rims[0:HALO], rims[HALO : 2 * HALO], out_ref)
    own_ref[...] = nn(mat_ref[0:ROWS, :], q)


def hop_kernel(
    count, last, bit, got_ref, was_ref, was_left_ref, was_right_ref,
    held_ref, left_ref, right_ref, out_ref,
):
    held_ref[...] = was_ref[...]
    left, right = unpack_hop(
        count, last, got_ref, held_ref, was_left_ref[...], was_right_ref[...]
    )
    left_ref[...] = left
    right_ref[...] = right
    pack_hop(count, bit, held_ref, left, right, out_ref)


def features_kernel(
    count, last, pick_ref, own_ref, got_ref, was_ref, was_left_ref, was_right_ref,
    out_ref, sum_scr, held_scr, block_scr,
):
    device = lax.axis_index("node")
    far = count * SLOT
    held_scr[...] = was_ref[...]
    left, right = unpack_hop(
        count, last, got_ref, held_scr, was_left_ref[...], was_right_ref[...]
    )
    for r in range(count):
        block_scr[device ^ r] = held_scr[r]
    sum_scr[...] = own_ref[...] + nn(pick_ref[...], block_scr[...].reshape(far, D))
    sum_scr[0:HALO, :] += right.astype(F32)
    sum_scr[ROWS - HALO : ROWS, :] += left.astype(F32)
    out_ref[...] = sum_scr[...].astype(BF16)


def sum_kernel(*refs):
    total = refs[0][...].astype(F32)
    for ref in refs[1:-1]:
        total = total + ref[...].astype(F32)
    refs[-1][...] = total.astype(BF16)


def pair_sum_kernel(scale, one_ref, two_ref, out_ref):
    total = one_ref[...].astype(F32) + two_ref[...].astype(F32)
    out_ref[...] = (total * scale).astype(BF16)


def last_kernel(count, last, *refs):
    chunk_refs, refs = refs[: 2 * PLANE], refs[2 * PLANE :]
    in_refs, (out_ref, two_ref, one_ref, *scratch, sems) = refs[:6], refs[6:]
    device = lax.axis_index("node")
    place, side = device % PLANE, device // PLANE % 2

    def copies(low):
        for at, ref in enumerate(chunk_refs):
            row = pl.multiple_of((place ^ (at % PLANE)) * WIDE, WIDE)
            grad_ref = (two_ref, one_ref)[low ^ (at // PLANE)]
            yield pltpu.make_async_copy(ref, grad_ref.at[pl.ds(row, WIDE), :], sems.at[at])

    for low in range(2):

        @pl.when(side == low)
        def _():
            for copy in copies(low):
                copy.start()

    features_kernel(count, last, *in_refs, out_ref, *scratch)
    for low in range(2):

        @pl.when(side == low)
        def _():
            for copy in copies(low):
                copy.wait()


def shards(
    features, upstream, weight_one, weight_two, neighbours, edge_weight, fetch_block, fetch_count
):
    count = lax.axis_size("node")
    far = count * SLOT
    chain = FAR_COL + far
    onward = [(i, i + 1) for i in range(1, count - 1, 2)]
    onward = onward + [(target, source) for source, target in onward]

    def swap(value, flip):
        return lax.ppermute(value, "node", [(i, i ^ flip) for i in range(count)])

    vmem, hbm = (pl.BlockSpec(memory_space=space) for space in (pltpu.VMEM, pltpu.HBM))
    matrix, pick, total, own, send, near, onto = call(
        functools.partial(prepare_kernel, count),
        (
            struct((chain, ROWS), BF16),
            struct((ROWS, far), BF16),
            struct((ROWS, ROWS), F32),
            struct((ROWS, D), F32),
            struct((count, 2 * SLOT, D), BF16),
            struct((2 * HALO, D), BF16),
            struct((2 * HALO, D), BF16),
        ),
        (
            pltpu.VMEM((K, ROWS), jnp.int32),
            pltpu.VMEM((K, ROWS), jnp.int32),
            pltpu.VMEM((CAP, count * count), jnp.int32),
            pltpu.VMEM((1, count * count), jnp.int32),
            pltpu.VMEM((ROWS, D), BF16),
            pltpu.VMEM((ROWS, D), BF16),
            pltpu.SemaphoreType.DMA((6,)),
            pltpu.VMEM((8, count * count), F32),
            pltpu.VMEM((chain, ROWS), F32),
            pltpu.VMEM((count, SLOT, D), BF16),
            pltpu.VMEM((count, SLOT, D), BF16),
            pltpu.SemaphoreType.DMA((2,)),
        ),
        in_specs=[hbm] * 6,
        out_specs=(vmem, vmem, vmem, vmem, hbm, vmem, vmem),
    )(
        *(
            pltpu.with_memory_space_constraint(value, pltpu.HBM)
            for value in (
                neighbours.T, edge_weight.T, fetch_block.T, fetch_count.reshape(1, -1),
                features, upstream,
            )
        )
    )
    near = swap(near, 1)
    onto = lax.ppermute(onto, "node", onward)
    received = lax.all_to_all(send, "node", split_axis=0, concat_axis=0, tiled=True)

    piece, sent = struct((WIDE, D), F32), struct((WIDE, D), BF16)
    *parts, d_pre = call(
        functools.partial(layer_kernel, count),
        (*([piece] + [sent] * (PLANE - 1)) * 2, struct((ROWS, D), BF16)),
        (
            pltpu.VMEM((ROWS, D), BF16),
            pltpu.VMEM((ROWS, D), F32),
            pltpu.VMEM((2, ROWS, D), BF16),
            pltpu.VMEM((2, ROWS, D), BF16),
        ),
    )(matrix, pick, total, features, own, received, near, onto, weight_one, weight_two)
    kept, given = parts[:PLANE], parts[PLANE:]
    given = [given[0]] + [swap(given[v], v) for v in range(1, PLANE)]
    kept = [kept[0]] + [swap(kept[v], v) for v in range(1, PLANE)]

    bits = hop_bits(count)
    carried = (
        struct((count, SLOT, D), BF16),
        struct((HALO, D), BF16),
        struct((HALO, D), BF16),
    )

    def message(bit):
        return struct((hop_rows(count, bit), D), BF16)

    def next_hop(at, got, held):
        *held, out = call(
            functools.partial(hop_kernel, count, bits[at - 1], bits[at]),
            (*carried, message(bits[at])),
        )(got, *held)
        return out, held

    own, *held, out = call(
        functools.partial(back_kernel, count, bits[0]),
        (struct((ROWS, D), F32), *carried, message(bits[0])),
    )(matrix, total, d_pre, weight_one)
    got = swap(out, 1 << bits[0])
    for at in range(1, len(bits)):
        out, held = next_hop(at, got, held)
        got = swap(out, 1 << bits[at])
    total = call(sum_kernel, sent, work=268435456)(*kept, swap(call(sum_kernel, sent, work=1073741824)(*given), PLANE))
    for bit in range(3, len(bits) - 1):
        total = call(functools.partial(pair_sum_kernel, 1.0), sent)(
            total, swap(total, 1 << bit)
        )
    other = swap(total, count // 2)
    total = call(
        functools.partial(pair_sum_kernel, 1.0 / math.sqrt(ROWS * count)), sent
    )(total, other)
    far_total = swap(total, PLANE)
    chunks = [total] + [swap(total, v) for v in range(1, PLANE)]
    chunks = chunks + [far_total] + [swap(far_total, v) for v in range(1, PLANE)]
    anywhere = pl.BlockSpec(memory_space=pl.ANY)
    d_features, grad_two, grad_one = call(
        functools.partial(last_kernel, count, bits[-1]),
        (struct((ROWS, D), BF16), struct((D, D), BF16), struct((D, D), BF16)),
        (
            pltpu.VMEM((ROWS, D), F32),
            pltpu.VMEM((count, SLOT, D), BF16),
            pltpu.VMEM((count, SLOT, D), BF16),
            pltpu.SemaphoreType.DMA((2 * PLANE,)),
        ),
        in_specs=[anywhere] * (2 * PLANE) + [vmem] * 6,
        out_specs=(vmem, anywhere, anywhere),
    )(*chunks, pick, own, got, *held)
    return d_features, grad_one, grad_two


def solution(mesh):
    placed = (
        P(("rep", "node"), None),
        P(("rep", "node"), None),
        P(),
        P(),
        P(("rep", "node"), None),
        P(("rep", "node"), None),
        P("rep", None),
        P("rep"),
    )
    return jax.shard_map(
        shards,
        mesh=mesh,
        in_specs=placed,
        out_specs=(P(("rep", "node"), None), P("rep", None), P("rep", None)),
        check_vma=False,
    )
```

```python
import functools
import math

import jax
import jax.numpy as jnp
from jax import lax
from jax.experimental import pallas as pl
from jax.experimental.pallas import tpu as pltpu
from jax.sharding import PartitionSpec as P

D = 512
K = 32
ROWS = 128
HALO = 32
BLK = 8
CAP = 2
SELF_WEIGHT = 8.0
SLOT = CAP * BLK
HALO_COL = ROWS
FAR_COL = 2 * ROWS
PLANE = 4
WIDE = D // PLANE

F32 = jnp.float32
BF16 = jnp.bfloat16
VMEM_LIMIT = 48 * 1024 * 1024


def nn(left, right):
    return jnp.dot(left, right, preferred_element_type=F32)


def nt(left, right):
    return lax.dot_general(left, right, (((1,), (1,)), ((), ())), preferred_element_type=F32)


def tn(left, right):
    return lax.dot_general(left, right, (((0,), (0,)), ((), ())), preferred_element_type=F32)


def iota(shape, dim):
    return lax.broadcasted_iota(jnp.int32, shape, dim)


def call(kernel, out_shape, scratch=(), work=0, **specs):
    if work:
        specs["cost_estimate"] = pl.CostEstimate(
            flops=work, transcendentals=0, bytes_accessed=work // 64
        )
    return pl.pallas_call(
        kernel,
        out_shape=out_shape,
        **specs,
        scratch_shapes=list(scratch),
        compiler_params=pltpu.CompilerParams(vmem_limit_bytes=VMEM_LIMIT),
    )


def struct(shape, dtype):
    return jax.ShapeDtypeStruct(shape, dtype)


def prepare_kernel(
    count, nbr_hbm, wgt_hbm, tab_hbm, cnt_hbm, feat_hbm, up_hbm,
    mat_ref, pick_ref, total_ref, own_ref, send_hbm, near_ref, next_ref,
    nbr_ref, wgt_ref, tab_ref, cnt_ref, feat_ref, up_ref, sems, rows_scr, at_scr,
    rows_out, terms_out, out_sems,
):
    inputs = (
        (tab_hbm, tab_ref), (cnt_hbm, cnt_ref), (feat_hbm, feat_ref),
        (nbr_hbm, nbr_ref), (wgt_hbm, wgt_ref), (up_hbm, up_ref),
    )
    copies = [
        pltpu.make_async_copy(src, dst, sems.at[i]) for i, (src, dst) in enumerate(inputs)
    ]
    for copy in copies:
        copy.start()
    copies[0].wait()
    copies[1].wait()
    device = lax.axis_index("node")
    first = device * ROWS
    far = count * SLOT
    pairs = count * count
    rows_scr[...] = jnp.zeros_like(rows_scr)
    rows_scr[0:CAP, :] = tab_ref[...].astype(F32)
    rows_scr[CAP : CAP + 1, :] = cnt_ref[...].astype(F32)
    step = min(pairs, 256)
    listed = jnp.zeros((far, 8), F32)
    asked = jnp.zeros((far, 8), F32)
    asked_wide = jnp.zeros((8, far), F32)
    peer_wide = iota((far, step), 0) // SLOT
    for at in range(0, pairs, step):
        pair = iota((far, step), 1) + at
        rows = rows_scr[:, at : at + step].astype(BF16)
        mine = jnp.where(pair == device * count + peer_wide, 1.0, 0.0).astype(BF16)
        theirs = jnp.where(pair == peer_wide * count + device, 1.0, 0.0).astype(BF16)
        listed = listed + nt(mine, rows)
        asked = asked + nt(theirs, rows)
        asked_wide = asked_wide + nt(rows, theirs)
    listed = listed.astype(jnp.int32)
    asked = asked.astype(jnp.int32)
    col = iota((far, 1), 0)
    slot = col // BLK % CAP
    inner = col % BLK
    block = jnp.where(slot == 0, listed[:, 0:1], listed[:, 1:2])
    node = col // SLOT * ROWS + block * BLK + inner
    in_band = (node >= first - HALO) & (node < first + ROWS + HALO)
    far_node = jnp.where((slot < listed[:, 2:3]) & jnp.logical_not(in_band), node, -1)
    asked_row = jnp.where(slot == 0, asked[:, 0:1], asked[:, 1:2]) * BLK + inner
    pick = jnp.where(asked_row == iota((far, ROWS), 1), 1.0, 0.0).astype(BF16)
    wide_col = iota((1, far), 1)
    asked_wide = asked_wide.astype(jnp.int32)
    wide_row = jnp.where(wide_col // BLK % CAP == 0, asked_wide[0:1], asked_wide[1:2]) * BLK
    wide_row = wide_row + wide_col % BLK
    pick_ref[...] = jnp.where(wide_row == iota((ROWS, far), 0), 1.0, 0.0).astype(BF16)
    copies[2].wait()
    features = feat_ref[...]
    rows_out[...] = nn(pick, features).astype(BF16).reshape(count, SLOT, D)
    rows_copy = pltpu.make_async_copy(rows_out, send_hbm.at[:, 0:SLOT, :], out_sems.at[0])
    rows_copy.start()

    copies[3].wait()
    copies[4].wait()
    weight = wgt_ref[...].astype(F32)
    neighbour = nbr_ref[...]

    def counted(nodes, total):
        for k in range(K):
            total = total + jnp.where(neighbour[k : k + 1, :] == nodes, weight[k : k + 1, :], 0.0)
        return total

    square = (ROWS, ROWS)
    row = iota(square, 0)
    at_scr[0:ROWS, :] = counted(first + row, jnp.where(row == iota(square, 1), SELF_WEIGHT, 0.0))
    rim = iota((2 * HALO, ROWS), 0)
    rim_node = first + jnp.where(rim < HALO, rim - HALO, rim - HALO + ROWS)
    at_scr[HALO_COL : HALO_COL + 2 * HALO, :] = counted(rim_node, jnp.zeros((2 * HALO, ROWS), F32))
    at_scr[HALO_COL + 2 * HALO : FAR_COL, :] = jnp.zeros((FAR_COL - HALO_COL - 2 * HALO, ROWS), F32)
    for at in range(0, far, ROWS):
        nodes = jnp.broadcast_to(far_node[at : at + ROWS], square)
        at_scr[FAR_COL + at : FAR_COL + at + ROWS, :] = counted(nodes, jnp.zeros(square, F32))

    adj_mat = at_scr[...]
    total = jnp.broadcast_to(jnp.sum(adj_mat, axis=0, keepdims=True), square).T
    total_ref[...] = total
    adj_mat = adj_mat.astype(BF16)
    mat_ref[...] = adj_mat
    copies[5].wait()
    scaled = (up_ref[...].astype(F32) / total[:, 0:1]).astype(BF16)
    terms_out[...] = nn(adj_mat[FAR_COL:], scaled).astype(BF16).reshape(count, SLOT, D)
    terms_copy = pltpu.make_async_copy(
        terms_out, send_hbm.at[:, SLOT : 2 * SLOT, :], out_sems.at[1]
    )
    terms_copy.start()
    own_ref[...] = nn(adj_mat[0:ROWS], scaled)
    rims = nn(adj_mat[HALO_COL : HALO_COL + 2 * HALO], scaled).astype(BF16)
    even = device % 2 == 0
    low, high = features[0:HALO], features[ROWS - HALO : ROWS]
    near_ref[0:HALO, :] = jnp.where(even, high, low)
    near_ref[HALO:, :] = jnp.where(even, rims[HALO:], rims[0:HALO])
    next_ref[0:HALO, :] = jnp.where(even, low, high)
    next_ref[HALO:, :] = jnp.where(even, rims[0:HALO], rims[HALO:])
    rows_copy.wait()
    terms_copy.wait()


def layer_kernel(
    count, mat_ref, pick_ref, total_ref, feat_ref, own_ref, recv_ref, near_ref, next_ref,
    w_one_ref, w_two_ref,
    *refs,
):
    part_refs = refs[:PLANE], refs[PLANE : 2 * PLANE]
    d_pre_ref, rim_scr, u_scr, first_scr, second_scr = refs[2 * PLANE :]
    device = lax.axis_index("node")
    place, side = device % PLANE, device // PLANE % 2
    even = device % 2 == 0
    left = jnp.where(even, next_ref[...], near_ref[...])
    right = jnp.where(even, near_ref[...], next_ref[...])
    far = count * SLOT
    rim_scr[0:HALO, :] = left[0:HALO]
    rim_scr[HALO : 2 * HALO, :] = right[0:HALO]
    rim_scr[2 * HALO :, :] = jnp.zeros((ROWS - 2 * HALO, D), BF16)
    sums = tn(mat_ref[0:ROWS, :], feat_ref[...])
    sums = sums + tn(mat_ref[HALO_COL:FAR_COL, :], rim_scr[...])
    sums = sums + tn(mat_ref[FAR_COL:, :], recv_ref[:, 0:SLOT, :].reshape(far, D))
    agg = (sums / total_ref[:, 0:1]).astype(BF16)
    first_scr[1] = agg
    u_scr[...] = own_ref[...] + nn(
        pick_ref[...], recv_ref[:, SLOT : 2 * SLOT, :].reshape(far, D)
    )
    u_scr[0:HALO, :] += left[HALO:].astype(F32)
    u_scr[ROWS - HALO : ROWS, :] += right[HALO:].astype(F32)
    u = u_scr[...].astype(BF16)
    second_scr[0] = u
    back = nt(u, w_two_ref[...])
    pre = nn(agg, w_one_ref[...])
    square = pre * pre
    bend = jnp.tanh(0.7978845608 * pre * (1.0 + 0.044715 * square))
    first_scr[0] = (0.5 * pre * (1.0 + bend)).astype(BF16)
    slope = 0.5 * (1.0 + bend) + 0.5 * pre * (1.0 - bend * bend) * (
        0.7978845608 * (1.0 + 3.0 * 0.044715 * square)
    )
    d_pre = (back * slope).astype(BF16)
    d_pre_ref[...] = d_pre
    second_scr[1] = d_pre
    for half, half_refs in enumerate(part_refs):
        for v, ref in enumerate(half_refs):
            cols = pl.ds(pl.multiple_of((place ^ v) * WIDE, WIDE), WIDE)
            part = tn(first_scr[side ^ half, :, cols], second_scr[side ^ half])
            ref[...] = part.astype(ref.dtype)


def hop_bits(count):
    return list(range(count.bit_length() - 2, 2, -1)) + [0, 1, 2]


def hop_rows(count, bit):
    return count // 2 * SLOT + HALO * (2 if bit == 0 else 1)


def moves(device, bit):
    low = device % (1 << bit)
    ones = (1 << bit) - 1
    return (low == 0, low == ones) if bit > 2 else (low == ones, low == 0)


def pack_hop(count, bit, held_ref, left, right, out_ref):
    device = lax.axis_index("node")
    chosen = [r for r in range(count) if r >> bit & 1]
    for at, r in enumerate(chosen):
        out_ref[at * SLOT : (at + 1) * SLOT, :] = held_ref[r]
    size = len(chosen) * SLOT
    if bit == 0:
        out_ref[size : size + HALO, :] = left
        out_ref[size + HALO :, :] = right
    else:
        out_ref[size:, :] = jnp.where(moves(device, bit)[1], right, left)


def unpack_hop(count, bit, got_ref, held_ref, left, right):
    device = lax.axis_index("node")
    chosen = [r for r in range(count) if r >> bit & 1]
    for at, r in enumerate(chosen):
        held_ref[r] = got_ref[at * SLOT : (at + 1) * SLOT, :]
    size = len(chosen) * SLOT
    if bit == 0:
        return got_ref[size : size + HALO, :], got_ref[size + HALO :, :]
    got = got_ref[size:, :]
    left_moves, right_moves = moves(device, bit)
    return jnp.where(left_moves, got, left), jnp.where(right_moves, got, right)


def back_kernel(
    count, bit, mat_ref, total_ref, d_pre_ref, w_one_ref,
    own_ref, held_ref, left_ref, right_ref, out_ref,
):
    device = lax.axis_index("node")
    q = (nt(d_pre_ref[...], w_one_ref[...]) / total_ref[:, 0:1]).astype(BF16)
    rims = nn(mat_ref[HALO_COL : HALO_COL + 2 * HALO, :], q).astype(BF16)
    left_ref[...] = rims[0:HALO]
    right_ref[...] = rims[HALO : 2 * HALO]
    terms = nn(mat_ref[FAR_COL:, :], q).astype(BF16).reshape(count, SLOT, D)
    for peer in range(count):
        held_ref[device ^ peer] = terms[peer]
    pack_hop(count, bit, held_ref, rims[0:HALO], rims[HALO : 2 * HALO], out_ref)
    own_ref[...] = nn(mat_ref[0:ROWS, :], q)


def hop_kernel(
    count, last, bit, got_ref, was_ref, was_left_ref, was_right_ref,
    held_ref, left_ref, right_ref, out_ref,
):
    held_ref[...] = was_ref[...]
    left, right = unpack_hop(
        count, last, got_ref, held_ref, was_left_ref[...], was_right_ref[...]
    )
    left_ref[...] = left
    right_ref[...] = right
    pack_hop(count, bit, held_ref, left, right, out_ref)


def features_kernel(
    count, last, pick_ref, own_ref, got_ref, was_ref, was_left_ref, was_right_ref,
    out_ref, sum_scr, held_scr, block_scr,
):
    device = lax.axis_index("node")
    far = count * SLOT
    held_scr[...] = was_ref[...]
    left, right = unpack_hop(
        count, last, got_ref, held_scr, was_left_ref[...], was_right_ref[...]
    )
    for r in range(count):
        block_scr[device ^ r] = held_scr[r]
    sum_scr[...] = own_ref[...] + nn(pick_ref[...], block_scr[...].reshape(far, D))
    sum_scr[0:HALO, :] += right.astype(F32)
    sum_scr[ROWS - HALO : ROWS, :] += left.astype(F32)
    out_ref[...] = sum_scr[...].astype(BF16)


def sum_kernel(*refs):
    total = refs[0][...].astype(F32)
    for ref in refs[1:-1]:
        total = total + ref[...].astype(F32)
    refs[-1][...] = total.astype(BF16)


def pair_sum_kernel(scale, one_ref, two_ref, out_ref):
    total = one_ref[...].astype(F32) + two_ref[...].astype(F32)
    out_ref[...] = (total * scale).astype(BF16)


def last_kernel(count, last, *refs):
    chunk_refs, refs = refs[: 2 * PLANE], refs[2 * PLANE :]
    in_refs, (out_ref, two_ref, one_ref, *scratch, sems) = refs[:6], refs[6:]
    device = lax.axis_index("node")
    place, side = device % PLANE, device // PLANE % 2

    def copies(low):
        for at, ref in enumerate(chunk_refs):
            row = pl.multiple_of((place ^ (at % PLANE)) * WIDE, WIDE)
            grad_ref = (two_ref, one_ref)[low ^ (at // PLANE)]
            yield pltpu.make_async_copy(ref, grad_ref.at[pl.ds(row, WIDE), :], sems.at[at])

    for low in range(2):

        @pl.when(side == low)
        def _():
            for copy in copies(low):
                copy.start()

    features_kernel(count, last, *in_refs, out_ref, *scratch)
    for low in range(2):

        @pl.when(side == low)
        def _():
            for copy in copies(low):
                copy.wait()


def shards(
    features, upstream, weight_one, weight_two, neighbours, edge_weight, fetch_block, fetch_count
):
    count = lax.axis_size("node")
    far = count * SLOT
    chain = FAR_COL + far
    onward = [(i, i + 1) for i in range(1, count - 1, 2)]
    onward = onward + [(target, source) for source, target in onward]

    def swap(value, flip):
        return lax.ppermute(value, "node", [(i, i ^ flip) for i in range(count)])

    vmem, hbm = (pl.BlockSpec(memory_space=space) for space in (pltpu.VMEM, pltpu.HBM))
    matrix, pick, total, own, send, near, onto = call(
        functools.partial(prepare_kernel, count),
        (
            struct((chain, ROWS), BF16),
            struct((ROWS, far), BF16),
            struct((ROWS, ROWS), F32),
            struct((ROWS, D), F32),
            struct((count, 2 * SLOT, D), BF16),
            struct((2 * HALO, D), BF16),
            struct((2 * HALO, D), BF16),
        ),
        (
            pltpu.VMEM((K, ROWS), jnp.int32),
            pltpu.VMEM((K, ROWS), jnp.int32),
            pltpu.VMEM((CAP, count * count), jnp.int32),
            pltpu.VMEM((1, count * count), jnp.int32),
            pltpu.VMEM((ROWS, D), BF16),
            pltpu.VMEM((ROWS, D), BF16),
            pltpu.SemaphoreType.DMA((6,)),
            pltpu.VMEM((8, count * count), F32),
            pltpu.VMEM((chain, ROWS), F32),
            pltpu.VMEM((count, SLOT, D), BF16),
            pltpu.VMEM((count, SLOT, D), BF16),
            pltpu.SemaphoreType.DMA((2,)),
        ),
        in_specs=[hbm] * 6,
        out_specs=(vmem, vmem, vmem, vmem, hbm, vmem, vmem),
    )(
        *(
            pltpu.with_memory_space_constraint(value, pltpu.HBM)
            for value in (
                neighbours.T, edge_weight.T, fetch_block.T, fetch_count.reshape(1, -1),
                features, upstream,
            )
        )
    )
    near = swap(near, 1)
    onto = lax.ppermute(onto, "node", onward)
    received = lax.all_to_all(send, "node", split_axis=0, concat_axis=0, tiled=True)

    piece, sent = struct((WIDE, D), F32), struct((WIDE, D), BF16)
    *parts, d_pre = call(
        functools.partial(layer_kernel, count),
        (*([piece] + [sent] * (PLANE - 1)) * 2, struct((ROWS, D), BF16)),
        (
            pltpu.VMEM((ROWS, D), BF16),
            pltpu.VMEM((ROWS, D), F32),
            pltpu.VMEM((2, ROWS, D), BF16),
            pltpu.VMEM((2, ROWS, D), BF16),
        ),
    )(matrix, pick, total, features, own, received, near, onto, weight_one, weight_two)
    kept, given = parts[:PLANE], parts[PLANE:]
    given = [given[0]] + [swap(given[v], v) for v in range(1, PLANE)]
    kept = [kept[0]] + [swap(kept[v], v) for v in range(1, PLANE)]

    bits = hop_bits(count)
    carried = (
        struct((count, SLOT, D), BF16),
        struct((HALO, D), BF16),
        struct((HALO, D), BF16),
    )

    def message(bit):
        return struct((hop_rows(count, bit), D), BF16)

    def next_hop(at, got, held):
        *held, out = call(
            functools.partial(hop_kernel, count, bits[at - 1], bits[at]),
            (*carried, message(bits[at])),
        )(got, *held)
        return out, held

    own, *held, out = call(
        functools.partial(back_kernel, count, bits[0]),
        (struct((ROWS, D), F32), *carried, message(bits[0])),
    )(matrix, total, d_pre, weight_one)
    got = swap(out, 1 << bits[0])
    for at in range(1, len(bits) - 1):
        out, held = next_hop(at, got, held)
        got = swap(out, 1 << bits[at])
    total = call(sum_kernel, sent, work=268435456)(*kept, swap(call(sum_kernel, sent, work=1073741824)(*given), PLANE))
    for bit in range(3, len(bits) - 1):
        total = call(functools.partial(pair_sum_kernel, 1.0), sent)(
            total, swap(total, 1 << bit)
        )
    other = swap(total, count // 2)
    total = call(
        functools.partial(pair_sum_kernel, 1.0 / math.sqrt(ROWS * count)), sent
    )(total, other)
    far_total = swap(total, PLANE)
    far_total, got = lax.optimization_barrier((far_total, got))
    out, held = next_hop(len(bits) - 1, got, held)
    got = swap(out, 1 << bits[-1])
    chunks = [total] + [swap(total, v) for v in range(1, PLANE)]
    chunks = chunks + [far_total] + [swap(far_total, v) for v in range(1, PLANE)]
    anywhere = pl.BlockSpec(memory_space=pl.ANY)
    d_features, grad_two, grad_one = call(
        functools.partial(last_kernel, count, bits[-1]),
        (struct((ROWS, D), BF16), struct((D, D), BF16), struct((D, D), BF16)),
        (
            pltpu.VMEM((ROWS, D), F32),
            pltpu.VMEM((count, SLOT, D), BF16),
            pltpu.VMEM((count, SLOT, D), BF16),
            pltpu.SemaphoreType.DMA((2 * PLANE,)),
        ),
        in_specs=[anywhere] * (2 * PLANE) + [vmem] * 6,
        out_specs=(vmem, anywhere, anywhere),
    )(*chunks, pick, own, got, *held)
    return d_features, grad_one, grad_two


def solution(mesh):
    placed = (
        P(("rep", "node"), None),
        P(("rep", "node"), None),
        P(),
        P(),
        P(("rep", "node"), None),
        P(("rep", "node"), None),
        P("rep", None),
        P("rep"),
    )
    return jax.shard_map(
        shards,
        mesh=mesh,
        in_specs=placed,
        out_specs=(P(("rep", "node"), None), P("rep", None), P("rep", None)),
        check_vma=False,
    )
```
